128 devices in a mesh: gx: 16 (over y, x), gy: 8 (over z, core).
Axes of the slice: x: 4, y: 4, z: 4, core: 2. Of those that a mesh axis runs over, the one named last changes fastest.
Arguments:
- records: bfloat16 [128, 128, 64, 128], P(('gx', 'gy')), may hold values from -6 to 6
- slot_voxels: int32 [128, 128, 256], P(('gx', 'gy')), may hold values from 0 to 8192, as said below
- brick_mask: int32 [32, 16, 4], P('gx', 'gy'), may hold values 0 or 1
- lift_weight: bfloat16 [32, 64], replicated, may hold values from -1 to 1
- leaf_convs: bfloat16 [2, 3, 3, 3, 64, 64], replicated, may hold values from -0.21875 to 0.21875
- down_leaf: bfloat16 [2, 2, 2, 64, 128], replicated, may hold values from -0.375 to 0.375
- down_coarse: bfloat16 [2, 2, 2, 2, 128, 128], replicated, may hold values from -0.25 to 0.25
- coarse_convs: bfloat16 [3, 3, 3, 3, 128, 128], replicated, may hold values from -0.15625 to 0.15625
Outputs:
- leaf_features: bfloat16 [256, 128, 16, 128], P('gx', 'gy')
- top_features: bfloat16 [32, 16, 4, 128], P('gx', 'gy')
The draws below stay inside these ranges and needn't reach their ends.
Inputs may be any that keep to these rules, and one draw needn't show every extreme that they name: `slot_voxels`: entry [s, d, j] is owner d's local voxel index of slot j of the records that device s sends to owner d, or 8192 where that slot is empty; filled slots come first in each bucket; in every draw some owner receives 256 filled slots from every device, and every bucket has an empty slot unless its owner is such a full one.
All inputs are finite; a program needn't handle non-finite values. No bound on the sum of `brick_mask` on one device may be relied on, other than what follows from the above.
Results may differ from the reference program's by a relative error of at most 0.023.
Values may be sent and summed in bfloat16 or wider, within the bound.
No kernel may reach another device: no remote copies, remote signals or barrier semaphores. Data moves between devices by JAX's collectives and lax.ppermute only.
A program may use at most 64 MiB of HBM per device.

```python
import jax
import jax.numpy as jnp
from jax import lax

FEAT = 32
CH_LEAF = 64
CH_COARSE = 128
BRICK = 8
BRICK_X = 2
BRICK_Y = 2
BRICK_Z = 4
CAP = 256
VOX_X = 16
VOX_Y = 16
VOX_Z = 32
VOXELS = 8192
GRID_X = 256
GRID_Y = 128
N_GX = 16
N_GY = 8
DEVICES = 128


def draw_slot_voxels(key, part):
    key_hot, key_forced, key_base, key_voxel = jax.random.split(key, 4)
    owner_hot = jax.random.randint(key_hot, (DEVICES,), 0, 4) == 0
    forced = jax.random.randint(key_forced, (), 0, DEVICES)
    owner_hot = owner_hot | (jnp.arange(DEVICES) == forced)
    base_count = jax.random.randint(key_base, (DEVICES, DEVICES), CAP // 8, CAP // 2 + 1)
    filled = jnp.where(owner_hot[None, :], CAP, base_count)
    voxel_draw = jax.random.randint(key_voxel, (DEVICES, DEVICES, CAP), 0, VOXELS)
    slot_index = jnp.arange(CAP)[None, None, :]
    return jnp.where(slot_index < filled[:, :, None], voxel_draw, VOXELS).astype(jnp.int32)


def set_ends(array, stream_key, least, largest):
    longest = array.shape.index(max(array.shape))
    spots = []
    for shift in (0, 1):
        where = [jax.random.randint(jax.random.fold_in(stream_key, axis), (), 0, length) for axis, length in enumerate(array.shape)]
        where[longest] = (where[longest] + shift) % array.shape[longest]
        spots.append(tuple(where))
    return array.at[spots[0]].set(least).at[spots[1]].set(largest)


def shard_levels(rng, dims, cuts, low, top_value):
    loudness, own = 1.0, jax.random.fold_in(rng, 6)
    for dim, parts in cuts:
        draws = jnp.exp(jax.random.uniform(jax.random.fold_in(own, dim), (parts,), jnp.float32, low / len(cuts), top_value / len(cuts)))
        loudness = loudness * jnp.repeat(draws, dims[dim] // parts).reshape([-1 if axis == dim else 1 for axis in range(len(dims))])
    return loudness


def gaussian(own_key, extent, deviation, most, cuts=(), kind=jnp.bfloat16):
    drawn = deviation * jax.random.normal(own_key, extent, jnp.float32)
    if cuts:
        drawn = drawn * shard_levels(own_key, extent, cuts, -0.22, 0.18)
    return jnp.clip(drawn, -most, most).astype(kind)


def setup_inputs(seed: int = 0) -> dict:
    seeds = jax.random.split(jax.random.key(seed), 9)
    return {
        "records": gaussian(seeds[0], (DEVICES, DEVICES, CAP // 4, 4 * FEAT), 1.0, 6.0, ((0, 128),)),
        "slot_voxels": draw_slot_voxels(jax.random.fold_in(seeds[8], 71), 0),
        "brick_mask": set_ends((jax.random.randint(seeds[2], (BRICK_X * N_GX, BRICK_Y * N_GY, BRICK_Z), 0, 4) < 3).astype(jnp.int32), jax.random.fold_in(seeds[2], 1), 0, 1),
        "lift_weight": gaussian(seeds[3], (FEAT, CH_LEAF), FEAT ** -0.5, 1.0),
        "leaf_convs": gaussian(seeds[4], (2, 3, 3, 3, CH_LEAF, CH_LEAF), (27 * CH_LEAF // 2) ** -0.5, 0.21875),
        "down_leaf": gaussian(seeds[5], (2, 2, 2, CH_LEAF, CH_COARSE), (4 * CH_LEAF) ** -0.5, 0.375),
        "down_coarse": gaussian(seeds[6], (2, 2, 2, 2, CH_COARSE, CH_COARSE), (4 * CH_COARSE) ** -0.5, 0.25),
        "coarse_convs": gaussian(seeds[7], (3, 3, 3, 3, CH_COARSE, CH_COARSE), (27 * CH_COARSE // 2) ** -0.5, 0.15625),
    }


def conv_cube(values, kernel):
    padded = jnp.pad(values, ((1, 1), (1, 1), (1, 1), (0, 0)))
    size_a, size_b, size_c, channels = values.shape
    summed = jnp.zeros((size_a * size_b * size_c, kernel.shape[-1]), jnp.float32)
    for step_x in range(3):
        for step_y in range(3):
            for step_z in range(3):
                window = padded[step_x:step_x + size_a, step_y:step_y + size_b, step_z:step_z + size_c]
                summed = summed + jnp.dot(window.reshape(-1, channels), kernel[step_x, step_y, step_z], preferred_element_type=jnp.float32)
    return summed.reshape(size_a, size_b, size_c, kernel.shape[-1])


def shrink_cube(values, kernel):
    size_a, size_b, size_c, channels = values.shape
    blocks = values.astype(jnp.float32).reshape(size_a // 2, 2, size_b // 2, 2, size_c // 2, 2, channels)
    return jnp.einsum("xaybzci,abcio->xyzo", blocks, kernel.astype(jnp.float32), precision=lax.Precision.HIGHEST)


def expand_mask(brick_mask, factor):
    widened_mask = jnp.repeat(jnp.repeat(jnp.repeat(brick_mask, factor, 0), factor, 1), factor, 2)
    return widened_mask.astype(jnp.float32)[..., None]


def reference(records, slot_voxels, brick_mask, lift_weight, leaf_convs, down_leaf, down_coarse, coarse_convs):
    owners = jnp.arange(DEVICES, dtype=jnp.int32)[None, :, None]
    owner_x = owners // N_GY
    owner_y = owners % N_GY
    coord_x = owner_x * VOX_X + slot_voxels // (VOX_Y * VOX_Z)
    coord_y = owner_y * VOX_Y + (slot_voxels // VOX_Z) % VOX_Y
    coord_z = slot_voxels % VOX_Z
    cell_count = GRID_X * GRID_Y * VOX_Z
    target = (coord_x * GRID_Y + coord_y) * VOX_Z + coord_z
    target = jnp.where(slot_voxels < VOXELS, target, cell_count).astype(jnp.int32).reshape(-1)
    flat_records = records.reshape(-1, FEAT).astype(jnp.float32)
    summed = jax.ops.segment_sum(flat_records, target, num_segments=cell_count + 1)[:cell_count]
    lifted = jnp.dot(summed, lift_weight.astype(jnp.float32), precision=lax.Precision.HIGHEST)
    hidden = lifted.reshape(GRID_X, GRID_Y, VOX_Z, CH_LEAF).astype(jnp.bfloat16)
    leaf_occupied = expand_mask(brick_mask, BRICK)
    for layer_index in range(2):
        hidden = (jax.nn.relu(conv_cube(hidden, leaf_convs[layer_index])) * leaf_occupied).astype(jnp.bfloat16)
    leaf_features = hidden.reshape(GRID_X, GRID_Y, VOX_Z // 2, 2 * CH_LEAF)
    for level_index in range(3):
        factor = BRICK // 2 ** (level_index + 1)
        occupied = expand_mask(brick_mask, factor)
        kernel = down_leaf if level_index == 0 else down_coarse[level_index - 1]
        hidden = (jax.nn.relu(shrink_cube(hidden, kernel)) * occupied).astype(jnp.bfloat16)
        hidden = (jax.nn.relu(conv_cube(hidden, coarse_convs[level_index])) * occupied).astype(jnp.bfloat16)
    return leaf_features, hidden
```

```python
import functools

import jax
import jax.numpy as jnp
from jax import lax
from jax.experimental import pallas as pl
from jax.experimental.pallas import tpu as pltpu
from jax.sharding import PartitionSpec as P

BRICK = 8
BUCKETS = 8


def with_halo(cells, sides, width):
    for axis, dim in sides:
        count = lax.axis_size(axis)
        here = lax.axis_index(axis)
        head = lax.slice_in_dim(cells, 0, width, axis=dim)
        tail = lax.slice_in_dim(cells, cells.shape[dim] - width, cells.shape[dim], axis=dim)
        before = lax.ppermute(tail, axis, [(i, (i + 1) % count) for i in range(count)])
        after = lax.ppermute(head, axis, [((i + 1) % count, i) for i in range(count)])
        before = jnp.where(here > 0, before, jnp.zeros_like(before))
        after = jnp.where(here < count - 1, after, jnp.zeros_like(after))
        cells = jnp.concatenate([before, cells, after], axis=dim)
    return cells


def join_columns(left_block, right_block):
    return jnp.concatenate([left_block, right_block], -1)


def leaf_taps(kernel):
    zero_block = jnp.zeros_like(kernel[:, :, 0])
    tap_low = kernel[:, :, 0]
    tap_mid = kernel[:, :, 1]
    tap_high = kernel[:, :, 2]
    from_before = jnp.concatenate(
        [join_columns(zero_block, zero_block), join_columns(tap_low, zero_block)], -2
    )
    from_middle = jnp.concatenate(
        [join_columns(tap_mid, tap_low), join_columns(tap_high, tap_mid)], -2
    )
    from_after = jnp.concatenate(
        [join_columns(zero_block, tap_high), join_columns(zero_block, zero_block)], -2
    )
    return jnp.concatenate([from_before, from_middle, from_after], -2)


def leaf_sweep(padded, tap_table, extent_x, extent_y):
    shifted = jnp.pad(padded, ((0, 0), (0, 0), (1, 1), (0, 0)))
    stacked = jnp.concatenate([shifted[:, :, :-2], shifted[:, :, 1:-1], shifted[:, :, 2:]], -1)
    summed = jnp.zeros((extent_x, extent_y, padded.shape[2], tap_table.shape[-1]), jnp.float32)
    for step_x in range(3):
        for step_y in range(3):
            window = stacked[step_x : step_x + extent_x, step_y : step_y + extent_y]
            summed = summed + jnp.einsum(
                "xyzk,kc->xyzc",
                window,
                tap_table[step_x, step_y],
                preferred_element_type=jnp.float32,
            )
    return summed


def leaf_layer(values, tap_table, occupied):
    padded = with_halo(values, (("gx", 0), ("gy", 1)), 1)
    swept = leaf_sweep(padded, tap_table, values.shape[0], values.shape[1])
    return (jax.nn.relu(swept) * occupied).astype(jnp.bfloat16)


def coarse_layer(values, kernel, occupied):
    padded = with_halo(values, (("gx", 0), ("gy", 1)), 1)
    padded = jnp.pad(padded, ((0, 0), (0, 0), (1, 1), (0, 0)))
    extent_x, extent_y, extent_z, channels = values.shape
    summed = jnp.zeros((extent_x, extent_y, extent_z, kernel.shape[-1]), jnp.float32)
    for step_x in range(3):
        for step_y in range(3):
            for step_z in range(3):
                window = padded[
                    step_x : step_x + extent_x,
                    step_y : step_y + extent_y,
                    step_z : step_z + extent_z,
                ]
                summed = summed + jnp.einsum(
                    "xyzk,kc->xyzc",
                    window,
                    kernel[step_x, step_y, step_z],
                    preferred_element_type=jnp.float32,
                )
    return (jax.nn.relu(summed) * occupied).astype(jnp.bfloat16)


def shrink_paired(values, kernel):
    extent_x, extent_y, extent_z, width = values.shape
    blocks = values.reshape(extent_x // 2, 2, extent_y // 2, 2, extent_z, width)
    merged = kernel.reshape(2, 2, width, kernel.shape[-1])
    return jnp.einsum("xaybzk,abko->xyzo", blocks, merged, preferred_element_type=jnp.float32)


def spread_mask(brick_mask, factor, factor_z):
    widened_mask = jnp.repeat(jnp.repeat(brick_mask, factor, 0), factor, 1)
    return jnp.repeat(widened_mask, factor_z, 2).astype(jnp.float32)


def pack_messages(records, slot_voxels):
    fours = slot_voxels.shape[-1] // 4
    high = (slot_voxels >> 9) * 16 + ((slot_voxels & 31) >> 1)
    low = ((slot_voxels >> 5) & 15) * 2 + (slot_voxels & 1)
    parity = lax.axis_index("gy") % 2
    source = lax.broadcasted_iota(jnp.int32, (4 * fours, 4, 2, fours), 0)
    quarter = lax.broadcasted_iota(jnp.int32, (4 * fours, 4, 2, fours), 1)
    side = lax.broadcasted_iota(jnp.int32, (4 * fours, 4, 2, fours), 2)
    row = lax.broadcasted_iota(jnp.int32, (4 * fours, 4, 2, fours), 3)
    picks = ((source == 4 * row + quarter) & (side == parity)).astype(jnp.bfloat16)
    picks = picks.reshape(4 * fours, 4 * 2 * fours)
    both = jnp.stack([high, low]).astype(jnp.bfloat16)
    ids = jnp.einsum("tds,sk->dtk", both, picks, preferred_element_type=jnp.float32)
    ids = ids.astype(jnp.bfloat16).reshape(slot_voxels.shape[0], 8, 2 * fours)
    return jnp.concatenate([records, ids], 1)


def scatter_kernel(msg_ref, lift_ref, cells_ref, total_ref):
    step = pl.program_id(0)

    @pl.when(step == 0)
    def _():
        total_ref[...] = jnp.zeros_like(total_ref)

    wide = 256
    lanes = lax.broadcasted_iota(jnp.int32, (wide, wide), 0).astype(jnp.bfloat16)
    zero = jnp.zeros((32, wide), jnp.bfloat16)
    for quad in range(BUCKETS // 4):
        turned, ids = [], []
        for pair in range(2):
            first = quad * 4 + pair * 2
            rows = jnp.concatenate([msg_ref[first, 0:64], msg_ref[first + 1, 0:64]], 0)
            turned.append(jnp.transpose(rows))
            ids.append(
                msg_ref[first, 64:72].astype(jnp.float32)
                + msg_ref[first + 1, 64:72].astype(jnp.float32)
            )
        turned = jnp.concatenate(turned, 1)
        ids = jnp.concatenate(ids, 1)
        for quarter in range(4):
            features = turned[quarter * 32 : quarter * 32 + 32]
            high = jnp.broadcast_to(ids[quarter : quarter + 1], (wide, wide)).astype(jnp.bfloat16)
            low = jnp.broadcast_to(ids[quarter + 4 : quarter + 5], (32, wide)).astype(jnp.bfloat16)
            hot = jnp.where(lanes == high, 1.0, 0.0).astype(jnp.bfloat16)
            spread = jnp.concatenate(
                [jnp.where(low == jnp.bfloat16(value), features, zero) for value in range(32)], 0
            )
            total_ref[...] += lax.dot_general(
                spread, hot, (((1,), (1,)), ((), ())), preferred_element_type=jnp.float32
            )

    @pl.when(step == pl.num_programs(0) - 1)
    def _():
        for part in range(4):
            summed = jnp.transpose(total_ref[part * wide : part * wide + wide])
            coarse = summed.astype(jnp.bfloat16)
            fine = (summed - coarse.astype(jnp.float32)).astype(jnp.bfloat16)
            lifted = jnp.dot(coarse, lift_ref[...], preferred_element_type=jnp.float32)
            lifted += jnp.dot(fine, lift_ref[...], preferred_element_type=jnp.float32)
            cells_ref[:, part * 512 : part * 512 + 512] = lifted.astype(jnp.bfloat16)


def scatter_and_lift(messages, lift_weight):
    sources, rows, width = messages.shape
    lift_block = jnp.kron(jnp.eye(8, dtype=jnp.bfloat16), lift_weight)
    return pl.pallas_call(
        scatter_kernel,
        grid=(sources // BUCKETS,),
        in_specs=[
            pl.BlockSpec((BUCKETS, rows, width), lambda i: (i, 0, 0)),
            pl.BlockSpec((256, 512), lambda i: (0, 0)),
        ],
        out_specs=pl.BlockSpec((256, 2048), lambda i: (0, 0)),
        out_shape=jax.ShapeDtypeStruct((256, 2048), jnp.bfloat16),
        scratch_shapes=[pltpu.VMEM((1024, 256), jnp.float32)],
        compiler_params=pltpu.CompilerParams(vmem_limit_bytes=48 << 20),
        name="scatter",
    )(messages, lift_block)


def per_device(
    records, slot_voxels, brick_mask, lift_weight, leaf_convs, down_leaf, down_coarse, coarse_convs
):
    messages = pack_messages(records[0], slot_voxels[0])
    arrived = lax.all_to_all(messages, ("gx", "gy"), split_axis=0, concat_axis=0, tiled=True)
    cells = scatter_and_lift(arrived, lift_weight)
    voxel_cells = cells.reshape(16, 16, 16, 128).transpose(0, 2, 1, 3)
    leaf_occupied = spread_mask(brick_mask, BRICK, BRICK // 2)
    taps_first = leaf_taps(leaf_convs[0])
    taps_second = leaf_taps(leaf_convs[1])
    first_layer = leaf_layer(voxel_cells, taps_first, leaf_occupied[..., None])
    second_layer = leaf_layer(first_layer, taps_second, leaf_occupied[..., None])
    level_input = second_layer
    for level_index in range(3):
        factor = BRICK // 2 ** (level_index + 1)
        occupied = spread_mask(brick_mask, factor, factor)[..., None]
        if level_index == 0:
            kernel = down_leaf
            paired = level_input
        else:
            kernel = down_coarse[level_index - 1]
            size_x, size_y, size_z, width = level_input.shape
            paired = level_input.reshape(size_x, size_y, size_z // 2, 2 * width)
        shrunk = (jax.nn.relu(shrink_paired(paired, kernel)) * occupied).astype(jnp.bfloat16)
        level_input = coarse_layer(shrunk, coarse_convs[level_index], occupied)
    return (second_layer, level_input)


def solution(mesh):
    in_specs = (
        P(("gx", "gy"), None, None, None),
        P(("gx", "gy"), None, None),
        P("gx", "gy", None),
        P(),
        P(),
        P(),
        P(),
        P(),
    )
    out_specs = (P("gx", "gy", None, None), P("gx", "gy", None, None))
    return jax.shard_map(
        per_device, mesh=mesh, in_specs=in_specs, out_specs=out_specs, check_vma=False
    )
```

```python
import functools

import jax
import jax.numpy as jnp
from jax import lax
from jax.experimental import pallas as pl
from jax.experimental.pallas import tpu as pltpu
from jax.sharding import PartitionSpec as P

BRICK = 8
BUCKETS = 8


def pack_messages(records, slot_voxels):
    fours = slot_voxels.shape[-1] // 4
    high = (slot_voxels >> 9) * 16 + ((slot_voxels & 31) >> 1)
    low = ((slot_voxels >> 5) & 15) * 2 + (slot_voxels & 1)
    parity = lax.axis_index("gy") % 2
    source = lax.broadcasted_iota(jnp.int32, (4 * fours, 4, 2, fours), 0)
    quarter = lax.broadcasted_iota(jnp.int32, (4 * fours, 4, 2, fours), 1)
    side = lax.broadcasted_iota(jnp.int32, (4 * fours, 4, 2, fours), 2)
    row = lax.broadcasted_iota(jnp.int32, (4 * fours, 4, 2, fours), 3)
    picks = ((source == 4 * row + quarter) & (side == parity)).astype(jnp.bfloat16)
    picks = picks.reshape(4 * fours, 4 * 2 * fours)
    both = jnp.stack([high, low]).astype(jnp.bfloat16)
    ids = jnp.einsum("tds,sk->dtk", both, picks, preferred_element_type=jnp.float32)
    ids = ids.astype(jnp.bfloat16).reshape(slot_voxels.shape[0], 8, 2 * fours)
    return jnp.concatenate([records, ids], 1)


def scatter_kernel(
    msg_ref, lift_ref, cells_ref, west_ref, east_ref, south_ref, north_ref, total_ref
):
    step = pl.program_id(0)

    @pl.when(step == 0)
    def _():
        total_ref[...] = jnp.zeros_like(total_ref)

    wide = 256
    lanes = lax.broadcasted_iota(jnp.int32, (wide, wide), 0).astype(jnp.bfloat16)
    zero = jnp.zeros((32, wide), jnp.bfloat16)
    for quad in range(BUCKETS // 4):
        turned, ids = [], []
        for pair in range(2):
            first = quad * 4 + pair * 2
            rows = jnp.concatenate([msg_ref[first, 0:64], msg_ref[first + 1, 0:64]], 0)
            turned.append(jnp.transpose(rows))
            ids.append(
                msg_ref[first, 64:72].astype(jnp.float32)
                + msg_ref[first + 1, 64:72].astype(jnp.float32)
            )
        turned = jnp.concatenate(turned, 1)
        ids = jnp.concatenate(ids, 1)
        for quarter in range(4):
            features = turned[quarter * 32 : quarter * 32 + 32]
            high = jnp.broadcast_to(ids[quarter : quarter + 1], (wide, wide)).astype(jnp.bfloat16)
            low = jnp.broadcast_to(ids[quarter + 4 : quarter + 5], (32, wide)).astype(jnp.bfloat16)
            hot = jnp.where(lanes == high, 1.0, 0.0).astype(jnp.bfloat16)
            spread = jnp.concatenate(
                [jnp.where(low == jnp.bfloat16(value), features, zero) for value in range(32)], 0
            )
            total_ref[...] += lax.dot_general(
                spread, hot, (((1,), (1,)), ((), ())), preferred_element_type=jnp.float32
            )

    @pl.when(step == pl.num_programs(0) - 1)
    def _():
        for part in range(4):
            summed = jnp.transpose(total_ref[part * wide : part * wide + wide])
            coarse = summed.astype(jnp.bfloat16)
            west_ref[:, part * wide : part * wide + wide] = coarse[:64]
            east_ref[:, part * wide : part * wide + wide] = coarse[192:]
            if part == 0:
                south_ref[...] = coarse
            if part == 3:
                north_ref[...] = coarse
            fine = (summed - coarse.astype(jnp.float32)).astype(jnp.bfloat16)
            lifted = jnp.dot(coarse, lift_ref[...], preferred_element_type=jnp.float32)
            lifted += jnp.dot(fine, lift_ref[...], preferred_element_type=jnp.float32)
            cells_ref[:, part * 512 : part * 512 + 512] = lifted.astype(jnp.bfloat16)


def scatter_and_lift(messages, lift_block):
    sources, rows, width = messages.shape
    shapes = [(256, 2048), (64, 1024), (64, 1024), (256, 256), (256, 256)]
    return pl.pallas_call(
        scatter_kernel,
        grid=(sources // BUCKETS,),
        in_specs=[
            pl.BlockSpec((BUCKETS, rows, width), lambda i: (i, 0, 0)),
            pl.BlockSpec((256, 512), lambda i: (0, 0)),
        ],
        out_specs=[pl.BlockSpec(shape, lambda i: (0, 0)) for shape in shapes],
        out_shape=[jax.ShapeDtypeStruct(shape, jnp.bfloat16) for shape in shapes],
        scratch_shapes=[pltpu.VMEM((1024, 256), jnp.float32)],
        compiler_params=pltpu.CompilerParams(vmem_limit_bytes=24 << 20),
        name="scatter",
    )(messages, lift_block)


def leaf_taps_kernel(convs_ref, taps_ref):
    zero = jnp.zeros((64, 64), jnp.bfloat16)
    for layer in range(2):
        for dx in range(3):
            for kind in range(2):
                for step_y in range(4):
                    for half in range(2):
                        row = kind * 512 + step_y * 128 + half * 64
                        for out_y in range(2):
                            blocks = []
                            for out_z in range(2):
                                dy = step_y - out_y
                                if kind == 0:
                                    dz = half - out_z + 1
                                else:
                                    dz = 3 - out_z if half == 0 else -out_z
                                inside = 0 <= dy <= 2 and 0 <= dz <= 2
                                blocks.append(convs_ref[layer, dx, dy, dz] if inside else zero)
                            taps_ref[layer, dx, row : row + 64, out_y * 128 : out_y * 128 + 128] = (
                                jnp.concatenate(blocks, 1)
                            )


def leaf_taps(leaf_convs):
    return pl.pallas_call(
        leaf_taps_kernel,
        out_shape=jax.ShapeDtypeStruct((2, 3, 1024, 256), jnp.bfloat16),
        name="leaf_taps",
    )(leaf_convs)


def row_shifts(values, period):
    count = values.shape[0]
    place = lax.rem(lax.broadcasted_iota(jnp.int32, values.shape, 0), period)
    before = jnp.where(place == 0, 0.0, pltpu.roll(values, 1, 0))
    after = jnp.where(place == period - 1, 0.0, pltpu.roll(values, count - 1, 0))
    return before, after


def z_neighbours(values):
    before, after = row_shifts(values, 16)
    lane = lax.rem(lax.broadcasted_iota(jnp.int32, values.shape, 1), 128)
    return jnp.where(lane < 64, after, before).astype(jnp.bfloat16)


def leaf_kernel(
    cells_ref,
    west_ref,
    east_ref,
    south_ref,
    north_ref,
    lift_ref,
    taps_ref,
    down_leaf_ref,
    coarse_ref,
    down_ref,
    leaf_mask_ref,
    mid_mask_ref,
    features_ref,
    down_two_ref,
    cell_ref,
    cell_z_ref,
    one_ref,
    one_z_ref,
    down_one_ref,
    parts_ref,
):
    here_x = lax.axis_index("gx")
    here_y = lax.axis_index("gy")
    from_west = jnp.where(here_x > 0, 1.0, 0.0)
    from_east = jnp.where(here_x < lax.axis_size("gx") - 1, 1.0, 0.0)
    from_south = jnp.where(here_y > 0, 1.0, 0.0)
    from_north = jnp.where(here_y < lax.axis_size("gy") - 1, 1.0, 0.0)
    lift = lift_ref[...]

    def place(row, lane, values):
        rows, lanes = values.shape
        cell_ref[row : row + rows, lane : lane + lanes] = values.astype(jnp.bfloat16)

    cell_ref[64:320, 512:2560] = cells_ref[...]
    for part in range(4):
        for row, ref, flag in ((0, west_ref, from_west), (320, east_ref, from_east)):
            sums = ref[:, part * 256 : part * 256 + 256]
            lifted = jnp.dot(sums, lift, preferred_element_type=jnp.float32)
            place(row, 512 + part * 512, lifted * flag)
    for lane, ref, flag in ((0, south_ref, from_south), (2560, north_ref, from_north)):
        for row, rows, other in ((0, 64, from_west), (64, 256, 1.0), (320, 64, from_east)):
            lifted = jnp.dot(ref[row : row + rows], lift, preferred_element_type=jnp.float32)
            place(row, lane, lifted * (flag * other))

    @pl.loop(0, 12)
    def _(step):
        lanes = pl.ds(pl.multiple_of(step * 256, 256), 256)
        cell_z_ref[:, lanes] = z_neighbours(cell_ref[:, lanes].astype(jnp.float32))

    def sweep(layer, source_ref, source_z_ref, rows, step):
        lanes = pl.ds(pl.multiple_of(step * 256, 256), 512)
        pieces = []
        for dx in range(3):
            pieces.append(source_ref[dx * 16 : dx * 16 + rows, lanes])
            pieces.append(source_z_ref[dx * 16 : dx * 16 + rows, lanes])
        taps = taps_ref[layer].reshape(3072, 256)
        total = jnp.dot(jnp.concatenate(pieces, 1), taps, preferred_element_type=jnp.float32)
        return jnp.maximum(total, 0.0)

    @pl.loop(0, 11)
    def _(step):
        total = sweep(0, cell_ref, cell_z_ref, 352, step)
        masks = [leaf_mask_ref[(2 * step + half + 5) // 8, 16:368] for half in range(2)]
        values = (total * jnp.concatenate(masks, 1)).astype(jnp.bfloat16)
        lanes = pl.ds(pl.multiple_of(step * 256, 256), 256)
        one_ref[:, lanes] = values
        one_z_ref[:, lanes] = z_neighbours(values.astype(jnp.float32))

    @pl.loop(0, 10)
    def _(step):
        total = sweep(1, one_ref, one_z_ref, 320, step)
        mask = leaf_mask_ref[(2 * step + 6) // 8, 32:352]
        values = (total * jnp.concatenate([mask, mask], 1)).astype(jnp.bfloat16)

        @pl.when((step >= 1) & (step < 9))
        def _():
            for half in range(2):
                inner = values[32:288, half * 128 : half * 128 + 128]
                features_ref[:, 2 * step - 2 + half] = inner.reshape(16, 16, 128)

        pairs = values.reshape(10, 2, 16, 256)
        merged = jnp.concatenate(
            [pairs[:, 0].reshape(160, 256), pairs[:, 1].reshape(160, 256)], 1
        )
        total = jnp.dot(merged, down_leaf_ref[...], preferred_element_type=jnp.float32)
        mask = mask.reshape(10, 2, 16, 128)[:, 0].reshape(160, 128)
        down = (jnp.maximum(total, 0.0) * mask).astype(jnp.bfloat16)
        before, after = row_shifts(down.astype(jnp.float32), 16)
        lanes = pl.ds(pl.multiple_of(step * 128, 128), 128)
        down_one_ref[0, :, lanes] = before.astype(jnp.bfloat16)
        down_one_ref[1, :, lanes] = down
        down_one_ref[2, :, lanes] = after.astype(jnp.bfloat16)

    windows = []
    for y in range(8):
        windows.append(
            jnp.concatenate(
                [
                    down_one_ref[dz, dx * 16 : dx * 16 + 128, y * 128 : y * 128 + 384]
                    for dx in range(3)
                    for dz in range(3)
                ],
                1,
            )
        )
    total = jnp.dot(jnp.concatenate(windows, 0), coarse_ref[...], preferred_element_type=jnp.float32)
    total = jnp.maximum(total, 0.0).reshape(8, 128, 128)
    masks = [leaf_mask_ref[1 + y // 4, 64:320].reshape(8, 2, 16, 128)[:, 0] for y in range(8)]
    level = total * jnp.concatenate(masks, 0).reshape(8, 128, 128)
    level = level.astype(jnp.bfloat16).reshape(4, 2, 4, 2, 16, 128)
    merged = jnp.concatenate(
        [level[:, b, :, a].reshape(256, 128) for a in range(2) for b in range(2)], 1
    )
    parts = jnp.dot(merged, down_ref[...], preferred_element_type=jnp.float32)
    parts_ref[0] = parts[:, :128]
    parts_ref[1] = parts[:, 128:]
    total = parts_ref[0, pl.ds(0, 128, stride=2)] + parts_ref[1, pl.ds(1, 128, stride=2)]
    mask = mid_mask_ref[2:6, 2:6].reshape(128, 128)
    down_two_ref[...] = (jnp.maximum(total, 0.0) * mask).astype(jnp.bfloat16)


def leaf_levels(cells, halos, lift_block, taps, down_leaf, coarse, down, leaf_mask, mid_mask):
    return pl.pallas_call(
        leaf_kernel,
        out_shape=[
            jax.ShapeDtypeStruct((16, 16, 16, 128), jnp.bfloat16),
            jax.ShapeDtypeStruct((128, 128), jnp.bfloat16),
        ],
        scratch_shapes=[
            pltpu.VMEM((384, 3072), jnp.bfloat16),
            pltpu.VMEM((384, 3072), jnp.bfloat16),
            pltpu.VMEM((352, 2816), jnp.bfloat16),
            pltpu.VMEM((352, 2816), jnp.bfloat16),
            pltpu.VMEM((3, 160, 1280), jnp.bfloat16),
            pltpu.VMEM((2, 256, 128), jnp.float32),
        ],
        compiler_params=pltpu.CompilerParams(vmem_limit_bytes=40 << 20),
        name="leaf_levels",
    )(cells, *halos, lift_block, taps, down_leaf, coarse, down, leaf_mask, mid_mask)


def coarse_kernel(
    south_ref,
    middle_ref,
    north_ref,
    coarse_ref,
    down_ref,
    last_ref,
    mid_mask_ref,
    top_mask_ref,
    top_ref,
    parts_ref,
):
    here_x = lax.axis_index("gx")
    here_y = lax.axis_index("gy")
    from_west = jnp.where(here_x > 0, 1.0, 0.0)
    from_east = jnp.where(here_x < lax.axis_size("gx") - 1, 1.0, 0.0)
    from_south = jnp.where(here_y > 0, 1.0, 0.0)
    from_north = jnp.where(here_y < lax.axis_size("gy") - 1, 1.0, 0.0)

    strips = []
    for ref, first, flag in ((south_ref, 1, from_south), (middle_ref, 0, 1.0), (north_ref, 0, from_north)):
        count = 4 if ref is middle_ref else 3
        tiles = [ref[i].astype(jnp.float32).reshape(4, 4, 8, 128) for i in range(3)]
        tiles = [tile[first : first + count] for tile in tiles]
        tiles = [
            tiles[0][:, 1:] * (flag * from_west),
            tiles[1] * flag,
            tiles[2][:, :3] * (flag * from_east),
        ]
        strips.append(jnp.concatenate(tiles, 1))
    grid = jnp.concatenate(strips, 0)
    before, after = row_shifts(grid.reshape(800, 128), 8)
    grids = [before.reshape(10, 10, 8, 128), grid, after.reshape(10, 10, 8, 128)]
    pieces = [
        grids[dz][dy : dy + 8, dx : dx + 8].reshape(512, 128).astype(jnp.bfloat16)
        for dx in range(3)
        for dy in range(3)
        for dz in range(3)
    ]
    total = jnp.dot(jnp.concatenate(pieces, 1), coarse_ref[...], preferred_element_type=jnp.float32)
    level = jnp.maximum(total, 0.0) * mid_mask_ref[...].reshape(512, 128)
    level = level.reshape(4, 2, 4, 2, 8, 128)
    merged = jnp.concatenate(
        [level[:, b, :, a].reshape(128, 128) for a in range(2) for b in range(2)], 1
    ).astype(jnp.bfloat16)
    parts = jnp.dot(merged, down_ref[...], preferred_element_type=jnp.float32)
    parts_ref[0] = parts[:, :128]
    parts_ref[1] = parts[:, 128:]
    total = parts_ref[0, pl.ds(0, 64, stride=2)] + parts_ref[1, pl.ds(1, 64, stride=2)]
    down = jnp.maximum(total, 0.0) * top_mask_ref[...]
    down = down.astype(jnp.bfloat16).astype(jnp.float32)
    before, after = row_shifts(down, 4)
    shifted = [before, down, after]
    pieces = []
    for dx in range(3):
        for dy in range(3):
            for dz in range(3):
                turn = (64 - (dy - 1) * 16 - (dx - 1) * 4) % 64
                moved = pltpu.roll(shifted[dz], turn, 0) if turn else shifted[dz]
                pieces.append(moved.astype(jnp.bfloat16))
    total = jnp.dot(jnp.concatenate(pieces, 1), last_ref[...], preferred_element_type=jnp.float32)
    top = (jnp.maximum(total, 0.0) * top_mask_ref[...]).astype(jnp.bfloat16)
    for x in range(2):
        for y in range(2):
            row = (y + 1) * 16 + (x + 1) * 4
            top_ref[x, y] = top[row : row + 4]


def coarse_levels(south, middle, north, coarse, down, last, mid_mask, top_mask):
    return pl.pallas_call(
        coarse_kernel,
        out_shape=jax.ShapeDtypeStruct((2, 2, 4, 128), jnp.bfloat16),
        scratch_shapes=[pltpu.VMEM((2, 128, 128), jnp.float32)],
        compiler_params=pltpu.CompilerParams(vmem_limit_bytes=24 << 20),
        name="coarse_levels",
    )(south, middle, north, coarse, down, last, mid_mask, top_mask)


def ring(values, axis, step):
    count = lax.axis_size(axis)
    return lax.ppermute(values, axis, [(i, (i + step) % count) for i in range(count)])


def masks_of(brick_mask):
    size_x, size_y, size_z = brick_mask.shape
    count_x, count_y = lax.axis_size("gx"), lax.axis_size("gy")
    whole = lax.all_gather(brick_mask, ("gx", "gy"), axis=0, tiled=False)
    whole = whole.reshape(count_x, count_y, size_x, size_y, size_z).transpose(0, 2, 1, 3, 4)
    whole = whole.reshape(count_x * size_x, count_y * size_y, size_z).astype(jnp.float32)
    whole = jnp.pad(whole, ((1, 1), (1, 1), (0, 0)))
    start = (lax.axis_index("gx") * size_x, lax.axis_index("gy") * size_y, 0)
    near = lax.dynamic_slice(whole, start, (size_x + 2, size_y + 2, size_z))
    near = near.transpose(1, 0, 2)
    leaf = jnp.repeat(jnp.repeat(near, 8, 1)[:, 4:28], 4, 2).reshape(4, 384, 1)
    middle = jnp.repeat(jnp.repeat(jnp.repeat(near, 2, 0), 2, 1), 2, 2)[..., None]
    top = near.reshape(64, 1)
    return (
        jnp.broadcast_to(leaf, (4, 384, 128)),
        jnp.broadcast_to(middle, (8, 8, 8, 128)),
        jnp.broadcast_to(top, (64, 128)),
    )


def per_device(
    records, slot_voxels, brick_mask, lift_weight, leaf_convs, down_leaf, down_coarse, coarse_convs
):
    messages = pack_messages(records[0], slot_voxels[0])
    arrived = lax.all_to_all(messages, ("gx", "gy"), split_axis=0, concat_axis=0, tiled=True)
    leaf_mask, mid_mask, top_mask = masks_of(brick_mask)
    lift_block = jnp.kron(jnp.eye(8, dtype=jnp.bfloat16), lift_weight)
    taps = leaf_taps(leaf_convs)
    coarse_one = coarse_convs[0].transpose(0, 2, 1, 3, 4).reshape(3456, 128)
    coarse_two = coarse_convs[1].reshape(3456, 128)
    coarse_three = coarse_convs[2].reshape(3456, 128)
    downs = down_coarse.transpose(0, 1, 2, 4, 3, 5).reshape(2, 512, 256)

    cells, low_x, high_x, low_y, high_y = scatter_and_lift(arrived, lift_block)
    west = ring(high_x, "gx", 1)
    east = ring(low_x, "gx", -1)
    south = ring(jnp.concatenate([west[:, 768:], high_y, east[:, 768:]], 0), "gy", 1)
    north = ring(jnp.concatenate([west[:, :256], low_y, east[:, :256]], 0), "gy", -1)
    features, down_two = leaf_levels(
        cells,
        (west, east, south, north),
        lift_block,
        taps,
        down_leaf.reshape(512, 128),
        coarse_one,
        downs[0],
        leaf_mask,
        mid_mask,
    )
    middle = jnp.stack([ring(down_two, "gx", 1), down_two, ring(down_two, "gx", -1)])
    top = coarse_levels(
        ring(middle, "gy", 1),
        middle,
        ring(middle, "gy", -1),
        coarse_two,
        downs[1],
        coarse_three,
        mid_mask,
        top_mask,
    )
    return (features, top)


def solution(mesh):
    in_specs = (
        P(("gx", "gy"), None, None, None),
        P(("gx", "gy"), None, None),
        P("gx", "gy", None),
        P(),
        P(),
        P(),
        P(),
        P(),
    )
    out_specs = (P("gx", "gy", None, None), P("gx", "gy", None, None))
    return jax.shard_map(
        per_device, mesh=mesh, in_specs=in_specs, out_specs=out_specs, check_vma=False
    )
```

```python
import functools

import jax
import jax.numpy as jnp
from jax import lax
from jax.experimental import pallas as pl
from jax.experimental.pallas import tpu as pltpu
from jax.sharding import PartitionSpec as P

BRICK = 8
BUCKETS = 8


def pack_kernel(records_ref, slots_ref, bricks_ref, messages_ref, ids_ref, records_sem, ids_sem):
    buckets = slots_ref.shape[0]
    chunk = buckets // 8
    copies = []
    for part in range(8):
        copies.append(
            pltpu.make_async_copy(
                records_ref.at[part * chunk : part * chunk + chunk],
                messages_ref.at[part * chunk : part * chunk + chunk, 0:64],
                records_sem.at[part],
            )
        )
    for copy in copies:
        copy.start()
    side = lax.rem(lax.axis_index("gy"), 2)
    slot = lax.broadcasted_iota(jnp.int32, (256, 128), 0)
    lane = lax.broadcasted_iota(jnp.int32, (256, 128), 1)
    picks = jnp.where((slot >> 2) + side * 64 == lane, 1.0, 0.0).astype(jnp.bfloat16)
    level = lax.broadcasted_iota(jnp.int32, (8, 128), 0) // 2
    place = lax.broadcasted_iota(jnp.int32, (8, 128), 1) - (1 - side) * 64
    bricks = jnp.zeros((8, 128), jnp.int32)
    for column in range(4):
        for z in range(4):
            here = (level == z) & (place >= column * 16) & (place < column * 16 + 16)
            bricks = jnp.where(here, bricks_ref[column // 2, column % 2, z], bricks)
    bricks = jnp.broadcast_to(bricks.astype(jnp.float32)[None], (chunk, 8, 128))
    shape = (chunk, 8, 256)
    row = lax.broadcasted_iota(jnp.int32, shape, 1)
    mine = (lax.broadcasted_iota(jnp.int32, shape, 2) & 3) == (row & 3)

    @pl.loop(0, 8)
    def _(part):
        here = pl.ds(pl.multiple_of(part * chunk, chunk), chunk)
        slots = slots_ref[here]
        high = (slots >> 9) * 16 + ((slots & 31) >> 1)
        low = ((slots >> 5) & 15) * 2 + (slots & 1)
        both = jnp.where(
            row < 4,
            jnp.broadcast_to(high.reshape(chunk, 1, 256), shape),
            jnp.broadcast_to(low.reshape(chunk, 1, 256), shape),
        )
        both = jnp.where(mine, both, 0).astype(jnp.float32)
        both = both.reshape(chunk * 8, 256).astype(jnp.bfloat16)
        ids = jnp.dot(both, picks, preferred_element_type=jnp.float32)
        ids_ref[here] = (ids.reshape(chunk, 8, 128) + bricks).astype(jnp.bfloat16)

    copies.append(pltpu.make_async_copy(ids_ref, messages_ref.at[:, 64:72], ids_sem))
    copies[-1].start()
    for copy in copies:
        copy.wait()


def pack_messages(records, slot_voxels, brick_mask):
    buckets, rows, width = records.shape
    return pl.pallas_call(
        pack_kernel,
        in_specs=[
            pl.BlockSpec(memory_space=pltpu.HBM),
            pl.BlockSpec(memory_space=pltpu.VMEM),
            pl.BlockSpec(memory_space=pltpu.SMEM),
        ],
        out_specs=pl.BlockSpec(memory_space=pltpu.HBM),
        out_shape=jax.ShapeDtypeStruct((buckets, rows + 8, width), jnp.bfloat16),
        scratch_shapes=[
            pltpu.VMEM((buckets, 8, width), jnp.bfloat16),
            pltpu.SemaphoreType.DMA((8,)),
            pltpu.SemaphoreType.DMA,
        ],
        name="pack",
    )(records, slot_voxels, brick_mask)


def scatter_kernel(
    msg_ref, lift_ref, cells_ref, west_ref, east_ref, south_ref, north_ref, total_ref
):
    step = pl.program_id(0)

    @pl.when(step == 0)
    def _():
        total_ref[...] = jnp.zeros_like(total_ref)

    wide = 256
    lanes = lax.broadcasted_iota(jnp.int32, (wide, wide), 0).astype(jnp.bfloat16)
    zero = jnp.zeros((32, wide), jnp.bfloat16)
    left = lax.broadcasted_iota(jnp.int32, (8, 128), 1) < 64
    for quad in range(BUCKETS // 4):
        turned, ids = [], []
        for pair in range(2):
            first = quad * 4 + pair * 2
            rows = jnp.concatenate([msg_ref[first, 0:64], msg_ref[first + 1, 0:64]], 0)
            turned.append(jnp.transpose(rows))
            ids.append(
                jnp.where(
                    left,
                    msg_ref[first, 64:72].astype(jnp.float32),
                    msg_ref[first + 1, 64:72].astype(jnp.float32),
                )
            )
        turned = jnp.concatenate(turned, 1)
        ids = jnp.concatenate(ids, 1)
        for quarter in range(4):
            features = turned[quarter * 32 : quarter * 32 + 32]
            high = jnp.broadcast_to(ids[quarter : quarter + 1], (wide, wide)).astype(jnp.bfloat16)
            low = jnp.broadcast_to(ids[quarter + 4 : quarter + 5], (32, wide)).astype(jnp.bfloat16)
            hot = jnp.where(lanes == high, 1.0, 0.0).astype(jnp.bfloat16)
            spread = jnp.concatenate(
                [jnp.where(low == jnp.bfloat16(value), features, zero) for value in range(32)], 0
            )
            total_ref[...] += lax.dot_general(
                spread, hot, (((1,), (1,)), ((), ())), preferred_element_type=jnp.float32
            )

    @pl.when(step == pl.num_programs(0) - 1)
    def _():
        for part in range(4):
            summed = jnp.transpose(total_ref[part * wide : part * wide + wide])
            coarse = summed.astype(jnp.bfloat16)
            west_ref[:, part * wide : part * wide + wide] = coarse[:64]
            east_ref[:, part * wide : part * wide + wide] = coarse[192:]
            if part == 0:
                south_ref[...] = coarse
            if part == 3:
                north_ref[...] = coarse
            fine = (summed - coarse.astype(jnp.float32)).astype(jnp.bfloat16)
            lifted = jnp.dot(coarse, lift_ref[...], preferred_element_type=jnp.float32)
            lifted += jnp.dot(fine, lift_ref[...], preferred_element_type=jnp.float32)
            cells_ref[:, part * 512 : part * 512 + 512] = lifted.astype(jnp.bfloat16)


def scatter_and_lift(messages, lift_block):
    sources, rows, width = messages.shape
    shapes = [(256, 2048), (64, 1024), (64, 1024), (256, 256), (256, 256)]
    return pl.pallas_call(
        scatter_kernel,
        grid=(sources // BUCKETS,),
        in_specs=[
            pl.BlockSpec((BUCKETS, rows, width), lambda i: (i, 0, 0)),
            pl.BlockSpec((256, 512), lambda i: (0, 0)),
        ],
        out_specs=[pl.BlockSpec(shape, lambda i: (0, 0)) for shape in shapes],
        out_shape=[jax.ShapeDtypeStruct(shape, jnp.bfloat16) for shape in shapes],
        scratch_shapes=[pltpu.VMEM((1024, 256), jnp.float32)],
        compiler_params=pltpu.CompilerParams(vmem_limit_bytes=12 << 20),
        name="scatter",
    )(messages, lift_block)


def leaf_taps_kernel(convs_ref, taps_ref):
    zero = jnp.zeros((64, 64), jnp.bfloat16)
    for layer in range(2):
        for dx in range(3):
            for kind in range(2):
                for step_y in range(4):
                    for half in range(2):
                        row = kind * 512 + step_y * 128 + half * 64
                        for out_y in range(2):
                            blocks = []
                            for out_z in range(2):
                                dy = step_y - out_y
                                if kind == 0:
                                    dz = half - out_z + 1
                                else:
                                    dz = 3 - out_z if half == 0 else -out_z
                                inside = 0 <= dy <= 2 and 0 <= dz <= 2
                                blocks.append(convs_ref[layer, dx, dy, dz] if inside else zero)
                            taps_ref[layer, dx, row : row + 64, out_y * 128 : out_y * 128 + 128] = (
                                jnp.concatenate(blocks, 1)
                            )


def leaf_taps(leaf_convs):
    return pl.pallas_call(
        leaf_taps_kernel,
        out_shape=jax.ShapeDtypeStruct((2, 3, 1024, 256), jnp.bfloat16),
        name="leaf_taps",
    )(leaf_convs)


def row_shifts(values, period):
    count = values.shape[0]
    place = lax.rem(lax.broadcasted_iota(jnp.int32, values.shape, 0), period)
    before = jnp.where(place == 0, 0.0, pltpu.roll(values, 1, 0))
    after = jnp.where(place == period - 1, 0.0, pltpu.roll(values, count - 1, 0))
    return before, after


def z_neighbours(values):
    before, after = row_shifts(values, 16)
    lane = lax.rem(lax.broadcasted_iota(jnp.int32, values.shape, 1), 128)
    return jnp.where(lane < 64, after, before).astype(jnp.bfloat16)


def spread_bricks(near, flags):
    side = lax.rem(lax.axis_index("gy"), 2)
    columns = []
    for y in range(4):
        for x in range(4):
            source_x, source_y = (0, 1, 1, 2)[x], (0, 1, 1, 2)[y]
            lane = ((1, 0, 1, 0)[x] * 2 + (1, 0, 1, 0)[y]) * 16
            tile = near[source_x * 3 + source_y].astype(jnp.float32)
            upper = side == 0 if source_y == 1 else side == 1
            value = jnp.where(upper, tile[:, 64 + lane : 65 + lane], tile[:, lane : lane + 1])
            flag = flags[0][source_x] * flags[1][source_y]
            columns.append(jnp.broadcast_to(value, (8, 128)) * flag)
    return columns


def doubled(column):
    level = lax.broadcasted_iota(jnp.int32, (16, 128), 0) // 4
    tile = jnp.broadcast_to(column[0:1], (16, 128))
    for z in range(1, 4):
        tile = jnp.where(level == z, jnp.broadcast_to(column[2 * z : 2 * z + 1], (16, 128)), tile)
    return tile


def leaf_kernel(
    cells_ref,
    west_ref,
    east_ref,
    south_ref,
    north_ref,
    lift_ref,
    taps_ref,
    down_leaf_ref,
    coarse_ref,
    down_ref,
    arrived_ref,
    features_ref,
    down_two_ref,
    bricks_ref,
    cell_ref,
    cell_z_ref,
    one_ref,
    one_z_ref,
    down_one_ref,
    parts_ref,
    down_leaf_vmem,
    coarse_vmem,
    down_vmem,
    leaf_mask_ref,
    near_vmem,
    near_sem,
    leaf_sem,
    coarse_sem,
    down_sem,
):
    here_x = lax.axis_index("gx")
    here_y = lax.axis_index("gy")
    last_x, last_y = lax.axis_size("gx") - 1, lax.axis_size("gy") - 1
    near_copies = []
    for x in range(3):
        for y in range(3):
            source = jnp.clip(here_x + x - 1, 0, last_x) * (last_y + 1)
            source = source + jnp.clip(here_y + y - 1, 0, last_y)
            near_copies.append(
                pltpu.make_async_copy(
                    arrived_ref.at[source, 64:72], near_vmem.at[x * 3 + y], near_sem.at[x, y]
                )
            )
    for copy in near_copies:
        copy.start()
    copies = [pltpu.make_async_copy(down_leaf_ref, down_leaf_vmem, leaf_sem)]
    for dx in range(3):
        for dz in range(3):
            copies.append(
                pltpu.make_async_copy(
                    coarse_ref.at[0, dx, :, dz], coarse_vmem.at[dx, dz], coarse_sem.at[dx, dz]
                )
            )
    for a in range(2):
        for b in range(2):
            for c in range(2):
                copies.append(
                    pltpu.make_async_copy(
                        down_ref.at[0, a, b, c],
                        down_vmem.at[a, b, :, c * 128 : c * 128 + 128],
                        down_sem.at[a, b, c],
                    )
                )
    for copy in copies:
        copy.start()

    from_west = jnp.where(here_x > 0, 1.0, 0.0)
    from_east = jnp.where(here_x < last_x, 1.0, 0.0)
    from_south = jnp.where(here_y > 0, 1.0, 0.0)
    from_north = jnp.where(here_y < last_y, 1.0, 0.0)
    lift = lift_ref[...]

    def place(row, lane, values):
        rows, lanes = values.shape
        cell_ref[row : row + rows, lane : lane + lanes] = values.astype(jnp.bfloat16)

    cell_ref[64:320, 512:2560] = cells_ref[...]
    for part in range(4):
        for row, ref, flag in ((0, west_ref, from_west), (320, east_ref, from_east)):
            sums = ref[:, part * 256 : part * 256 + 256]
            lifted = jnp.dot(sums, lift, preferred_element_type=jnp.float32)
            place(row, 512 + part * 512, lifted * flag)
    for lane, ref, flag in ((0, south_ref, from_south), (2560, north_ref, from_north)):
        for row, rows, other in ((0, 64, from_west), (64, 256, 1.0), (320, 64, from_east)):
            lifted = jnp.dot(ref[row : row + rows], lift, preferred_element_type=jnp.float32)
            place(row, lane, lifted * (flag * other))

    for copy in near_copies:
        copy.wait()
    flags = ((from_west, 1.0, from_east), (from_south, 1.0, from_north))
    columns = spread_bricks([near_vmem[i] for i in range(9)], flags)
    for y in range(4):
        for x in range(4):
            bricks_ref[y * 4 + x] = columns[y * 4 + x]
            tile = doubled(columns[y * 4 + x])
            for place_x in range(*((0, 4), (4, 12), (12, 20), (20, 24))[x]):
                leaf_mask_ref[y, place_x * 16 : place_x * 16 + 16] = tile

    @pl.loop(0, 12)
    def _(step):
        lanes = pl.ds(pl.multiple_of(step * 256, 256), 256)
        cell_z_ref[:, lanes] = z_neighbours(cell_ref[:, lanes].astype(jnp.float32))

    def sweep(layer, source_ref, source_z_ref, rows, step):
        lanes = pl.ds(pl.multiple_of(step * 256, 256), 512)
        pieces = []
        for dx in range(3):
            pieces.append(source_ref[dx * 16 : dx * 16 + rows, lanes])
            pieces.append(source_z_ref[dx * 16 : dx * 16 + rows, lanes])
        taps = taps_ref[layer].reshape(3072, 256)
        total = jnp.dot(jnp.concatenate(pieces, 1), taps, preferred_element_type=jnp.float32)
        return jnp.maximum(total, 0.0)

    @pl.loop(0, 11)
    def _(step):
        total = sweep(0, cell_ref, cell_z_ref, 352, step)
        masks = [leaf_mask_ref[(2 * step + half + 5) // 8, 16:368] for half in range(2)]
        values = (total * jnp.concatenate(masks, 1)).astype(jnp.bfloat16)
        lanes = pl.ds(pl.multiple_of(step * 256, 256), 256)
        one_ref[:, lanes] = values
        one_z_ref[:, lanes] = z_neighbours(values.astype(jnp.float32))

    copies[0].wait()

    @pl.loop(0, 10)
    def _(step):
        total = sweep(1, one_ref, one_z_ref, 320, step)
        mask = leaf_mask_ref[(2 * step + 6) // 8, 32:352]
        values = (total * jnp.concatenate([mask, mask], 1)).astype(jnp.bfloat16)

        @pl.when((step >= 1) & (step < 9))
        def _():
            for half in range(2):
                inner = values[32:288, half * 128 : half * 128 + 128]
                features_ref[:, 2 * step - 2 + half] = inner.reshape(16, 16, 128)

        pairs = values.reshape(10, 2, 16, 256)
        merged = jnp.concatenate(
            [pairs[:, 0].reshape(160, 256), pairs[:, 1].reshape(160, 256)], 1
        )
        total = jnp.dot(merged, down_leaf_vmem[...].reshape(512, 128), preferred_element_type=jnp.float32)
        mask = mask.reshape(10, 2, 16, 128)[:, 0].reshape(160, 128)
        down = (jnp.maximum(total, 0.0) * mask).astype(jnp.bfloat16)
        before, after = row_shifts(down.astype(jnp.float32), 16)
        lanes = pl.ds(pl.multiple_of(step * 128, 128), 128)
        down_one_ref[0, :, lanes] = before.astype(jnp.bfloat16)
        down_one_ref[1, :, lanes] = down
        down_one_ref[2, :, lanes] = after.astype(jnp.bfloat16)

    for copy in copies[1:]:
        copy.wait()
    windows = []
    for y in range(8):
        windows.append(
            jnp.concatenate(
                [
                    down_one_ref[dz, dx * 16 : dx * 16 + 128, y * 128 : y * 128 + 384]
                    for dx in range(3)
                    for dz in range(3)
                ],
                1,
            )
        )
    taps = coarse_vmem[...].reshape(3456, 128)
    total = jnp.dot(jnp.concatenate(windows, 0), taps, preferred_element_type=jnp.float32)
    total = jnp.maximum(total, 0.0).reshape(8, 128, 128)
    masks = [leaf_mask_ref[1 + y // 4, 64:320].reshape(8, 2, 16, 128)[:, 0] for y in range(8)]
    level = total * jnp.concatenate(masks, 0).reshape(8, 128, 128)
    level = level.astype(jnp.bfloat16).reshape(4, 2, 4, 2, 16, 128)
    merged = jnp.concatenate(
        [level[:, b, :, a].reshape(256, 128) for a in range(2) for b in range(2)], 1
    )
    taps = down_vmem[...].reshape(512, 256)
    parts = jnp.dot(merged, taps, preferred_element_type=jnp.float32)
    parts_ref[0] = parts[:, :128]
    parts_ref[1] = parts[:, 128:]
    total = parts_ref[0, pl.ds(0, 128, stride=2)] + parts_ref[1, pl.ds(1, 128, stride=2)]
    tiles = [bricks_ref[(1 + y // 2) * 4 + 1 + x // 2] for y in range(4) for x in range(4)]
    mask = jnp.concatenate(tiles, 0)
    down_two_ref[...] = (jnp.maximum(total, 0.0) * mask).astype(jnp.bfloat16)


def leaf_levels(cells, halos, lift_block, taps, down_leaf, coarse, down, arrived):
    return pl.pallas_call(
        leaf_kernel,
        out_shape=[
            jax.ShapeDtypeStruct((16, 16, 16, 128), jnp.bfloat16),
            jax.ShapeDtypeStruct((128, 128), jnp.bfloat16),
            jax.ShapeDtypeStruct((16, 8, 128), jnp.float32),
        ],
        in_specs=[pl.BlockSpec(memory_space=pltpu.VMEM)] * 7
        + [pl.BlockSpec(memory_space=pltpu.HBM)] * 4,
        scratch_shapes=[
            pltpu.VMEM((384, 3072), jnp.bfloat16),
            pltpu.VMEM((384, 3072), jnp.bfloat16),
            pltpu.VMEM((352, 2816), jnp.bfloat16),
            pltpu.VMEM((352, 2816), jnp.bfloat16),
            pltpu.VMEM((3, 160, 1280), jnp.bfloat16),
            pltpu.VMEM((2, 256, 128), jnp.float32),
            pltpu.VMEM((2, 2, 2, 64, 128), jnp.bfloat16),
            pltpu.VMEM((3, 3, 3, 128, 128), jnp.bfloat16),
            pltpu.VMEM((2, 2, 128, 256), jnp.bfloat16),
            pltpu.VMEM((4, 384, 128), jnp.float32),
            pltpu.VMEM((9, 8, 128), jnp.bfloat16),
            pltpu.SemaphoreType.DMA((3, 3)),
            pltpu.SemaphoreType.DMA,
            pltpu.SemaphoreType.DMA((3, 3)),
            pltpu.SemaphoreType.DMA((2, 2, 2)),
        ],
        compiler_params=pltpu.CompilerParams(vmem_limit_bytes=24 << 20),
        name="leaf_levels",
    )(cells, *halos, lift_block, taps, down_leaf, coarse, down, arrived)


def coarse_kernel(
    south_ref,
    middle_ref,
    north_ref,
    coarse_ref,
    down_ref,
    bricks_ref,
    top_ref,
    parts_ref,
    coarse_vmem,
    last_vmem,
    down_vmem,
    coarse_sem,
    last_sem,
    down_sem,
):
    copies = [
        pltpu.make_async_copy(coarse_ref.at[1], coarse_vmem, coarse_sem),
        pltpu.make_async_copy(coarse_ref.at[2], last_vmem, last_sem),
    ]
    for a in range(2):
        for b in range(2):
            for c in range(2):
                copies.append(
                    pltpu.make_async_copy(
                        down_ref.at[1, a, b, c],
                        down_vmem.at[a, b, :, c * 128 : c * 128 + 128],
                        down_sem.at[a, b, c],
                    )
                )
    for copy in copies:
        copy.start()
    here_x = lax.axis_index("gx")
    here_y = lax.axis_index("gy")
    from_west = jnp.where(here_x > 0, 1.0, 0.0)
    from_east = jnp.where(here_x < lax.axis_size("gx") - 1, 1.0, 0.0)
    from_south = jnp.where(here_y > 0, 1.0, 0.0)
    from_north = jnp.where(here_y < lax.axis_size("gy") - 1, 1.0, 0.0)

    strips = []
    for ref, first, flag in ((south_ref, 1, from_south), (middle_ref, 0, 1.0), (north_ref, 0, from_north)):
        count = 4 if ref is middle_ref else 3
        tiles = [ref[i].astype(jnp.float32).reshape(4, 4, 8, 128) for i in range(3)]
        tiles = [tile[first : first + count] for tile in tiles]
        tiles = [
            tiles[0][:, 1:] * (flag * from_west),
            tiles[1] * flag,
            tiles[2][:, :3] * (flag * from_east),
        ]
        strips.append(jnp.concatenate(tiles, 1))
    grid = jnp.concatenate(strips, 0)
    before, after = row_shifts(grid.reshape(800, 128), 8)
    grids = [before.reshape(10, 10, 8, 128), grid, after.reshape(10, 10, 8, 128)]
    pieces = [
        grids[dz][dy : dy + 8, dx : dx + 8].reshape(512, 128).astype(jnp.bfloat16)
        for dx in range(3)
        for dy in range(3)
        for dz in range(3)
    ]
    for copy in copies:
        copy.wait()
    taps = coarse_vmem[...].reshape(3456, 128)
    total = jnp.dot(jnp.concatenate(pieces, 1), taps, preferred_element_type=jnp.float32)
    tiles = [bricks_ref[y // 2 * 4 + x // 2] for y in range(8) for x in range(8)]
    mask = jnp.concatenate(tiles, 0)
    level = jnp.maximum(total, 0.0) * mask
    level = level.reshape(4, 2, 4, 2, 8, 128)
    merged = jnp.concatenate(
        [level[:, b, :, a].reshape(128, 128) for a in range(2) for b in range(2)], 1
    ).astype(jnp.bfloat16)
    taps = down_vmem[...].reshape(512, 256)
    parts = jnp.dot(merged, taps, preferred_element_type=jnp.float32)
    parts_ref[0] = parts[:, :128]
    parts_ref[1] = parts[:, 128:]
    total = parts_ref[0, pl.ds(0, 64, stride=2)] + parts_ref[1, pl.ds(1, 64, stride=2)]
    picks = lax.broadcasted_iota(jnp.int32, (64, 128), 0) * 2
    picks = picks == lax.broadcasted_iota(jnp.int32, (64, 128), 1)
    picks = jnp.where(picks, 1.0, 0.0).astype(jnp.bfloat16)
    bricks = bricks_ref[...].reshape(128, 128).astype(jnp.bfloat16)
    mask = jnp.dot(picks, bricks, preferred_element_type=jnp.float32)
    down = jnp.maximum(total, 0.0) * mask
    down = down.astype(jnp.bfloat16).astype(jnp.float32)
    before, after = row_shifts(down, 4)
    shifted = [before, down, after]
    pieces = []
    for dx in range(3):
        for dy in range(3):
            for dz in range(3):
                turn = (64 - (dy - 1) * 16 - (dx - 1) * 4) % 64
                moved = pltpu.roll(shifted[dz], turn, 0) if turn else shifted[dz]
                pieces.append(moved.astype(jnp.bfloat16))
    taps = last_vmem[...].reshape(3456, 128)
    total = jnp.dot(jnp.concatenate(pieces, 1), taps, preferred_element_type=jnp.float32)
    top = (jnp.maximum(total, 0.0) * mask).astype(jnp.bfloat16)
    for x in range(2):
        for y in range(2):
            row = (y + 1) * 16 + (x + 1) * 4
            top_ref[x, y] = top[row : row + 4]


def coarse_levels(south, middle, north, coarse, down, bricks):
    return pl.pallas_call(
        coarse_kernel,
        out_shape=jax.ShapeDtypeStruct((2, 2, 4, 128), jnp.bfloat16),
        in_specs=[pl.BlockSpec(memory_space=pltpu.VMEM)] * 3
        + [pl.BlockSpec(memory_space=pltpu.HBM)] * 2
        + [pl.BlockSpec(memory_space=pltpu.VMEM)],
        scratch_shapes=[
            pltpu.VMEM((2, 128, 128), jnp.float32),
            pltpu.VMEM((3, 3, 3, 128, 128), jnp.bfloat16),
            pltpu.VMEM((3, 3, 3, 128, 128), jnp.bfloat16),
            pltpu.VMEM((2, 2, 128, 256), jnp.bfloat16),
            pltpu.SemaphoreType.DMA,
            pltpu.SemaphoreType.DMA,
            pltpu.SemaphoreType.DMA((2, 2, 2)),
        ],
        compiler_params=pltpu.CompilerParams(vmem_limit_bytes=16 << 20),
        name="coarse_levels",
    )(south, middle, north, coarse, down, bricks)


def ring(values, axis, step):
    count = lax.axis_size(axis)
    return lax.ppermute(values, axis, [(i, (i + step) % count) for i in range(count)])


def per_device(
    records, slot_voxels, brick_mask, lift_weight, leaf_convs, down_leaf, down_coarse, coarse_convs
):
    messages = pack_messages(records[0], slot_voxels[0], brick_mask)
    arrived = lax.all_to_all(messages, ("gx", "gy"), split_axis=0, concat_axis=0, tiled=True)
    lift_block = jnp.kron(jnp.eye(8, dtype=jnp.bfloat16), lift_weight)
    taps = leaf_taps(leaf_convs)
    arrived, lift_block, taps = lax.optimization_barrier((arrived, lift_block, taps))
    coarse_convs = pltpu.with_memory_space_constraint(coarse_convs, pltpu.HBM)
    down_coarse = pltpu.with_memory_space_constraint(down_coarse, pltpu.HBM)
    arrived = pltpu.with_memory_space_constraint(arrived, pltpu.HBM)

    cells, low_x, high_x, low_y, high_y = scatter_and_lift(arrived, lift_block)
    west = ring(high_x, "gx", 1)
    east = ring(low_x, "gx", -1)
    south = ring(jnp.concatenate([west[:, 768:], high_y, east[:, 768:]], 0), "gy", 1)
    north = ring(jnp.concatenate([west[:, :256], low_y, east[:, :256]], 0), "gy", -1)
    halos = (west, east, south, north)
    features, down_two, bricks = leaf_levels(
        cells, halos, lift_block, taps, down_leaf, coarse_convs, down_coarse, arrived
    )
    middle = jnp.stack([ring(down_two, "gx", 1), down_two, ring(down_two, "gx", -1)])
    south, north = ring(middle, "gy", 1), ring(middle, "gy", -1)
    top = coarse_levels(south, middle, north, coarse_convs, down_coarse, bricks)
    return (features, top)


def solution(mesh):
    in_specs = (
        P(("gx", "gy"), None, None, None),
        P(("gx", "gy"), None, None),
        P("gx", "gy", None),
        P(),
        P(),
        P(),
        P(),
        P(),
    )
    out_specs = (P("gx", "gy", None, None), P("gx", "gy", None, None))
    return jax.shard_map(
        per_device, mesh=mesh, in_specs=in_specs, out_specs=out_specs, check_vma=False
    )
```

```python
import functools

import jax
import jax.numpy as jnp
from jax import lax
from jax.experimental import pallas as pl
from jax.experimental.pallas import tpu as pltpu
from jax.sharding import PartitionSpec as P

BRICK = 8
BUCKETS = 32


def pack_kernel(records_ref, slots_ref, bricks_ref, messages_ref, buffer_ref, in_sem, out_sem):
    buckets = slots_ref.shape[0]
    chunk = buckets // 8
    incoming, outgoing = [], []
    for part in range(8):
        here = slice(part * chunk, part * chunk + chunk)
        incoming.append(
            pltpu.make_async_copy(records_ref.at[here], buffer_ref.at[here, 0:64], in_sem.at[part])
        )
        outgoing.append(
            pltpu.make_async_copy(buffer_ref.at[here], messages_ref.at[here], out_sem.at[part])
        )
    for copy in incoming:
        copy.start()
    side = lax.rem(lax.axis_index("gy"), 2)
    slot = lax.broadcasted_iota(jnp.int32, (256, 128), 0)
    lane = lax.broadcasted_iota(jnp.int32, (256, 128), 1)
    picks = jnp.where((slot >> 2) + side * 64 == lane, 1.0, 0.0).astype(jnp.bfloat16)
    level = lax.broadcasted_iota(jnp.int32, (8, 128), 0) // 2
    place = lax.broadcasted_iota(jnp.int32, (8, 128), 1) - (1 - side) * 64
    bricks = jnp.zeros((8, 128), jnp.int32)
    for column in range(4):
        for z in range(4):
            here = (level == z) & (place >= column * 16) & (place < column * 16 + 16)
            bricks = jnp.where(here, bricks_ref[column // 2, column % 2, z], bricks)
    bricks = jnp.broadcast_to(bricks.astype(jnp.float32)[None], (chunk, 8, 128))
    shape = (chunk, 8, 256)
    row = lax.broadcasted_iota(jnp.int32, shape, 1)
    mine = (lax.broadcasted_iota(jnp.int32, shape, 2) & 3) == (row & 3)

    for part in range(8):
        here = slice(part * chunk, part * chunk + chunk)
        slots = slots_ref[here]
        high = (slots >> 9) * 16 + ((slots & 31) >> 1)
        low = ((slots >> 5) & 15) * 2 + (slots & 1)
        both = jnp.where(
            row < 4,
            jnp.broadcast_to(high.reshape(chunk, 1, 256), shape),
            jnp.broadcast_to(low.reshape(chunk, 1, 256), shape),
        )
        both = jnp.where(mine, both, 0).astype(jnp.float32)
        both = both.reshape(chunk * 8, 256).astype(jnp.bfloat16)
        ids = jnp.dot(both, picks, preferred_element_type=jnp.float32)
        buffer_ref[here, 64:72] = (ids.reshape(chunk, 8, 128) + bricks).astype(jnp.bfloat16)
        incoming[part].wait()
        outgoing[part].start()
    for copy in outgoing:
        copy.wait()


def pack_messages(records, slot_voxels, brick_mask):
    buckets, rows, width = records.shape
    return pl.pallas_call(
        pack_kernel,
        in_specs=[
            pl.BlockSpec(memory_space=pltpu.HBM),
            pl.BlockSpec(memory_space=pltpu.VMEM),
            pl.BlockSpec(memory_space=pltpu.SMEM),
        ],
        out_specs=pl.BlockSpec(memory_space=pltpu.HBM),
        out_shape=jax.ShapeDtypeStruct((buckets, rows + 8, width), jnp.bfloat16),
        scratch_shapes=[
            pltpu.VMEM((buckets, rows + 8, width), jnp.bfloat16),
            pltpu.SemaphoreType.DMA((8,)),
            pltpu.SemaphoreType.DMA((8,)),
        ],
        name="pack",
    )(records, slot_voxels, brick_mask)


def scatter_kernel(
    msg_ref, lift_ref, cells_ref, west_ref, east_ref, south_ref, north_ref, total_ref
):
    step = pl.program_id(0)

    @pl.when(step == 0)
    def _():
        total_ref[...] = jnp.zeros_like(total_ref)

    wide = 256
    lanes = lax.broadcasted_iota(jnp.int32, (wide, wide), 0).astype(jnp.bfloat16)
    zero = jnp.zeros((32, wide), jnp.bfloat16)
    left = lax.broadcasted_iota(jnp.int32, (8, 128), 1) < 64
    for quad in range(BUCKETS // 4):
        turned, ids = [], []
        for pair in range(2):
            first = quad * 4 + pair * 2
            rows = jnp.concatenate([msg_ref[first, 0:64], msg_ref[first + 1, 0:64]], 0)
            turned.append(jnp.transpose(rows))
            ids.append(
                jnp.where(
                    left,
                    msg_ref[first, 64:72].astype(jnp.float32),
                    msg_ref[first + 1, 64:72].astype(jnp.float32),
                )
            )
        turned = jnp.concatenate(turned, 1)
        ids = jnp.concatenate(ids, 1)
        for base in (0, 2):
            spreads, hots = [], []
            for quarter in (base, base + 1):
                features = turned[quarter * 32 : quarter * 32 + 32]
                high = jnp.broadcast_to(ids[quarter : quarter + 1], (wide, wide))
                low = jnp.broadcast_to(ids[quarter + 4 : quarter + 5], (32, wide))
                high, low = high.astype(jnp.bfloat16), low.astype(jnp.bfloat16)
                hots.append(jnp.where(lanes == high, 1.0, 0.0).astype(jnp.bfloat16))
                spreads += [
                    jnp.concatenate(
                        [jnp.where(low == jnp.bfloat16(i), features, zero) for i in range(32)], 0
                    )
                ]
            total_ref[...] += lax.dot_general(
                jnp.concatenate(spreads, 1),
                jnp.concatenate(hots, 1),
                (((1,), (1,)), ((), ())),
                preferred_element_type=jnp.float32,
            )

    @pl.when(step == pl.num_programs(0) - 1)
    def _():
        for part in range(4):
            summed = jnp.transpose(total_ref[part * wide : part * wide + wide])
            coarse = summed.astype(jnp.bfloat16)
            west_ref[:, part * wide : part * wide + wide] = coarse[:64]
            east_ref[:, part * wide : part * wide + wide] = coarse[192:]
            if part == 0:
                south_ref[...] = coarse
            if part == 3:
                north_ref[...] = coarse
            fine = (summed - coarse.astype(jnp.float32)).astype(jnp.bfloat16)
            lifted = jnp.dot(coarse, lift_ref[...], preferred_element_type=jnp.float32)
            lifted += jnp.dot(fine, lift_ref[...], preferred_element_type=jnp.float32)
            cells_ref[:, part * 512 : part * 512 + 512] = lifted.astype(jnp.bfloat16)


def scatter_and_lift(messages, lift_block):
    sources, rows, width = messages.shape
    shapes = [(256, 2048), (64, 1024), (64, 1024), (256, 256), (256, 256)]
    return pl.pallas_call(
        scatter_kernel,
        grid=(sources // BUCKETS,),
        in_specs=[
            pl.BlockSpec((BUCKETS, rows, width), lambda i: (i, 0, 0)),
            pl.BlockSpec((256, 512), lambda i: (0, 0)),
        ],
        out_specs=[pl.BlockSpec(shape, lambda i: (0, 0)) for shape in shapes],
        out_shape=[jax.ShapeDtypeStruct(shape, jnp.bfloat16) for shape in shapes],
        scratch_shapes=[pltpu.VMEM((1024, 256), jnp.float32)],
        compiler_params=pltpu.CompilerParams(vmem_limit_bytes=12 << 20),
        name="scatter",
    )(messages, lift_block)


def leaf_taps_kernel(convs_ref, taps_ref):
    zero = jnp.zeros((64, 64), jnp.bfloat16)
    for layer in range(2):
        for dx in range(3):
            for kind in range(2):
                for step_y in range(4):
                    for half in range(2):
                        row = kind * 512 + step_y * 128 + half * 64
                        for out_y in range(2):
                            blocks = []
                            for out_z in range(2):
                                dy = step_y - out_y
                                if kind == 0:
                                    dz = half - out_z + 1
                                else:
                                    dz = 3 - out_z if half == 0 else -out_z
                                inside = 0 <= dy <= 2 and 0 <= dz <= 2
                                blocks.append(convs_ref[layer, dx, dy, dz] if inside else zero)
                            taps_ref[layer, dx, row : row + 64, out_y * 128 : out_y * 128 + 128] = (
                                jnp.concatenate(blocks, 1)
                            )


def leaf_taps(leaf_convs):
    return pl.pallas_call(
        leaf_taps_kernel,
        out_shape=jax.ShapeDtypeStruct((2, 3, 1024, 256), jnp.bfloat16),
        name="leaf_taps",
    )(leaf_convs)


def row_shifts(values, period):
    count = values.shape[0]
    place = lax.rem(lax.broadcasted_iota(jnp.int32, values.shape, 0), period)
    before = jnp.where(place == 0, 0.0, pltpu.roll(values, 1, 0))
    after = jnp.where(place == period - 1, 0.0, pltpu.roll(values, count - 1, 0))
    return before, after


def z_neighbours(values):
    before, after = row_shifts(values, 16)
    lane = lax.rem(lax.broadcasted_iota(jnp.int32, values.shape, 1), 128)
    return jnp.where(lane < 64, after, before).astype(jnp.bfloat16)


def spread_bricks(near, flags):
    side = lax.rem(lax.axis_index("gy"), 2)
    columns = []
    for y in range(4):
        for x in range(4):
            source_x, source_y = (0, 1, 1, 2)[x], (0, 1, 1, 2)[y]
            lane = ((1, 0, 1, 0)[x] * 2 + (1, 0, 1, 0)[y]) * 16
            tile = near[source_x * 3 + source_y].astype(jnp.float32)
            upper = side == 0 if source_y == 1 else side == 1
            value = jnp.where(upper, tile[:, 64 + lane : 65 + lane], tile[:, lane : lane + 1])
            flag = flags[0][source_x] * flags[1][source_y]
            columns.append(jnp.broadcast_to(value, (8, 128)) * flag)
    return columns


def doubled(column):
    level = lax.broadcasted_iota(jnp.int32, (16, 128), 0) // 4
    tile = jnp.broadcast_to(column[0:1], (16, 128))
    for z in range(1, 4):
        tile = jnp.where(level == z, jnp.broadcast_to(column[2 * z : 2 * z + 1], (16, 128)), tile)
    return tile


def grid_flags():
    here_x, here_y = lax.axis_index("gx"), lax.axis_index("gy")
    last_x, last_y = lax.axis_size("gx") - 1, lax.axis_size("gy") - 1
    return (
        (jnp.where(here_x > 0, 1.0, 0.0), 1.0, jnp.where(here_x < last_x, 1.0, 0.0)),
        (jnp.where(here_y > 0, 1.0, 0.0), 1.0, jnp.where(here_y < last_y, 1.0, 0.0)),
    )


def fill_leaf_mask(columns, leaf_mask_ref):
    for y in range(4):
        for x in range(4):
            tile = doubled(columns[y * 4 + x])
            for place_x in range(*((0, 4), (4, 12), (12, 20), (20, 24))[x]):
                leaf_mask_ref[y, place_x * 16 : place_x * 16 + 16] = tile


def leaf_sweep(sources, taps, rows):
    windows = []
    for source_ref, source_z_ref, lane in sources:
        pieces = []
        for dx in range(3):
            pieces.append(source_ref[dx * 16 : dx * 16 + rows, pl.ds(lane, 512)])
            pieces.append(source_z_ref[dx * 16 : dx * 16 + rows, pl.ds(lane, 512)])
        windows.append(jnp.concatenate(pieces, 1))
    total = jnp.dot(jnp.concatenate(windows, 0), taps, preferred_element_type=jnp.float32)
    total = jnp.maximum(total, 0.0)
    return [total[i * rows : i * rows + rows] for i in range(len(sources))]


def middle_kernel(
    cells_ref,
    west_ref,
    east_ref,
    lift_ref,
    taps_ref,
    arrived_ref,
    one_ref,
    one_z_ref,
    low_ref,
    high_ref,
    bricks_ref,
    cell_ref,
    cell_z_ref,
    leaf_mask_ref,
    near_vmem,
    near_sem,
):
    last_x, last_y = lax.axis_size("gx") - 1, lax.axis_size("gy") - 1
    copies = []
    for x in range(3):
        for y in range(3):
            source = jnp.clip(lax.axis_index("gx") + x - 1, 0, last_x) * (last_y + 1)
            source = source + jnp.clip(lax.axis_index("gy") + y - 1, 0, last_y)
            copies.append(
                pltpu.make_async_copy(
                    arrived_ref.at[source, 64:72], near_vmem.at[x * 3 + y], near_sem.at[x, y]
                )
            )
    for copy in copies:
        copy.start()
    flags = grid_flags()
    cell_ref[64:320] = cells_ref[...]
    for part in range(4):
        for row, ref, flag in ((0, west_ref, flags[0][0]), (320, east_ref, flags[0][2])):
            sums = ref[:, part * 256 : part * 256 + 256]
            lifted = jnp.dot(sums, lift_ref[...], preferred_element_type=jnp.float32) * flag
            cell_ref[row : row + 64, part * 512 : part * 512 + 512] = lifted.astype(jnp.bfloat16)
    low_ref[...] = cell_ref[:, :256]
    high_ref[...] = cell_ref[:, 1792:]

    @pl.loop(0, 8)
    def _(step):
        lanes = pl.ds(pl.multiple_of(step * 256, 256), 256)
        cell_z_ref[:, lanes] = z_neighbours(cell_ref[:, lanes].astype(jnp.float32))

    for copy in copies:
        copy.wait()
    columns = spread_bricks([near_vmem[i] for i in range(9)], flags)
    for index, column in enumerate(columns):
        bricks_ref[index] = column
    fill_leaf_mask(columns, leaf_mask_ref)
    taps = taps_ref[0].reshape(3072, 256)
    for first, count in ((0, 4), (4, 3)):
        sources = [(cell_ref, cell_z_ref, (first + i) * 256) for i in range(count)]
        for window, total in enumerate(leaf_sweep(sources, taps, 352)):
            step = first + window
            masks = [leaf_mask_ref[(2 * step + half + 9) // 8, 16:368] for half in range(2)]
            values = (total * jnp.concatenate(masks, 1)).astype(jnp.bfloat16)
            one_ref[:, step * 256 : step * 256 + 256] = values
            one_z_ref[:, step * 256 : step * 256 + 256] = z_neighbours(values.astype(jnp.float32))


def middle_part(cells, west, east, lift_block, taps, arrived):
    return pl.pallas_call(
        middle_kernel,
        out_shape=[
            jax.ShapeDtypeStruct((352, 1792), jnp.bfloat16),
            jax.ShapeDtypeStruct((352, 1792), jnp.bfloat16),
            jax.ShapeDtypeStruct((384, 256), jnp.bfloat16),
            jax.ShapeDtypeStruct((384, 256), jnp.bfloat16),
            jax.ShapeDtypeStruct((16, 8, 128), jnp.float32),
        ],
        in_specs=[pl.BlockSpec(memory_space=pltpu.VMEM)] * 5
        + [pl.BlockSpec(memory_space=pltpu.HBM)],
        scratch_shapes=[
            pltpu.VMEM((384, 2048), jnp.bfloat16),
            pltpu.VMEM((384, 2048), jnp.bfloat16),
            pltpu.VMEM((4, 384, 128), jnp.float32),
            pltpu.VMEM((9, 8, 128), jnp.bfloat16),
            pltpu.SemaphoreType.DMA((3, 3)),
        ],
        compiler_params=pltpu.CompilerParams(vmem_limit_bytes=24 << 20),
        name="leaf_middle",
    )(cells, west, east, lift_block, taps, arrived)


def border_kernel(
    low_ref,
    high_ref,
    south_ref,
    north_ref,
    lift_ref,
    taps_ref,
    bricks_ref,
    one_middle_ref,
    one_z_middle_ref,
    down_leaf_ref,
    coarse_ref,
    down_ref,
    features_ref,
    down_two_ref,
    edge_ref,
    edge_z_ref,
    one_ref,
    one_z_ref,
    down_one_ref,
    parts_ref,
    down_leaf_vmem,
    coarse_vmem,
    down_vmem,
    leaf_mask_ref,
    one_sem,
    leaf_sem,
    coarse_sem,
    down_sem,
):
    early = [
        pltpu.make_async_copy(one_middle_ref, one_ref.at[:, 512:2304], one_sem.at[0]),
        pltpu.make_async_copy(one_z_middle_ref, one_z_ref.at[:, 512:2304], one_sem.at[1]),
        pltpu.make_async_copy(down_leaf_ref, down_leaf_vmem, leaf_sem),
    ]
    copies = []
    for dx in range(3):
        for dz in range(3):
            copies.append(
                pltpu.make_async_copy(
                    coarse_ref.at[0, dx, :, dz], coarse_vmem.at[dx, dz], coarse_sem.at[dx, dz]
                )
            )
    for a in range(2):
        for b in range(2):
            for c in range(2):
                copies.append(
                    pltpu.make_async_copy(
                        down_ref.at[0, a, b, c],
                        down_vmem.at[a, b, :, c * 128 : c * 128 + 128],
                        down_sem.at[a, b, c],
                    )
                )
    for copy in early + copies:
        copy.start()
    flags = grid_flags()
    edge_ref[0, :, 512:768] = low_ref[...]
    edge_ref[1, :, 0:256] = high_ref[...]
    for edge, lane, ref, flag in ((0, 0, south_ref, flags[1][0]), (1, 256, north_ref, flags[1][2])):
        for row, rows, other in ((0, 64, flags[0][0]), (64, 256, 1.0), (320, 64, flags[0][2])):
            sums = ref[row : row + rows]
            lifted = jnp.dot(sums, lift_ref[...], preferred_element_type=jnp.float32)
            lifted = (lifted * (flag * other)).astype(jnp.bfloat16)
            edge_ref[edge, row : row + rows, lane : lane + 512] = lifted
    fill_leaf_mask([bricks_ref[i] for i in range(16)], leaf_mask_ref)
    for edge in range(2):
        for part in range(3):
            lanes = slice(part * 256, part * 256 + 256)
            edge_z_ref[edge, :, lanes] = z_neighbours(edge_ref[edge, :, lanes].astype(jnp.float32))
    sources, steps = [], []
    for edge in range(2):
        for window in range(2):
            sources.append((edge_ref.at[edge], edge_z_ref.at[edge], window * 256))
            steps.append(edge * 9 + window)
    taps = taps_ref[0].reshape(3072, 256)
    for step, total in zip(steps, leaf_sweep(sources, taps, 352)):
        masks = [leaf_mask_ref[(2 * step + half + 5) // 8, 16:368] for half in range(2)]
        values = (total * jnp.concatenate(masks, 1)).astype(jnp.bfloat16)
        one_ref[:, step * 256 : step * 256 + 256] = values
        one_z_ref[:, step * 256 : step * 256 + 256] = z_neighbours(values.astype(jnp.float32))
    for copy in early:
        copy.wait()

    @pl.loop(0, 2)
    def _(half_step):
        first = half_step * 5
        lanes = [pl.multiple_of((first + i) * 256, 256) for i in range(5)]
        taps = taps_ref[1].reshape(3072, 256)
        totals = leaf_sweep([(one_ref, one_z_ref, lane) for lane in lanes], taps, 320)
        merges, masks = [], []
        for window, total in enumerate(totals):
            step = first + window
            mask = leaf_mask_ref[(2 * step + 6) // 8, 32:352]
            values = (total * jnp.concatenate([mask, mask], 1)).astype(jnp.bfloat16)

            @pl.when((step >= 1) & (step < 9))
            def _():
                for half in range(2):
                    inner = values[32:288, half * 128 : half * 128 + 128]
                    features_ref[:, 2 * step - 2 + half] = inner.reshape(16, 16, 128)

            pairs = values.reshape(10, 2, 16, 256)
            halves = [pairs[:, a].reshape(160, 256) for a in range(2)]
            merges.append(jnp.concatenate(halves, 1))
            masks.append(mask.reshape(10, 2, 16, 128)[:, 0].reshape(160, 128))
        taps = down_leaf_vmem[...].reshape(512, 128)
        total = jnp.dot(jnp.concatenate(merges, 0), taps, preferred_element_type=jnp.float32)
        total = jnp.maximum(total, 0.0) * jnp.concatenate(masks, 0)
        for window in range(5):
            down = total[window * 160 : window * 160 + 160].astype(jnp.bfloat16)
            before, after = row_shifts(down.astype(jnp.float32), 16)
            here = pl.ds(pl.multiple_of((first + window) * 128, 128), 128)
            down_one_ref[0, :, here] = before.astype(jnp.bfloat16)
            down_one_ref[1, :, here] = down
            down_one_ref[2, :, here] = after.astype(jnp.bfloat16)

    for copy in copies:
        copy.wait()
    windows = []
    for y in range(8):
        windows.append(
            jnp.concatenate(
                [
                    down_one_ref[dz, dx * 16 : dx * 16 + 128, y * 128 : y * 128 + 384]
                    for dx in range(3)
                    for dz in range(3)
                ],
                1,
            )
        )
    taps = coarse_vmem[...].reshape(3456, 128)
    total = jnp.dot(jnp.concatenate(windows, 0), taps, preferred_element_type=jnp.float32)
    total = jnp.maximum(total, 0.0).reshape(8, 128, 128)
    masks = [leaf_mask_ref[1 + y // 4, 64:320].reshape(8, 2, 16, 128)[:, 0] for y in range(8)]
    level = total * jnp.concatenate(masks, 0).reshape(8, 128, 128)
    level = level.astype(jnp.bfloat16).reshape(4, 2, 4, 2, 16, 128)
    merged = jnp.concatenate(
        [level[:, b, :, a].reshape(256, 128) for a in range(2) for b in range(2)], 1
    )
    taps = down_vmem[...].reshape(512, 256)
    parts = jnp.dot(merged, taps, preferred_element_type=jnp.float32)
    parts_ref[0] = parts[:, :128]
    parts_ref[1] = parts[:, 128:]
    total = parts_ref[0, pl.ds(0, 128, stride=2)] + parts_ref[1, pl.ds(1, 128, stride=2)]
    tiles = [bricks_ref[(1 + y // 2) * 4 + 1 + x // 2] for y in range(4) for x in range(4)]
    mask = jnp.concatenate(tiles, 0)
    down_two_ref[...] = (jnp.maximum(total, 0.0) * mask).astype(jnp.bfloat16)


def border_part(low, high, south, north, lift_block, taps, bricks, one, one_z, down_leaf, coarse, down):
    return pl.pallas_call(
        border_kernel,
        out_shape=[
            jax.ShapeDtypeStruct((16, 16, 16, 128), jnp.bfloat16),
            jax.ShapeDtypeStruct((128, 128), jnp.bfloat16),
        ],
        in_specs=[pl.BlockSpec(memory_space=pltpu.VMEM)] * 7
        + [pl.BlockSpec(memory_space=pl.ANY)] * 3
        + [pl.BlockSpec(memory_space=pltpu.HBM)] * 2,
        scratch_shapes=[
            pltpu.VMEM((2, 384, 768), jnp.bfloat16),
            pltpu.VMEM((2, 384, 768), jnp.bfloat16),
            pltpu.VMEM((352, 2816), jnp.bfloat16),
            pltpu.VMEM((352, 2816), jnp.bfloat16),
            pltpu.VMEM((3, 160, 1280), jnp.bfloat16),
            pltpu.VMEM((2, 256, 128), jnp.float32),
            pltpu.VMEM((2, 2, 2, 64, 128), jnp.bfloat16),
            pltpu.VMEM((3, 3, 3, 128, 128), jnp.bfloat16),
            pltpu.VMEM((2, 2, 128, 256), jnp.bfloat16),
            pltpu.VMEM((4, 384, 128), jnp.float32),
            pltpu.SemaphoreType.DMA((2,)),
            pltpu.SemaphoreType.DMA,
            pltpu.SemaphoreType.DMA((3, 3)),
            pltpu.SemaphoreType.DMA((2, 2, 2)),
        ],
        compiler_params=pltpu.CompilerParams(vmem_limit_bytes=32 << 20),
        name="leaf_border",
    )(low, high, south, north, lift_block, taps, bricks, one, one_z, down_leaf, coarse, down)


def coarse_kernel(
    south_ref,
    middle_ref,
    north_ref,
    coarse_ref,
    down_ref,
    bricks_ref,
    top_ref,
    parts_ref,
    coarse_vmem,
    last_vmem,
    down_vmem,
    coarse_sem,
    last_sem,
    down_sem,
):
    copies = [
        pltpu.make_async_copy(coarse_ref.at[1], coarse_vmem, coarse_sem),
        pltpu.make_async_copy(coarse_ref.at[2], last_vmem, last_sem),
    ]
    for a in range(2):
        for b in range(2):
            for c in range(2):
                copies.append(
                    pltpu.make_async_copy(
                        down_ref.at[1, a, b, c],
                        down_vmem.at[a, b, :, c * 128 : c * 128 + 128],
                        down_sem.at[a, b, c],
                    )
                )
    for copy in copies:
        copy.start()
    here_x = lax.axis_index("gx")
    here_y = lax.axis_index("gy")
    from_west = jnp.where(here_x > 0, 1.0, 0.0)
    from_east = jnp.where(here_x < lax.axis_size("gx") - 1, 1.0, 0.0)
    from_south = jnp.where(here_y > 0, 1.0, 0.0)
    from_north = jnp.where(here_y < lax.axis_size("gy") - 1, 1.0, 0.0)

    strips = []
    for ref, first, flag in ((south_ref, 1, from_south), (middle_ref, 0, 1.0), (north_ref, 0, from_north)):
        count = 4 if ref is middle_ref else 3
        tiles = [ref[i].astype(jnp.float32).reshape(4, 4, 8, 128) for i in range(3)]
        tiles = [tile[first : first + count] for tile in tiles]
        tiles = [
            tiles[0][:, 1:] * (flag * from_west),
            tiles[1] * flag,
            tiles[2][:, :3] * (flag * from_east),
        ]
        strips.append(jnp.concatenate(tiles, 1))
    grid = jnp.concatenate(strips, 0)
    before, after = row_shifts(grid.reshape(800, 128), 8)
    grids = [before.reshape(10, 10, 8, 128), grid, after.reshape(10, 10, 8, 128)]
    pieces = [
        grids[dz][dy : dy + 8, dx : dx + 8].reshape(512, 128).astype(jnp.bfloat16)
        for dx in range(3)
        for dy in range(3)
        for dz in range(3)
    ]
    for copy in copies:
        copy.wait()
    taps = coarse_vmem[...].reshape(3456, 128)
    total = jnp.dot(jnp.concatenate(pieces, 1), taps, preferred_element_type=jnp.float32)
    tiles = [bricks_ref[y // 2 * 4 + x // 2] for y in range(8) for x in range(8)]
    mask = jnp.concatenate(tiles, 0)
    level = jnp.maximum(total, 0.0) * mask
    level = level.reshape(4, 2, 4, 2, 8, 128)
    merged = jnp.concatenate(
        [level[:, b, :, a].reshape(128, 128) for a in range(2) for b in range(2)], 1
    ).astype(jnp.bfloat16)
    taps = down_vmem[...].reshape(512, 256)
    parts = jnp.dot(merged, taps, preferred_element_type=jnp.float32)
    parts_ref[0] = parts[:, :128]
    parts_ref[1] = parts[:, 128:]
    total = parts_ref[0, pl.ds(0, 64, stride=2)] + parts_ref[1, pl.ds(1, 64, stride=2)]
    picks = lax.broadcasted_iota(jnp.int32, (64, 128), 0) * 2
    picks = picks == lax.broadcasted_iota(jnp.int32, (64, 128), 1)
    picks = jnp.where(picks, 1.0, 0.0).astype(jnp.bfloat16)
    bricks = bricks_ref[...].reshape(128, 128).astype(jnp.bfloat16)
    mask = jnp.dot(picks, bricks, preferred_element_type=jnp.float32)
    down = jnp.maximum(total, 0.0) * mask
    down = down.astype(jnp.bfloat16).astype(jnp.float32)
    before, after = row_shifts(down, 4)
    shifted = [before, down, after]
    pieces = []
    for dx in range(3):
        for dy in range(3):
            for dz in range(3):
                turn = (64 - (dy - 1) * 16 - (dx - 1) * 4) % 64
                moved = pltpu.roll(shifted[dz], turn, 0) if turn else shifted[dz]
                pieces.append(moved.astype(jnp.bfloat16))
    taps = last_vmem[...].reshape(3456, 128)
    total = jnp.dot(jnp.concatenate(pieces, 1), taps, preferred_element_type=jnp.float32)
    top = (jnp.maximum(total, 0.0) * mask).astype(jnp.bfloat16)
    for x in range(2):
        for y in range(2):
            row = (y + 1) * 16 + (x + 1) * 4
            top_ref[x, y] = top[row : row + 4]


def coarse_levels(south, middle, north, coarse, down, bricks):
    return pl.pallas_call(
        coarse_kernel,
        out_shape=jax.ShapeDtypeStruct((2, 2, 4, 128), jnp.bfloat16),
        in_specs=[pl.BlockSpec(memory_space=pltpu.VMEM)] * 3
        + [pl.BlockSpec(memory_space=pltpu.HBM)] * 2
        + [pl.BlockSpec(memory_space=pltpu.VMEM)],
        scratch_shapes=[
            pltpu.VMEM((2, 128, 128), jnp.float32),
            pltpu.VMEM((3, 3, 3, 128, 128), jnp.bfloat16),
            pltpu.VMEM((3, 3, 3, 128, 128), jnp.bfloat16),
            pltpu.VMEM((2, 2, 128, 256), jnp.bfloat16),
            pltpu.SemaphoreType.DMA,
            pltpu.SemaphoreType.DMA,
            pltpu.SemaphoreType.DMA((2, 2, 2)),
        ],
        compiler_params=pltpu.CompilerParams(vmem_limit_bytes=16 << 20),
        name="coarse_levels",
    )(south, middle, north, coarse, down, bricks)


def ring(values, axis, step):
    count = lax.axis_size(axis)
    return lax.ppermute(values, axis, [(i, (i + step) % count) for i in range(count)])


def per_device(
    records, slot_voxels, brick_mask, lift_weight, leaf_convs, down_leaf, down_coarse, coarse_convs
):
    messages = pack_messages(records[0], slot_voxels[0], brick_mask)
    arrived = lax.all_to_all(messages, ("gx", "gy"), split_axis=0, concat_axis=0, tiled=True)
    lift_block = jnp.kron(jnp.eye(8, dtype=jnp.bfloat16), lift_weight)
    taps = leaf_taps(leaf_convs)
    arrived, lift_block, taps = lax.optimization_barrier((arrived, lift_block, taps))
    coarse_convs = pltpu.with_memory_space_constraint(coarse_convs, pltpu.HBM)
    down_coarse = pltpu.with_memory_space_constraint(down_coarse, pltpu.HBM)
    arrived = pltpu.with_memory_space_constraint(arrived, pltpu.HBM)

    cells, low_x, high_x, low_y, high_y = scatter_and_lift(arrived, lift_block)
    west = ring(high_x, "gx", 1)
    east = ring(low_x, "gx", -1)
    south = ring(jnp.concatenate([west[:, 768:], high_y, east[:, 768:]], 0), "gy", 1)
    north = ring(jnp.concatenate([west[:, :256], low_y, east[:, :256]], 0), "gy", -1)
    one, one_z, low, high, bricks = middle_part(cells, west, east, lift_block, taps, arrived)
    features, down_two = border_part(
        low,
        high,
        south,
        north,
        lift_block,
        taps,
        bricks,
        one,
        one_z,
        down_leaf,
        coarse_convs,
        down_coarse,
    )
    middle = jnp.stack([ring(down_two, "gx", 1), down_two, ring(down_two, "gx", -1)])
    south, north = ring(middle, "gy", 1), ring(middle, "gy", -1)
    top = coarse_levels(south, middle, north, coarse_convs, down_coarse, bricks)
    return (features, top)


def solution(mesh):
    in_specs = (
        P(("gx", "gy"), None, None, None),
        P(("gx", "gy"), None, None),
        P("gx", "gy", None),
        P(),
        P(),
        P(),
        P(),
        P(),
    )
    out_specs = (P("gx", "gy", None, None), P("gx", "gy", None, None))
    return jax.shard_map(
        per_device, mesh=mesh, in_specs=in_specs, out_specs=out_specs, check_vma=False
    )
```

```python
import functools

import jax
import jax.numpy as jnp
from jax import lax
from jax.experimental import pallas as pl
from jax.experimental.pallas import tpu as pltpu
from jax.sharding import PartitionSpec as P

BRICK = 8
BUCKETS = 64


def pack_kernel(records_ref, slots_ref, bricks_ref, messages_ref, buffer_ref, in_sem, out_sem):
    buckets = slots_ref.shape[0]
    chunk = buckets // 8
    incoming, outgoing = [], []
    for part in range(8):
        here = slice(part * chunk, part * chunk + chunk)
        incoming.append(
            pltpu.make_async_copy(records_ref.at[here], buffer_ref.at[here, 0:64], in_sem.at[part])
        )
        outgoing.append(
            pltpu.make_async_copy(buffer_ref.at[here], messages_ref.at[here], out_sem.at[part])
        )
    for copy in incoming:
        copy.start()
    side = lax.rem(lax.axis_index("gy"), 2)
    slot = lax.broadcasted_iota(jnp.int32, (256, 128), 0)
    lane = lax.broadcasted_iota(jnp.int32, (256, 128), 1)
    picks = jnp.where((slot >> 2) + side * 64 == lane, 1.0, 0.0).astype(jnp.bfloat16)
    level = lax.broadcasted_iota(jnp.int32, (8, 128), 0) // 2
    place = lax.broadcasted_iota(jnp.int32, (8, 128), 1) - (1 - side) * 64
    bricks = jnp.zeros((8, 128), jnp.int32)
    for column in range(4):
        for z in range(4):
            here = (level == z) & (place >= column * 16) & (place < column * 16 + 16)
            bricks = jnp.where(here, bricks_ref[column // 2, column % 2, z], bricks)
    bricks = jnp.broadcast_to(bricks.astype(jnp.float32)[None], (chunk, 8, 128))
    shape = (chunk, 8, 256)
    row = lax.broadcasted_iota(jnp.int32, shape, 1)
    mine = (lax.broadcasted_iota(jnp.int32, shape, 2) & 3) == (row & 3)

    for part in range(8):
        here = slice(part * chunk, part * chunk + chunk)
        slots = slots_ref[here]
        high = (slots >> 9) * 16 + ((slots & 31) >> 1)
        low = ((slots >> 5) & 15) * 2 + (slots & 1)
        both = jnp.where(
            row < 4,
            jnp.broadcast_to(high.reshape(chunk, 1, 256), shape),
            jnp.broadcast_to(low.reshape(chunk, 1, 256), shape),
        )
        both = jnp.where(mine, both, 0).astype(jnp.float32)
        both = both.reshape(chunk * 8, 256).astype(jnp.bfloat16)
        ids = jnp.dot(both, picks, preferred_element_type=jnp.float32)
        buffer_ref[here, 64:72] = (ids.reshape(chunk, 8, 128) + bricks).astype(jnp.bfloat16)
        incoming[part].wait()
        outgoing[part].start()
    for copy in outgoing:
        copy.wait()


def pack_messages(records, slot_voxels, brick_mask):
    buckets, rows, width = records.shape
    return pl.pallas_call(
        pack_kernel,
        in_specs=[
            pl.BlockSpec(memory_space=pltpu.HBM),
            pl.BlockSpec(memory_space=pltpu.VMEM),
            pl.BlockSpec(memory_space=pltpu.SMEM),
        ],
        out_specs=pl.BlockSpec(memory_space=pltpu.HBM),
        out_shape=jax.ShapeDtypeStruct((buckets, rows + 8, width), jnp.bfloat16),
        scratch_shapes=[
            pltpu.VMEM((buckets, rows + 8, width), jnp.bfloat16),
            pltpu.SemaphoreType.DMA((8,)),
            pltpu.SemaphoreType.DMA((8,)),
        ],
        name="pack",
    )(records, slot_voxels, brick_mask)


def scatter_kernel(
    msg_ref, lift_ref, cells_ref, west_ref, east_ref, south_ref, north_ref, total_ref
):
    step = pl.program_id(0)

    @pl.when(step == 0)
    def _():
        total_ref[...] = jnp.zeros_like(total_ref)

    wide = 256
    lanes = lax.broadcasted_iota(jnp.int32, (wide, wide), 0).astype(jnp.bfloat16)
    zero = jnp.zeros((32, wide), jnp.bfloat16)
    left = lax.broadcasted_iota(jnp.int32, (8, 128), 1) < 64
    for quad in range(BUCKETS // 4):
        turned, ids = [], []
        for pair in range(2):
            first = quad * 4 + pair * 2
            rows = jnp.concatenate([msg_ref[first, 0:64], msg_ref[first + 1, 0:64]], 0)
            turned.append(jnp.transpose(rows))
            ids.append(
                jnp.where(
                    left,
                    msg_ref[first, 64:72].astype(jnp.float32),
                    msg_ref[first + 1, 64:72].astype(jnp.float32),
                )
            )
        turned = jnp.concatenate(turned, 1)
        ids = jnp.concatenate(ids, 1)
        for base in (0, 2):
            spreads, hots = [], []
            for quarter in (base, base + 1):
                features = turned[quarter * 32 : quarter * 32 + 32]
                high = jnp.broadcast_to(ids[quarter : quarter + 1], (wide, wide))
                low = jnp.broadcast_to(ids[quarter + 4 : quarter + 5], (32, wide))
                high, low = high.astype(jnp.bfloat16), low.astype(jnp.bfloat16)
                hots.append(jnp.where(lanes == high, 1.0, 0.0).astype(jnp.bfloat16))
                spreads += [
                    jnp.concatenate(
                        [jnp.where(low == jnp.bfloat16(i), features, zero) for i in range(32)], 0
                    )
                ]
            total_ref[...] += lax.dot_general(
                jnp.concatenate(spreads, 1),
                jnp.concatenate(hots, 1),
                (((1,), (1,)), ((), ())),
                preferred_element_type=jnp.float32,
            )

    @pl.when(step == pl.num_programs(0) - 1)
    def _():
        for part in range(4):
            summed = jnp.transpose(total_ref[part * wide : part * wide + wide])
            coarse = summed.astype(jnp.bfloat16)
            west_ref[:, part * wide : part * wide + wide] = coarse[:64]
            east_ref[:, part * wide : part * wide + wide] = coarse[192:]
            if part == 0:
                south_ref[...] = coarse
            if part == 3:
                north_ref[...] = coarse
            fine = (summed - coarse.astype(jnp.float32)).astype(jnp.bfloat16)
            lifted = jnp.dot(coarse, lift_ref[...], preferred_element_type=jnp.float32)
            lifted += jnp.dot(fine, lift_ref[...], preferred_element_type=jnp.float32)
            cells_ref[:, part * 512 : part * 512 + 512] = lifted.astype(jnp.bfloat16)


def scatter_and_lift(messages, lift_block):
    sources, rows, width = messages.shape
    shapes = [(256, 2048), (64, 1024), (64, 1024), (256, 256), (256, 256)]
    return pl.pallas_call(
        scatter_kernel,
        grid=(sources // BUCKETS,),
        in_specs=[
            pl.BlockSpec((BUCKETS, rows, width), lambda i: (i, 0, 0)),
            pl.BlockSpec((256, 512), lambda i: (0, 0)),
        ],
        out_specs=[pl.BlockSpec(memory_space=pltpu.VMEM)] * 5,
        out_shape=[jax.ShapeDtypeStruct(shape, jnp.bfloat16) for shape in shapes],
        scratch_shapes=[pltpu.VMEM((1024, 256), jnp.float32)],
        compiler_params=pltpu.CompilerParams(vmem_limit_bytes=14 << 20),
        name="scatter",
    )(messages, lift_block)


def leaf_taps_kernel(convs_ref, taps_ref):
    zero = jnp.zeros((64, 64), jnp.bfloat16)
    for layer in range(2):
        for dx in range(3):
            for kind in range(2):
                for step_y in range(4):
                    for half in range(2):
                        row = kind * 512 + step_y * 128 + half * 64
                        for out_y in range(2):
                            blocks = []
                            for out_z in range(2):
                                dy = step_y - out_y
                                if kind == 0:
                                    dz = half - out_z + 1
                                else:
                                    dz = 3 - out_z if half == 0 else -out_z
                                inside = 0 <= dy <= 2 and 0 <= dz <= 2
                                blocks.append(convs_ref[layer, dx, dy, dz] if inside else zero)
                            taps_ref[layer, dx, row : row + 64, out_y * 128 : out_y * 128 + 128] = (
                                jnp.concatenate(blocks, 1)
                            )


def leaf_taps(leaf_convs):
    return pl.pallas_call(
        leaf_taps_kernel,
        out_shape=jax.ShapeDtypeStruct((2, 3, 1024, 256), jnp.bfloat16),
        name="leaf_taps",
    )(leaf_convs)


def row_shifts(values, period):
    count = values.shape[0]
    place = lax.rem(lax.broadcasted_iota(jnp.int32, values.shape, 0), period)
    before = jnp.where(place == 0, 0.0, pltpu.roll(values, 1, 0))
    after = jnp.where(place == period - 1, 0.0, pltpu.roll(values, count - 1, 0))
    return before, after


def z_neighbours(values):
    before, after = row_shifts(values, 16)
    lane = lax.rem(lax.broadcasted_iota(jnp.int32, values.shape, 1), 128)
    return jnp.where(lane < 64, after, before).astype(jnp.bfloat16)


def spread_bricks(near, flags):
    side = lax.rem(lax.axis_index("gy"), 2)
    columns = []
    for y in range(4):
        for x in range(4):
            source_x, source_y = (0, 1, 1, 2)[x], (0, 1, 1, 2)[y]
            lane = ((1, 0, 1, 0)[x] * 2 + (1, 0, 1, 0)[y]) * 16
            tile = near[source_x * 3 + source_y].astype(jnp.float32)
            upper = side == 0 if source_y == 1 else side == 1
            value = jnp.where(upper, tile[:, 64 + lane : 65 + lane], tile[:, lane : lane + 1])
            flag = flags[0][source_x] * flags[1][source_y]
            columns.append(jnp.broadcast_to(value, (8, 128)) * flag)
    return columns


def doubled(column):
    level = lax.broadcasted_iota(jnp.int32, (16, 128), 0) // 4
    tile = jnp.broadcast_to(column[0:1], (16, 128))
    for z in range(1, 4):
        tile = jnp.where(level == z, jnp.broadcast_to(column[2 * z : 2 * z + 1], (16, 128)), tile)
    return tile


def grid_flags():
    here_x, here_y = lax.axis_index("gx"), lax.axis_index("gy")
    last_x, last_y = lax.axis_size("gx") - 1, lax.axis_size("gy") - 1
    return (
        (jnp.where(here_x > 0, 1.0, 0.0), 1.0, jnp.where(here_x < last_x, 1.0, 0.0)),
        (jnp.where(here_y > 0, 1.0, 0.0), 1.0, jnp.where(here_y < last_y, 1.0, 0.0)),
    )


def fill_leaf_mask(columns, leaf_mask_ref):
    for y in range(4):
        for x in range(4):
            tile = doubled(columns[y * 4 + x])
            for place_x in range(*((0, 4), (4, 12), (12, 20), (20, 24))[x]):
                leaf_mask_ref[y, place_x * 16 : place_x * 16 + 16] = tile


def leaf_sweep(sources, taps, rows):
    windows = []
    for source_ref, source_z_ref, lane in sources:
        pieces = []
        for dx in range(3):
            pieces.append(source_ref[dx * 16 : dx * 16 + rows, pl.ds(lane, 512)])
            pieces.append(source_z_ref[dx * 16 : dx * 16 + rows, pl.ds(lane, 512)])
        windows.append(jnp.concatenate(pieces, 1))
    total = jnp.dot(jnp.concatenate(windows, 0), taps, preferred_element_type=jnp.float32)
    total = jnp.maximum(total, 0.0)
    return [total[i * rows : i * rows + rows] for i in range(len(sources))]


def own_kernel(cells_ref, arrived_ref, cell_z_ref, bricks_ref, near_vmem, near_sem):
    last_x, last_y = lax.axis_size("gx") - 1, lax.axis_size("gy") - 1
    copies = []
    for x in range(3):
        for y in range(3):
            source = jnp.clip(lax.axis_index("gx") + x - 1, 0, last_x) * (last_y + 1)
            source = source + jnp.clip(lax.axis_index("gy") + y - 1, 0, last_y)
            copies.append(
                pltpu.make_async_copy(
                    arrived_ref.at[source, 64:72], near_vmem.at[x * 3 + y], near_sem.at[x, y]
                )
            )
    for copy in copies:
        copy.start()

    @pl.loop(0, 8)
    def _(step):
        lanes = pl.ds(pl.multiple_of(step * 256, 256), 256)
        cell_z_ref[:, lanes] = z_neighbours(cells_ref[:, lanes].astype(jnp.float32))

    for copy in copies:
        copy.wait()
    for index, column in enumerate(spread_bricks([near_vmem[i] for i in range(9)], grid_flags())):
        bricks_ref[index] = column


def own_part(cells, arrived):
    return pl.pallas_call(
        own_kernel,
        out_shape=[
            jax.ShapeDtypeStruct((256, 2048), jnp.bfloat16),
            jax.ShapeDtypeStruct((16, 8, 128), jnp.float32),
        ],
        in_specs=[pl.BlockSpec(memory_space=pltpu.VMEM), pl.BlockSpec(memory_space=pl.ANY)],
        out_specs=[pl.BlockSpec(memory_space=pltpu.VMEM)] * 2,
        scratch_shapes=[
            pltpu.VMEM((9, 8, 128), jnp.bfloat16),
            pltpu.SemaphoreType.DMA((3, 3)),
        ],
        compiler_params=pltpu.CompilerParams(vmem_limit_bytes=8 << 20),
        name="leaf_own",
    )(cells, arrived)


def middle_kernel(
    cells_ref,
    west_ref,
    east_ref,
    lift_ref,
    taps_ref,
    own_z_ref,
    bricks_ref,
    one_ref,
    one_z_ref,
    low_ref,
    high_ref,
    cell_ref,
    cell_z_ref,
    leaf_mask_ref,
):
    flags = grid_flags()
    cell_ref[64:320] = cells_ref[...]
    for part in range(4):
        for row, ref, flag in ((0, west_ref, flags[0][0]), (320, east_ref, flags[0][2])):
            sums = ref[:, part * 256 : part * 256 + 256]
            lifted = jnp.dot(sums, lift_ref[...], preferred_element_type=jnp.float32) * flag
            cell_ref[row : row + 64, part * 512 : part * 512 + 512] = lifted.astype(jnp.bfloat16)
    low_ref[...] = cell_ref[:, :256]
    high_ref[...] = cell_ref[:, 1792:]

    cell_z_ref[64:320] = own_z_ref[...]
    for row in (0, 320):
        for part in range(4):
            lanes = slice(part * 512, part * 512 + 512)
            halo = cell_ref[row : row + 64, lanes].astype(jnp.float32)
            cell_z_ref[row : row + 64, lanes] = z_neighbours(halo)
    fill_leaf_mask([bricks_ref[i] for i in range(16)], leaf_mask_ref)
    taps = taps_ref[0].reshape(3072, 256)
    for first, count in ((0, 4), (4, 3)):
        sources = [(cell_ref, cell_z_ref, (first + i) * 256) for i in range(count)]
        for window, total in enumerate(leaf_sweep(sources, taps, 352)):
            step = first + window
            masks = [leaf_mask_ref[(2 * step + half + 9) // 8, 16:368] for half in range(2)]
            values = (total * jnp.concatenate(masks, 1)).astype(jnp.bfloat16)
            one_ref[:, step * 256 : step * 256 + 256] = values
            one_z_ref[:, step * 256 : step * 256 + 256] = z_neighbours(values.astype(jnp.float32))


def middle_part(cells, west, east, lift_block, taps, own_z, bricks):
    return pl.pallas_call(
        middle_kernel,
        out_shape=[
            jax.ShapeDtypeStruct((352, 1792), jnp.bfloat16),
            jax.ShapeDtypeStruct((352, 1792), jnp.bfloat16),
            jax.ShapeDtypeStruct((384, 256), jnp.bfloat16),
            jax.ShapeDtypeStruct((384, 256), jnp.bfloat16),
        ],
        in_specs=[pl.BlockSpec(memory_space=pltpu.VMEM)] * 7,
        out_specs=[pl.BlockSpec(memory_space=pltpu.VMEM)] * 4,
        scratch_shapes=[
            pltpu.VMEM((384, 2048), jnp.bfloat16),
            pltpu.VMEM((384, 2048), jnp.bfloat16),
            pltpu.VMEM((4, 384, 128), jnp.float32),
        ],
        compiler_params=pltpu.CompilerParams(vmem_limit_bytes=24 << 20),
        name="leaf_middle",
    )(cells, west, east, lift_block, taps, own_z, bricks)


def border_kernel(
    low_ref,
    high_ref,
    south_ref,
    north_ref,
    lift_ref,
    taps_ref,
    bricks_ref,
    one_middle_ref,
    one_z_middle_ref,
    down_leaf_ref,
    coarse_ref,
    down_ref,
    features_ref,
    down_two_ref,
    edge_ref,
    edge_z_ref,
    one_ref,
    one_z_ref,
    down_one_ref,
    parts_ref,
    down_leaf_vmem,
    coarse_vmem,
    down_vmem,
    leaf_mask_ref,
    one_sem,
    leaf_sem,
    coarse_sem,
    down_sem,
):
    early = [
        pltpu.make_async_copy(one_middle_ref, one_ref.at[:, 512:2304], one_sem.at[0]),
        pltpu.make_async_copy(one_z_middle_ref, one_z_ref.at[:, 512:2304], one_sem.at[1]),
        pltpu.make_async_copy(down_leaf_ref, down_leaf_vmem, leaf_sem),
    ]
    copies = []
    for dx in range(3):
        for dz in range(3):
            copies.append(
                pltpu.make_async_copy(
                    coarse_ref.at[0, dx, :, dz], coarse_vmem.at[dx, dz], coarse_sem.at[dx, dz]
                )
            )
    for a in range(2):
        for b in range(2):
            for c in range(2):
                copies.append(
                    pltpu.make_async_copy(
                        down_ref.at[0, a, b, c],
                        down_vmem.at[a, b, :, c * 128 : c * 128 + 128],
                        down_sem.at[a, b, c],
                    )
                )
    for copy in early + copies:
        copy.start()
    flags = grid_flags()
    edge_ref[0, :, 512:768] = low_ref[...]
    edge_ref[1, :, 0:256] = high_ref[...]
    for edge, lane, ref, flag in ((0, 0, south_ref, flags[1][0]), (1, 256, north_ref, flags[1][2])):
        for row, rows, other in ((0, 64, flags[0][0]), (64, 256, 1.0), (320, 64, flags[0][2])):
            sums = ref[row : row + rows]
            lifted = jnp.dot(sums, lift_ref[...], preferred_element_type=jnp.float32)
            lifted = (lifted * (flag * other)).astype(jnp.bfloat16)
            edge_ref[edge, row : row + rows, lane : lane + 512] = lifted
    fill_leaf_mask([bricks_ref[i] for i in range(16)], leaf_mask_ref)
    for edge in range(2):
        for part in range(3):
            lanes = slice(part * 256, part * 256 + 256)
            edge_z_ref[edge, :, lanes] = z_neighbours(edge_ref[edge, :, lanes].astype(jnp.float32))
    sources, steps = [], []
    for edge in range(2):
        for window in range(2):
            sources.append((edge_ref.at[edge], edge_z_ref.at[edge], window * 256))
            steps.append(edge * 9 + window)
    taps = taps_ref[0].reshape(3072, 256)
    for step, total in zip(steps, leaf_sweep(sources, taps, 352)):
        masks = [leaf_mask_ref[(2 * step + half + 5) // 8, 16:368] for half in range(2)]
        values = (total * jnp.concatenate(masks, 1)).astype(jnp.bfloat16)
        one_ref[:, step * 256 : step * 256 + 256] = values
        one_z_ref[:, step * 256 : step * 256 + 256] = z_neighbours(values.astype(jnp.float32))
    for copy in early:
        copy.wait()

    @pl.loop(0, 2)
    def _(half_step):
        first = half_step * 5
        lanes = [pl.multiple_of((first + i) * 256, 256) for i in range(5)]
        taps = taps_ref[1].reshape(3072, 256)
        totals = leaf_sweep([(one_ref, one_z_ref, lane) for lane in lanes], taps, 320)
        merges, masks = [], []
        for window, total in enumerate(totals):
            step = first + window
            mask = leaf_mask_ref[(2 * step + 6) // 8, 32:352]
            values = (total * jnp.concatenate([mask, mask], 1)).astype(jnp.bfloat16)

            @pl.when((step >= 1) & (step < 9))
            def _():
                for half in range(2):
                    inner = values[32:288, half * 128 : half * 128 + 128]
                    features_ref[:, 2 * step - 2 + half] = inner.reshape(16, 16, 128)

            pairs = values.reshape(10, 2, 16, 256)
            halves = [pairs[:, a].reshape(160, 256) for a in range(2)]
            merges.append(jnp.concatenate(halves, 1))
            masks.append(mask.reshape(10, 2, 16, 128)[:, 0].reshape(160, 128))
        taps = down_leaf_vmem[...].reshape(512, 128)
        total = jnp.dot(jnp.concatenate(merges, 0), taps, preferred_element_type=jnp.float32)
        total = jnp.maximum(total, 0.0) * jnp.concatenate(masks, 0)
        for window in range(5):
            down = total[window * 160 : window * 160 + 160].astype(jnp.bfloat16)
            before, after = row_shifts(down.astype(jnp.float32), 16)
            here = pl.ds(pl.multiple_of((first + window) * 128, 128), 128)
            down_one_ref[0, :, here] = before.astype(jnp.bfloat16)
            down_one_ref[1, :, here] = down
            down_one_ref[2, :, here] = after.astype(jnp.bfloat16)

    for copy in copies:
        copy.wait()
    windows = []
    for y in range(8):
        windows.append(
            jnp.concatenate(
                [
                    down_one_ref[dz, dx * 16 : dx * 16 + 128, y * 128 : y * 128 + 384]
                    for dx in range(3)
                    for dz in range(3)
                ],
                1,
            )
        )
    taps = coarse_vmem[...].reshape(3456, 128)
    total = jnp.dot(jnp.concatenate(windows, 0), taps, preferred_element_type=jnp.float32)
    total = jnp.maximum(total, 0.0).reshape(8, 128, 128)
    masks = [leaf_mask_ref[1 + y // 4, 64:320].reshape(8, 2, 16, 128)[:, 0] for y in range(8)]
    level = total * jnp.concatenate(masks, 0).reshape(8, 128, 128)
    level = level.astype(jnp.bfloat16).reshape(4, 2, 4, 2, 16, 128)
    merged = jnp.concatenate(
        [level[:, b, :, a].reshape(256, 128) for a in range(2) for b in range(2)], 1
    )
    taps = down_vmem[...].reshape(512, 256)
    parts = jnp.dot(merged, taps, preferred_element_type=jnp.float32)
    parts_ref[0] = parts[:, :128]
    parts_ref[1] = parts[:, 128:]
    total = parts_ref[0, pl.ds(0, 128, stride=2)] + parts_ref[1, pl.ds(1, 128, stride=2)]
    tiles = [bricks_ref[(1 + y // 2) * 4 + 1 + x // 2] for y in range(4) for x in range(4)]
    mask = jnp.concatenate(tiles, 0)
    down_two_ref[...] = (jnp.maximum(total, 0.0) * mask).astype(jnp.bfloat16)


def border_part(low, high, south, north, lift_block, taps, bricks, one, one_z, down_leaf, coarse, down):
    return pl.pallas_call(
        border_kernel,
        out_shape=[
            jax.ShapeDtypeStruct((16, 16, 16, 128), jnp.bfloat16),
            jax.ShapeDtypeStruct((128, 128), jnp.bfloat16),
        ],
        in_specs=[pl.BlockSpec(memory_space=pltpu.VMEM)] * 7
        + [pl.BlockSpec(memory_space=pl.ANY)] * 3
        + [pl.BlockSpec(memory_space=pltpu.HBM)] * 2,
        scratch_shapes=[
            pltpu.VMEM((2, 384, 768), jnp.bfloat16),
            pltpu.VMEM((2, 384, 768), jnp.bfloat16),
            pltpu.VMEM((352, 2816), jnp.bfloat16),
            pltpu.VMEM((352, 2816), jnp.bfloat16),
            pltpu.VMEM((3, 160, 1280), jnp.bfloat16),
            pltpu.VMEM((2, 256, 128), jnp.float32),
            pltpu.VMEM((2, 2, 2, 64, 128), jnp.bfloat16),
            pltpu.VMEM((3, 3, 3, 128, 128), jnp.bfloat16),
            pltpu.VMEM((2, 2, 128, 256), jnp.bfloat16),
            pltpu.VMEM((4, 384, 128), jnp.float32),
            pltpu.SemaphoreType.DMA((2,)),
            pltpu.SemaphoreType.DMA,
            pltpu.SemaphoreType.DMA((3, 3)),
            pltpu.SemaphoreType.DMA((2, 2, 2)),
        ],
        compiler_params=pltpu.CompilerParams(vmem_limit_bytes=32 << 20),
        name="leaf_border",
    )(low, high, south, north, lift_block, taps, bricks, one, one_z, down_leaf, coarse, down)


def coarse_kernel(
    south_ref,
    middle_ref,
    north_ref,
    coarse_ref,
    down_ref,
    bricks_ref,
    top_ref,
    parts_ref,
):
    here_x = lax.axis_index("gx")
    here_y = lax.axis_index("gy")
    from_west = jnp.where(here_x > 0, 1.0, 0.0)
    from_east = jnp.where(here_x < lax.axis_size("gx") - 1, 1.0, 0.0)
    from_south = jnp.where(here_y > 0, 1.0, 0.0)
    from_north = jnp.where(here_y < lax.axis_size("gy") - 1, 1.0, 0.0)

    strips = []
    for ref, first, flag in ((south_ref, 1, from_south), (middle_ref, 0, 1.0), (north_ref, 0, from_north)):
        count = 4 if ref is middle_ref else 3
        tiles = [ref[i].astype(jnp.float32).reshape(4, 4, 8, 128) for i in (2, 1, 0)]
        tiles = [tile[first : first + count] for tile in tiles]
        tiles = [
            tiles[0][:, 1:] * (flag * from_west),
            tiles[1] * flag,
            tiles[2][:, :3] * (flag * from_east),
        ]
        strips.append(jnp.concatenate(tiles, 1))
    grid = jnp.concatenate(strips, 0)
    before, after = row_shifts(grid.reshape(800, 128), 8)
    grids = [before.reshape(10, 10, 8, 128), grid, after.reshape(10, 10, 8, 128)]
    pieces = [
        grids[dz][dy : dy + 8, dx : dx + 8].reshape(512, 128).astype(jnp.bfloat16)
        for dx in range(3)
        for dy in range(3)
        for dz in range(3)
    ]
    taps = coarse_ref[1].reshape(3456, 128)
    total = jnp.dot(jnp.concatenate(pieces, 1), taps, preferred_element_type=jnp.float32)
    tiles = [bricks_ref[y // 2 * 4 + x // 2] for y in range(8) for x in range(8)]
    mask = jnp.concatenate(tiles, 0)
    level = jnp.maximum(total, 0.0) * mask
    level = level.reshape(4, 2, 4, 2, 8, 128)
    merged = jnp.concatenate(
        [level[:, b, :, a].reshape(128, 128) for a in range(2) for b in range(2)], 1
    ).astype(jnp.bfloat16)
    taps = [
        jnp.concatenate([down_ref[1, a, b, c] for c in range(2)], 1)
        for a in range(2)
        for b in range(2)
    ]
    taps = jnp.concatenate(taps, 0)
    parts = jnp.dot(merged, taps, preferred_element_type=jnp.float32)
    parts_ref[0] = parts[:, :128]
    parts_ref[1] = parts[:, 128:]
    total = parts_ref[0, pl.ds(0, 64, stride=2)] + parts_ref[1, pl.ds(1, 64, stride=2)]
    picks = lax.broadcasted_iota(jnp.int32, (64, 128), 0) * 2
    picks = picks == lax.broadcasted_iota(jnp.int32, (64, 128), 1)
    picks = jnp.where(picks, 1.0, 0.0).astype(jnp.bfloat16)
    bricks = bricks_ref[...].reshape(128, 128).astype(jnp.bfloat16)
    mask = jnp.dot(picks, bricks, preferred_element_type=jnp.float32)
    down = jnp.maximum(total, 0.0) * mask
    down = down.astype(jnp.bfloat16).astype(jnp.float32)
    before, after = row_shifts(down, 4)
    shifted = [before, down, after]
    pieces = []
    for dx in range(3):
        for dy in range(3):
            for dz in range(3):
                turn = (64 - (dy - 1) * 16 - (dx - 1) * 4) % 64
                moved = pltpu.roll(shifted[dz], turn, 0) if turn else shifted[dz]
                pieces.append(moved.astype(jnp.bfloat16))
    taps = coarse_ref[2].reshape(3456, 128)
    total = jnp.dot(jnp.concatenate(pieces, 1), taps, preferred_element_type=jnp.float32)
    top = (jnp.maximum(total, 0.0) * mask).astype(jnp.bfloat16)
    for x in range(2):
        for y in range(2):
            row = (y + 1) * 16 + (x + 1) * 4
            top_ref[x, y] = top[row : row + 4]


def coarse_levels(south, middle, north, coarse, down, bricks):
    return pl.pallas_call(
        coarse_kernel,
        out_shape=jax.ShapeDtypeStruct((2, 2, 4, 128), jnp.bfloat16),
        in_specs=[pl.BlockSpec(memory_space=pltpu.VMEM)] * 6,
        scratch_shapes=[pltpu.VMEM((2, 128, 128), jnp.float32)],
        compiler_params=pltpu.CompilerParams(vmem_limit_bytes=16 << 20),
        name="coarse_levels",
    )(south, middle, north, coarse, down, bricks)


def ring(values, axis, step):
    count = lax.axis_size(axis)
    return lax.ppermute(values, axis, [(i, (i + step) % count) for i in range(count)])


def per_device(
    records, slot_voxels, brick_mask, lift_weight, leaf_convs, down_leaf, down_coarse, coarse_convs
):
    messages = pack_messages(records[0], slot_voxels[0], brick_mask)
    arrived = lax.all_to_all(messages, ("gx", "gy"), split_axis=0, concat_axis=0, tiled=True)
    lift_block = jnp.kron(jnp.eye(8, dtype=jnp.bfloat16), lift_weight)
    taps = leaf_taps(leaf_convs)
    arrived, lift_block, taps = lax.optimization_barrier((arrived, lift_block, taps))
    coarse_hbm = pltpu.with_memory_space_constraint(coarse_convs, pltpu.HBM)
    down_hbm = pltpu.with_memory_space_constraint(down_coarse, pltpu.HBM)

    cells, low_x, high_x, low_y, high_y = scatter_and_lift(arrived, lift_block)
    west = ring(high_x, "gx", 1)
    east = ring(low_x, "gx", -1)
    own_z, bricks = own_part(cells, arrived)
    west, east, own_z = lax.optimization_barrier((west, east, own_z))
    south = ring(jnp.concatenate([west[:, 768:], high_y, east[:, 768:]], 0), "gy", 1)
    north = ring(jnp.concatenate([west[:, :256], low_y, east[:, :256]], 0), "gy", -1)
    one, one_z, low, high = middle_part(cells, west, east, lift_block, taps, own_z, bricks)
    features, down_two = border_part(
        low,
        high,
        south,
        north,
        lift_block,
        taps,
        bricks,
        one,
        one_z,
        down_leaf,
        coarse_hbm,
        down_hbm,
    )
    west = ring(down_two, "gx", 1)
    east = ring(down_two, "gx", -1)
    middle = jnp.stack([east, down_two, west])
    south = ring(middle, "gy", 1)
    north = ring(middle, "gy", -1)
    top = coarse_levels(south, middle, north, coarse_convs, down_coarse, bricks)
    return (features, top)


def solution(mesh):
    in_specs = (
        P(("gx", "gy"), None, None, None),
        P(("gx", "gy"), None, None),
        P("gx", "gy", None),
        P(),
        P(),
        P(),
        P(),
        P(),
    )
    out_specs = (P("gx", "gy", None, None), P("gx", "gy", None, None))
    return jax.shard_map(
        per_device, mesh=mesh, in_specs=in_specs, out_specs=out_specs, check_vma=False
    )
```

```python
import functools

import jax
import jax.numpy as jnp
from jax import lax
from jax.experimental import pallas as pl
from jax.experimental.pallas import tpu as pltpu
from jax.sharding import PartitionSpec as P

BRICK = 8
BUCKETS = 64


def pack_kernel(records_ref, slots_ref, bricks_ref, messages_ref, buffer_ref, in_sem, out_sem):
    buckets = slots_ref.shape[0]
    chunk = buckets // 4
    incoming, outgoing = [], []
    for part in range(4):
        here = slice(part * chunk, part * chunk + chunk)
        incoming.append(
            pltpu.make_async_copy(records_ref.at[here], buffer_ref.at[here, 0:64], in_sem.at[part])
        )
        outgoing.append(
            pltpu.make_async_copy(buffer_ref.at[here], messages_ref.at[here], out_sem.at[part])
        )
    for copy in incoming:
        copy.start()
    side = lax.rem(lax.axis_index("gy"), 2)
    slot = lax.broadcasted_iota(jnp.int32, (256, 128), 0)
    lane = lax.broadcasted_iota(jnp.int32, (256, 128), 1)
    picks = jnp.where((slot >> 2) + side * 64 == lane, 1.0, 0.0).astype(jnp.bfloat16)
    level = lax.broadcasted_iota(jnp.int32, (8, 128), 0) // 2
    place = lax.broadcasted_iota(jnp.int32, (8, 128), 1) - (1 - side) * 64
    bricks = jnp.zeros((8, 128), jnp.int32)
    for column in range(4):
        for z in range(4):
            here = (level == z) & (place >= column * 16) & (place < column * 16 + 16)
            bricks = jnp.where(here, bricks_ref[column // 2, column % 2, z], bricks)
    bricks = jnp.broadcast_to(bricks.astype(jnp.float32)[None], (chunk, 8, 128))
    shape = (chunk, 8, 256)
    row = lax.broadcasted_iota(jnp.int32, shape, 1)
    mine = (lax.broadcasted_iota(jnp.int32, shape, 2) & 3) == (row & 3)

    for part in range(4):
        here = slice(part * chunk, part * chunk + chunk)
        slots = slots_ref[here]
        high = (slots >> 9) * 16 + ((slots & 31) >> 1)
        low = ((slots >> 5) & 15) * 2 + (slots & 1)
        both = jnp.where(
            row < 4,
            jnp.broadcast_to(high.reshape(chunk, 1, 256), shape),
            jnp.broadcast_to(low.reshape(chunk, 1, 256), shape),
        )
        both = jnp.where(mine, both, 0).astype(jnp.float32)
        both = both.reshape(chunk * 8, 256).astype(jnp.bfloat16)
        ids = jnp.dot(both, picks, preferred_element_type=jnp.float32)
        buffer_ref[here, 64:72] = (ids.reshape(chunk, 8, 128) + bricks).astype(jnp.bfloat16)
        incoming[part].wait()
        outgoing[part].start()
    for copy in outgoing:
        copy.wait()


def pack_messages(records, slot_voxels, brick_mask):
    buckets, rows, width = records.shape
    return pl.pallas_call(
        pack_kernel,
        in_specs=[
            pl.BlockSpec(memory_space=pltpu.HBM),
            pl.BlockSpec(memory_space=pltpu.VMEM),
            pl.BlockSpec(memory_space=pltpu.SMEM),
        ],
        out_specs=pl.BlockSpec(memory_space=pltpu.HBM),
        out_shape=jax.ShapeDtypeStruct((buckets, rows + 8, width), jnp.bfloat16),
        scratch_shapes=[
            pltpu.VMEM((buckets, rows + 8, width), jnp.bfloat16),
            pltpu.SemaphoreType.DMA((4,)),
            pltpu.SemaphoreType.DMA((4,)),
        ],
        name="pack",
    )(records, slot_voxels, brick_mask)


def scatter_kernel(
    msg_ref, lift_ref, cells_ref, west_ref, east_ref, south_ref, north_ref, total_ref
):
    step = pl.program_id(0)

    @pl.when(step == 0)
    def _():
        total_ref[...] = jnp.zeros_like(total_ref)

    wide = 256
    lanes = lax.broadcasted_iota(jnp.int32, (wide, wide), 0).astype(jnp.bfloat16)
    zero = jnp.zeros((32, wide), jnp.bfloat16)
    left = lax.broadcasted_iota(jnp.int32, (8, 128), 1) < 64
    for quad in range(BUCKETS // 4):
        turned, ids = [], []
        for pair in range(2):
            first = quad * 4 + pair * 2
            rows = jnp.concatenate([msg_ref[first, 0:64], msg_ref[first + 1, 0:64]], 0)
            turned.append(jnp.transpose(rows))
            ids.append(
                jnp.where(
                    left,
                    msg_ref[first, 64:72].astype(jnp.float32),
                    msg_ref[first + 1, 64:72].astype(jnp.float32),
                )
            )
        turned = jnp.concatenate(turned, 1)
        ids = jnp.concatenate(ids, 1)
        for base in (0, 2):
            spreads, hots = [], []
            for quarter in (base, base + 1):
                features = turned[quarter * 32 : quarter * 32 + 32]
                high = jnp.broadcast_to(ids[quarter : quarter + 1], (wide, wide))
                low = jnp.broadcast_to(ids[quarter + 4 : quarter + 5], (32, wide))
                high, low = high.astype(jnp.bfloat16), low.astype(jnp.bfloat16)
                hots.append(jnp.where(lanes == high, 1.0, 0.0).astype(jnp.bfloat16))
                spreads += [
                    jnp.concatenate(
                        [jnp.where(low == jnp.bfloat16(i), features, zero) for i in range(32)], 0
                    )
                ]
            total_ref[...] += lax.dot_general(
                jnp.concatenate(spreads, 1),
                jnp.concatenate(hots, 1),
                (((1,), (1,)), ((), ())),
                preferred_element_type=jnp.float32,
            )

    @pl.when(step == pl.num_programs(0) - 1)
    def _():
        for part in range(4):
            summed = jnp.transpose(total_ref[part * wide : part * wide + wide])
            coarse = summed.astype(jnp.bfloat16)
            west_ref[:, part * wide : part * wide + wide] = coarse[:64]
            east_ref[:, part * wide : part * wide + wide] = coarse[192:]
            if part == 0:
                south_ref[...] = coarse
            if part == 3:
                north_ref[...] = coarse
            fine = (summed - coarse.astype(jnp.float32)).astype(jnp.bfloat16)
            lifted = jnp.dot(coarse, lift_ref[...], preferred_element_type=jnp.float32)
            lifted += jnp.dot(fine, lift_ref[...], preferred_element_type=jnp.float32)
            cells_ref[:, part * 512 : part * 512 + 512] = lifted.astype(jnp.bfloat16)


def scatter_and_lift(messages, lift_block):
    sources, rows, width = messages.shape
    shapes = [(256, 2048), (64, 1024), (64, 1024), (256, 256), (256, 256)]
    return pl.pallas_call(
        scatter_kernel,
        grid=(sources // BUCKETS,),
        in_specs=[
            pl.BlockSpec((BUCKETS, rows, width), lambda i: (i, 0, 0)),
            pl.BlockSpec((256, 512), lambda i: (0, 0)),
        ],
        out_specs=[pl.BlockSpec(memory_space=pltpu.VMEM)] * 5,
        out_shape=[jax.ShapeDtypeStruct(shape, jnp.bfloat16) for shape in shapes],
        scratch_shapes=[pltpu.VMEM((1024, 256), jnp.float32)],
        compiler_params=pltpu.CompilerParams(vmem_limit_bytes=14 << 20),
        name="scatter",
    )(messages, lift_block)


def leaf_taps_kernel(convs_ref, taps_ref):
    zero = jnp.zeros((64, 64), jnp.bfloat16)
    for layer in range(2):
        for dx in range(3):
            for kind in range(2):
                for step_y in range(4):
                    for half in range(2):
                        row = kind * 512 + step_y * 128 + half * 64
                        for out_y in range(2):
                            blocks = []
                            for out_z in range(2):
                                dy = step_y - out_y
                                if kind == 0:
                                    dz = half - out_z + 1
                                else:
                                    dz = 3 - out_z if half == 0 else -out_z
                                inside = 0 <= dy <= 2 and 0 <= dz <= 2
                                blocks.append(convs_ref[layer, dx, dy, dz] if inside else zero)
                            taps_ref[layer, dx, row : row + 64, out_y * 128 : out_y * 128 + 128] = (
                                jnp.concatenate(blocks, 1)
                            )


def leaf_taps(leaf_convs):
    return pl.pallas_call(
        leaf_taps_kernel,
        out_shape=jax.ShapeDtypeStruct((2, 3, 1024, 256), jnp.bfloat16),
        name="leaf_taps",
    )(leaf_convs)


def row_shifts(values, period):
    count = values.shape[0]
    place = lax.rem(lax.broadcasted_iota(jnp.int32, values.shape, 0), period)
    before = jnp.where(place == 0, 0.0, pltpu.roll(values, 1, 0))
    after = jnp.where(place == period - 1, 0.0, pltpu.roll(values, count - 1, 0))
    return before, after


def z_neighbours(values):
    before, after = row_shifts(values, 16)
    lane = lax.rem(lax.broadcasted_iota(jnp.int32, values.shape, 1), 128)
    return jnp.where(lane < 64, after, before).astype(jnp.bfloat16)


def spread_bricks(near, flags):
    side = lax.rem(lax.axis_index("gy"), 2)
    columns = []
    for y in range(4):
        for x in range(4):
            source_x, source_y = (0, 1, 1, 2)[x], (0, 1, 1, 2)[y]
            lane = ((1, 0, 1, 0)[x] * 2 + (1, 0, 1, 0)[y]) * 16
            tile = near[source_x * 3 + source_y].astype(jnp.float32)
            upper = side == 0 if source_y == 1 else side == 1
            value = jnp.where(upper, tile[:, 64 + lane : 65 + lane], tile[:, lane : lane + 1])
            flag = flags[0][source_x] * flags[1][source_y]
            columns.append(jnp.broadcast_to(value, (8, 128)) * flag)
    return columns


def doubled(column):
    level = lax.broadcasted_iota(jnp.int32, (16, 128), 0) // 4
    tile = jnp.broadcast_to(column[0:1], (16, 128))
    for z in range(1, 4):
        tile = jnp.where(level == z, jnp.broadcast_to(column[2 * z : 2 * z + 1], (16, 128)), tile)
    return tile


def grid_flags():
    here_x, here_y = lax.axis_index("gx"), lax.axis_index("gy")
    last_x, last_y = lax.axis_size("gx") - 1, lax.axis_size("gy") - 1
    return (
        (jnp.where(here_x > 0, 1.0, 0.0), 1.0, jnp.where(here_x < last_x, 1.0, 0.0)),
        (jnp.where(here_y > 0, 1.0, 0.0), 1.0, jnp.where(here_y < last_y, 1.0, 0.0)),
    )


def fill_leaf_mask(columns, leaf_mask_ref):
    for y in range(4):
        for x in range(4):
            tile = doubled(columns[y * 4 + x])
            for place_x in range(*((0, 4), (4, 12), (12, 20), (20, 24))[x]):
                leaf_mask_ref[y, place_x * 16 : place_x * 16 + 16] = tile


def leaf_sweep(sources, taps, rows):
    windows = []
    for source_ref, source_z_ref, lane in sources:
        pieces = []
        for dx in range(3):
            pieces.append(source_ref[dx * 16 : dx * 16 + rows, pl.ds(lane, 512)])
            pieces.append(source_z_ref[dx * 16 : dx * 16 + rows, pl.ds(lane, 512)])
        windows.append(jnp.concatenate(pieces, 1))
    total = jnp.dot(jnp.concatenate(windows, 0), taps, preferred_element_type=jnp.float32)
    total = jnp.maximum(total, 0.0)
    return [total[i * rows : i * rows + rows] for i in range(len(sources))]


def own_kernel(cells_ref, arrived_ref, cell_z_ref, bricks_ref, near_vmem, near_sem):
    last_x, last_y = lax.axis_size("gx") - 1, lax.axis_size("gy") - 1
    copies = []
    for x in range(3):
        for y in range(3):
            source = jnp.clip(lax.axis_index("gx") + x - 1, 0, last_x) * (last_y + 1)
            source = source + jnp.clip(lax.axis_index("gy") + y - 1, 0, last_y)
            copies.append(
                pltpu.make_async_copy(
                    arrived_ref.at[source, 64:72], near_vmem.at[x * 3 + y], near_sem.at[x, y]
                )
            )
    for copy in copies:
        copy.start()

    @pl.loop(0, 8)
    def _(step):
        lanes = pl.ds(pl.multiple_of(step * 256, 256), 256)
        cell_z_ref[:, lanes] = z_neighbours(cells_ref[:, lanes].astype(jnp.float32))

    for copy in copies:
        copy.wait()
    for index, column in enumerate(spread_bricks([near_vmem[i] for i in range(9)], grid_flags())):
        bricks_ref[index] = column


def own_part(cells, arrived):
    return pl.pallas_call(
        own_kernel,
        out_shape=[
            jax.ShapeDtypeStruct((256, 2048), jnp.bfloat16),
            jax.ShapeDtypeStruct((16, 8, 128), jnp.float32),
        ],
        in_specs=[pl.BlockSpec(memory_space=pltpu.VMEM), pl.BlockSpec(memory_space=pl.ANY)],
        out_specs=[pl.BlockSpec(memory_space=pltpu.VMEM)] * 2,
        scratch_shapes=[
            pltpu.VMEM((9, 8, 128), jnp.bfloat16),
            pltpu.SemaphoreType.DMA((3, 3)),
        ],
        compiler_params=pltpu.CompilerParams(vmem_limit_bytes=8 << 20),
        name="leaf_own",
    )(cells, arrived)


def middle_kernel(
    cells_ref,
    west_ref,
    east_ref,
    lift_ref,
    taps_ref,
    own_z_ref,
    bricks_ref,
    one_ref,
    one_z_ref,
    low_ref,
    high_ref,
    cell_ref,
    cell_z_ref,
    leaf_mask_ref,
):
    flags = grid_flags()
    cell_ref[64:320] = cells_ref[...]
    for part in range(4):
        for row, ref, flag in ((0, west_ref, flags[0][0]), (320, east_ref, flags[0][2])):
            sums = ref[:, part * 256 : part * 256 + 256]
            lifted = jnp.dot(sums, lift_ref[...], preferred_element_type=jnp.float32) * flag
            cell_ref[row : row + 64, part * 512 : part * 512 + 512] = lifted.astype(jnp.bfloat16)
    low_ref[...] = cell_ref[:, :256]
    high_ref[...] = cell_ref[:, 1792:]

    cell_z_ref[64:320] = own_z_ref[...]
    for row in (0, 320):
        for part in range(4):
            lanes = slice(part * 512, part * 512 + 512)
            halo = cell_ref[row : row + 64, lanes].astype(jnp.float32)
            cell_z_ref[row : row + 64, lanes] = z_neighbours(halo)
    fill_leaf_mask([bricks_ref[i] for i in range(16)], leaf_mask_ref)
    taps = taps_ref[0].reshape(3072, 256)
    for first, count in ((0, 4), (4, 3)):
        sources = [(cell_ref, cell_z_ref, (first + i) * 256) for i in range(count)]
        for window, total in enumerate(leaf_sweep(sources, taps, 352)):
            step = first + window
            masks = [leaf_mask_ref[(2 * step + half + 9) // 8, 16:368] for half in range(2)]
            values = (total * jnp.concatenate(masks, 1)).astype(jnp.bfloat16)
            one_ref[:, step * 256 : step * 256 + 256] = values
            one_z_ref[:, step * 256 : step * 256 + 256] = z_neighbours(values.astype(jnp.float32))


def middle_part(cells, west, east, lift_block, taps, own_z, bricks):
    return pl.pallas_call(
        middle_kernel,
        out_shape=[
            jax.ShapeDtypeStruct((352, 1792), jnp.bfloat16),
            jax.ShapeDtypeStruct((352, 1792), jnp.bfloat16),
            jax.ShapeDtypeStruct((384, 256), jnp.bfloat16),
            jax.ShapeDtypeStruct((384, 256), jnp.bfloat16),
        ],
        in_specs=[pl.BlockSpec(memory_space=pltpu.VMEM)] * 7,
        out_specs=[pl.BlockSpec(memory_space=pltpu.VMEM)] * 4,
        scratch_shapes=[
            pltpu.VMEM((384, 2048), jnp.bfloat16),
            pltpu.VMEM((384, 2048), jnp.bfloat16),
            pltpu.VMEM((4, 384, 128), jnp.float32),
        ],
        compiler_params=pltpu.CompilerParams(vmem_limit_bytes=24 << 20),
        name="leaf_middle",
    )(cells, west, east, lift_block, taps, own_z, bricks)


def border_kernel(
    low_ref,
    high_ref,
    north_ref,
    south_ref,
    lift_ref,
    taps_ref,
    bricks_ref,
    one_middle_ref,
    one_z_middle_ref,
    down_leaf_ref,
    coarse_ref,
    down_ref,
    features_ref,
    down_two_ref,
    edge_ref,
    edge_z_ref,
    one_ref,
    one_z_ref,
    down_one_ref,
    parts_ref,
    down_leaf_vmem,
    coarse_vmem,
    down_vmem,
    leaf_mask_ref,
    one_sem,
    leaf_sem,
    coarse_sem,
    down_sem,
):
    early = [
        pltpu.make_async_copy(one_middle_ref, one_ref.at[:, 512:2304], one_sem.at[0]),
        pltpu.make_async_copy(one_z_middle_ref, one_z_ref.at[:, 512:2304], one_sem.at[1]),
        pltpu.make_async_copy(down_leaf_ref, down_leaf_vmem, leaf_sem),
    ]
    copies = []
    for dx in range(3):
        for dz in range(3):
            copies.append(
                pltpu.make_async_copy(
                    coarse_ref.at[0, dx, :, dz], coarse_vmem.at[dx, dz], coarse_sem.at[dx, dz]
                )
            )
    for a in range(2):
        for b in range(2):
            for c in range(2):
                copies.append(
                    pltpu.make_async_copy(
                        down_ref.at[0, a, b, c],
                        down_vmem.at[a, b, :, c * 128 : c * 128 + 128],
                        down_sem.at[a, b, c],
                    )
                )
    for copy in early + copies:
        copy.start()
    flags = grid_flags()
    edge_ref[0, :, 512:768] = low_ref[...]
    edge_ref[1, :, 0:256] = high_ref[...]
    for edge, lane, ref, flag in ((0, 0, south_ref, flags[1][0]), (1, 256, north_ref, flags[1][2])):
        for row, rows, other in ((0, 64, flags[0][0]), (64, 256, 1.0), (320, 64, flags[0][2])):
            sums = ref[row : row + rows]
            lifted = jnp.dot(sums, lift_ref[...], preferred_element_type=jnp.float32)
            lifted = (lifted * (flag * other)).astype(jnp.bfloat16)
            edge_ref[edge, row : row + rows, lane : lane + 512] = lifted
    fill_leaf_mask([bricks_ref[i] for i in range(16)], leaf_mask_ref)
    for edge in range(2):
        for part in range(3):
            lanes = slice(part * 256, part * 256 + 256)
            edge_z_ref[edge, :, lanes] = z_neighbours(edge_ref[edge, :, lanes].astype(jnp.float32))
    sources, steps = [], []
    for edge in range(2):
        for window in range(2):
            sources.append((edge_ref.at[edge], edge_z_ref.at[edge], window * 256))
            steps.append(edge * 9 + window)
    taps = taps_ref[0].reshape(3072, 256)
    for step, total in zip(steps, leaf_sweep(sources, taps, 352)):
        masks = [leaf_mask_ref[(2 * step + half + 5) // 8, 16:368] for half in range(2)]
        values = (total * jnp.concatenate(masks, 1)).astype(jnp.bfloat16)
        one_ref[:, step * 256 : step * 256 + 256] = values
        one_z_ref[:, step * 256 : step * 256 + 256] = z_neighbours(values.astype(jnp.float32))
    for copy in early:
        copy.wait()

    @pl.loop(0, 2)
    def _(half_step):
        first = half_step * 5
        lanes = [pl.multiple_of((first + i) * 256, 256) for i in range(5)]
        taps = taps_ref[1].reshape(3072, 256)
        totals = leaf_sweep([(one_ref, one_z_ref, lane) for lane in lanes], taps, 320)
        merges, masks = [], []
        for window, total in enumerate(totals):
            step = first + window
            mask = leaf_mask_ref[(2 * step + 6) // 8, 32:352]
            values = (total * jnp.concatenate([mask, mask], 1)).astype(jnp.bfloat16)

            @pl.when((step >= 1) & (step < 9))
            def _():
                for half in range(2):
                    inner = values[32:288, half * 128 : half * 128 + 128]
                    features_ref[:, 2 * step - 2 + half] = inner.reshape(16, 16, 128)

            pairs = values.reshape(10, 2, 16, 256)
            halves = [pairs[:, a].reshape(160, 256) for a in range(2)]
            merges.append(jnp.concatenate(halves, 1))
            masks.append(mask.reshape(10, 2, 16, 128)[:, 0].reshape(160, 128))
        taps = down_leaf_vmem[...].reshape(512, 128)
        total = jnp.dot(jnp.concatenate(merges, 0), taps, preferred_element_type=jnp.float32)
        total = jnp.maximum(total, 0.0) * jnp.concatenate(masks, 0)
        for window in range(5):
            down = total[window * 160 : window * 160 + 160].astype(jnp.bfloat16)
            before, after = row_shifts(down.astype(jnp.float32), 16)
            here = pl.ds(pl.multiple_of((first + window) * 128, 128), 128)
            down_one_ref[0, :, here] = before.astype(jnp.bfloat16)
            down_one_ref[1, :, here] = down
            down_one_ref[2, :, here] = after.astype(jnp.bfloat16)

    for copy in copies:
        copy.wait()
    windows = []
    for y in range(8):
        windows.append(
            jnp.concatenate(
                [
                    down_one_ref[dz, dx * 16 : dx * 16 + 128, y * 128 : y * 128 + 384]
                    for dx in range(3)
                    for dz in range(3)
                ],
                1,
            )
        )
    taps = coarse_vmem[...].reshape(3456, 128)
    total = jnp.dot(jnp.concatenate(windows, 0), taps, preferred_element_type=jnp.float32)
    total = jnp.maximum(total, 0.0).reshape(8, 128, 128)
    masks = [leaf_mask_ref[1 + y // 4, 64:320].reshape(8, 2, 16, 128)[:, 0] for y in range(8)]
    level = total * jnp.concatenate(masks, 0).reshape(8, 128, 128)
    level = level.astype(jnp.bfloat16).reshape(4, 2, 4, 2, 16, 128)
    merged = jnp.concatenate(
        [level[:, b, :, a].reshape(256, 128) for a in range(2) for b in range(2)], 1
    )
    taps = down_vmem[...].reshape(512, 256)
    parts = jnp.dot(merged, taps, preferred_element_type=jnp.float32)
    parts_ref[0] = parts[:, :128]
    parts_ref[1] = parts[:, 128:]
    total = parts_ref[0, pl.ds(0, 128, stride=2)] + parts_ref[1, pl.ds(1, 128, stride=2)]
    tiles = [bricks_ref[(1 + y // 2) * 4 + 1 + x // 2] for y in range(4) for x in range(4)]
    mask = jnp.concatenate(tiles, 0)
    down_two_ref[...] = (jnp.maximum(total, 0.0) * mask).astype(jnp.bfloat16)


def border_part(low, high, north, south, lift_block, taps, bricks, one, one_z, down_leaf, coarse, down):
    return pl.pallas_call(
        border_kernel,
        out_shape=[
            jax.ShapeDtypeStruct((16, 16, 16, 128), jnp.bfloat16),
            jax.ShapeDtypeStruct((128, 128), jnp.bfloat16),
        ],
        in_specs=[pl.BlockSpec(memory_space=pltpu.VMEM)] * 7
        + [pl.BlockSpec(memory_space=pl.ANY)] * 3
        + [pl.BlockSpec(memory_space=pltpu.HBM)] * 2,
        scratch_shapes=[
            pltpu.VMEM((2, 384, 768), jnp.bfloat16),
            pltpu.VMEM((2, 384, 768), jnp.bfloat16),
            pltpu.VMEM((352, 2816), jnp.bfloat16),
            pltpu.VMEM((352, 2816), jnp.bfloat16),
            pltpu.VMEM((3, 160, 1280), jnp.bfloat16),
            pltpu.VMEM((2, 256, 128), jnp.float32),
            pltpu.VMEM((2, 2, 2, 64, 128), jnp.bfloat16),
            pltpu.VMEM((3, 3, 3, 128, 128), jnp.bfloat16),
            pltpu.VMEM((2, 2, 128, 256), jnp.bfloat16),
            pltpu.VMEM((4, 384, 128), jnp.float32),
            pltpu.SemaphoreType.DMA((2,)),
            pltpu.SemaphoreType.DMA,
            pltpu.SemaphoreType.DMA((3, 3)),
            pltpu.SemaphoreType.DMA((2, 2, 2)),
        ],
        compiler_params=pltpu.CompilerParams(vmem_limit_bytes=32 << 20),
        name="leaf_border",
    )(low, high, north, south, lift_block, taps, bricks, one, one_z, down_leaf, coarse, down)


def coarse_kernel(
    south_ref,
    middle_ref,
    north_ref,
    coarse_ref,
    down_ref,
    bricks_ref,
    top_ref,
    parts_ref,
):
    here_x = lax.axis_index("gx")
    here_y = lax.axis_index("gy")
    from_west = jnp.where(here_x > 0, 1.0, 0.0)
    from_east = jnp.where(here_x < lax.axis_size("gx") - 1, 1.0, 0.0)
    from_south = jnp.where(here_y > 0, 1.0, 0.0)
    from_north = jnp.where(here_y < lax.axis_size("gy") - 1, 1.0, 0.0)

    strips = []
    for ref, first, flag in ((south_ref, 1, from_south), (middle_ref, 0, 1.0), (north_ref, 0, from_north)):
        count = 4 if ref is middle_ref else 3
        tiles = [ref[i].astype(jnp.float32).reshape(4, 4, 8, 128) for i in (2, 1, 0)]
        tiles = [tile[first : first + count] for tile in tiles]
        tiles = [
            tiles[0][:, 1:] * (flag * from_west),
            tiles[1] * flag,
            tiles[2][:, :3] * (flag * from_east),
        ]
        strips.append(jnp.concatenate(tiles, 1))
    grid = jnp.concatenate(strips, 0)
    before, after = row_shifts(grid.reshape(800, 128), 8)
    grids = [before.reshape(10, 10, 8, 128), grid, after.reshape(10, 10, 8, 128)]
    pieces = [
        grids[dz][dy : dy + 8, dx : dx + 8].reshape(512, 128).astype(jnp.bfloat16)
        for dx in range(3)
        for dy in range(3)
        for dz in range(3)
    ]
    taps = coarse_ref[1].reshape(3456, 128)
    total = jnp.dot(jnp.concatenate(pieces, 1), taps, preferred_element_type=jnp.float32)
    tiles = [bricks_ref[y // 2 * 4 + x // 2] for y in range(8) for x in range(8)]
    mask = jnp.concatenate(tiles, 0)
    level = jnp.maximum(total, 0.0) * mask
    level = level.reshape(4, 2, 4, 2, 8, 128)
    merged = jnp.concatenate(
        [level[:, b, :, a].reshape(128, 128) for a in range(2) for b in range(2)], 1
    ).astype(jnp.bfloat16)
    taps = [
        jnp.concatenate([down_ref[1, a, b, c] for c in range(2)], 1)
        for a in range(2)
        for b in range(2)
    ]
    taps = jnp.concatenate(taps, 0)
    parts = jnp.dot(merged, taps, preferred_element_type=jnp.float32)
    parts_ref[0] = parts[:, :128]
    parts_ref[1] = parts[:, 128:]
    total = parts_ref[0, pl.ds(0, 64, stride=2)] + parts_ref[1, pl.ds(1, 64, stride=2)]
    picks = lax.broadcasted_iota(jnp.int32, (64, 128), 0) * 2
    picks = picks == lax.broadcasted_iota(jnp.int32, (64, 128), 1)
    picks = jnp.where(picks, 1.0, 0.0).astype(jnp.bfloat16)
    bricks = bricks_ref[...].reshape(128, 128).astype(jnp.bfloat16)
    mask = jnp.dot(picks, bricks, preferred_element_type=jnp.float32)
    down = jnp.maximum(total, 0.0) * mask
    down = down.astype(jnp.bfloat16).astype(jnp.float32)
    before, after = row_shifts(down, 4)
    shifted = [before, down, after]
    pieces = []
    for dx in range(3):
        for dy in range(3):
            for dz in range(3):
                turn = (64 - (dy - 1) * 16 - (dx - 1) * 4) % 64
                moved = pltpu.roll(shifted[dz], turn, 0) if turn else shifted[dz]
                pieces.append(moved.astype(jnp.bfloat16))
    taps = coarse_ref[2].reshape(3456, 128)
    total = jnp.dot(jnp.concatenate(pieces, 1), taps, preferred_element_type=jnp.float32)
    top = (jnp.maximum(total, 0.0) * mask).astype(jnp.bfloat16)
    for x in range(2):
        for y in range(2):
            row = (y + 1) * 16 + (x + 1) * 4
            top_ref[x, y] = top[row : row + 4]


def coarse_levels(south, middle, north, coarse, down, bricks):
    return pl.pallas_call(
        coarse_kernel,
        out_shape=jax.ShapeDtypeStruct((2, 2, 4, 128), jnp.bfloat16),
        in_specs=[pl.BlockSpec(memory_space=pltpu.VMEM)] * 6,
        scratch_shapes=[pltpu.VMEM((2, 128, 128), jnp.float32)],
        compiler_params=pltpu.CompilerParams(vmem_limit_bytes=16 << 20),
        name="coarse_levels",
    )(south, middle, north, coarse, down, bricks)


def ring(values, axis, step):
    count = lax.axis_size(axis)
    return lax.ppermute(values, axis, [(i, (i + step) % count) for i in range(count)])


def per_device(
    records, slot_voxels, brick_mask, lift_weight, leaf_convs, down_leaf, down_coarse, coarse_convs
):
    messages = pack_messages(records[0], slot_voxels[0], brick_mask)
    arrived = lax.all_to_all(messages, ("gx", "gy"), split_axis=0, concat_axis=0, tiled=True)
    lift_block = jnp.kron(jnp.eye(8, dtype=jnp.bfloat16), lift_weight)
    taps = leaf_taps(leaf_convs)
    arrived, lift_block, taps = lax.optimization_barrier((arrived, lift_block, taps))
    coarse_hbm = pltpu.with_memory_space_constraint(coarse_convs, pltpu.HBM)
    down_hbm = pltpu.with_memory_space_constraint(down_coarse, pltpu.HBM)

    cells, low_x, high_x, low_y, high_y = scatter_and_lift(arrived, lift_block)
    west = ring(high_x, "gx", 1)
    east = ring(low_x, "gx", -1)
    own_z, bricks = own_part(cells, arrived)
    west, east, own_z = lax.optimization_barrier((west, east, own_z))
    north = ring(jnp.concatenate([west[:, :256], low_y, east[:, :256]], 0), "gy", -1)
    south = ring(jnp.concatenate([west[:, 768:], high_y, east[:, 768:]], 0), "gy", 1)
    one, one_z, low, high = middle_part(cells, west, east, lift_block, taps, own_z, bricks)
    features, down_two = border_part(
        low,
        high,
        north,
        south,
        lift_block,
        taps,
        bricks,
        one,
        one_z,
        down_leaf,
        coarse_hbm,
        down_hbm,
    )
    west = ring(down_two, "gx", 1)
    east = ring(down_two, "gx", -1)
    middle = jnp.stack([east, down_two, west])
    south = ring(middle, "gy", 1)
    north = ring(middle, "gy", -1)
    top = coarse_levels(south, middle, north, coarse_convs, down_coarse, bricks)
    return (features, top)


def solution(mesh):
    in_specs = (
        P(("gx", "gy"), None, None, None),
        P(("gx", "gy"), None, None),
        P("gx", "gy", None),
        P(),
        P(),
        P(),
        P(),
        P(),
    )
    out_specs = (P("gx", "gy", None, None), P("gx", "gy", None, None))
    return jax.shard_map(
        per_device, mesh=mesh, in_specs=in_specs, out_specs=out_specs, check_vma=False
    )
```

```python
import functools

import jax
import jax.numpy as jnp
from jax import lax
from jax.experimental import pallas as pl
from jax.experimental.pallas import tpu as pltpu
from jax.sharding import PartitionSpec as P

BRICK = 8
BUCKETS = 64


def pack_kernel(records_ref, slots_ref, bricks_ref, messages_ref, buffer_ref, in_sem, out_sem):
    buckets = slots_ref.shape[0]
    chunk = buckets // 4
    incoming, outgoing = [], []
    for part in range(4):
        here = slice(part * chunk, part * chunk + chunk)
        incoming.append(
            pltpu.make_async_copy(records_ref.at[here], buffer_ref.at[here, 0:64], in_sem.at[part])
        )
        outgoing.append(
            pltpu.make_async_copy(buffer_ref.at[here], messages_ref.at[here], out_sem.at[part])
        )
    for copy in incoming:
        copy.start()
    side = lax.rem(lax.axis_index("gy"), 2)
    slot = lax.broadcasted_iota(jnp.int32, (256, 128), 0)
    lane = lax.broadcasted_iota(jnp.int32, (256, 128), 1)
    picks = jnp.where((slot >> 2) + side * 64 == lane, 1.0, 0.0).astype(jnp.bfloat16)
    level = lax.broadcasted_iota(jnp.int32, (8, 128), 0) // 2
    place = lax.broadcasted_iota(jnp.int32, (8, 128), 1) - (1 - side) * 64
    bricks = jnp.zeros((8, 128), jnp.int32)
    for column in range(4):
        for z in range(4):
            here = (level == z) & (place >= column * 16) & (place < column * 16 + 16)
            bricks = jnp.where(here, bricks_ref[column // 2, column % 2, z], bricks)
    bricks = jnp.broadcast_to(bricks.astype(jnp.float32)[None], (chunk, 8, 128))
    shape = (chunk, 8, 256)
    row = lax.broadcasted_iota(jnp.int32, shape, 1)
    mine = (lax.broadcasted_iota(jnp.int32, shape, 2) & 3) == (row & 3)

    for part in range(4):
        here = slice(part * chunk, part * chunk + chunk)
        slots = slots_ref[here]
        high = (slots >> 9) * 16 + ((slots & 31) >> 1)
        low = ((slots >> 5) & 15) * 2 + (slots & 1)
        both = jnp.where(
            row < 4,
            jnp.broadcast_to(high.reshape(chunk, 1, 256), shape),
            jnp.broadcast_to(low.reshape(chunk, 1, 256), shape),
        )
        both = jnp.where(mine, both, 0).astype(jnp.float32)
        both = both.reshape(chunk * 8, 256).astype(jnp.bfloat16)
        ids = jnp.dot(both, picks, preferred_element_type=jnp.float32)
        buffer_ref[here, 64:72] = (ids.reshape(chunk, 8, 128) + bricks).astype(jnp.bfloat16)
        incoming[part].wait()
        outgoing[part].start()
    for copy in outgoing:
        copy.wait()


def pack_messages(records, slot_voxels, brick_mask):
    buckets, rows, width = records.shape
    return pl.pallas_call(
        pack_kernel,
        in_specs=[
            pl.BlockSpec(memory_space=pltpu.HBM),
            pl.BlockSpec(memory_space=pltpu.VMEM),
            pl.BlockSpec(memory_space=pltpu.SMEM),
        ],
        out_specs=pl.BlockSpec(memory_space=pltpu.HBM),
        out_shape=jax.ShapeDtypeStruct((buckets, rows + 8, width), jnp.bfloat16),
        scratch_shapes=[
            pltpu.VMEM((buckets, rows + 8, width), jnp.bfloat16),
            pltpu.SemaphoreType.DMA((4,)),
            pltpu.SemaphoreType.DMA((4,)),
        ],
        name="pack",
    )(records, slot_voxels, brick_mask)


def scatter_kernel(
    msg_ref, coarse_ref, fine_ref, west_ref, east_ref, south_ref, north_ref, total_ref
):
    step = pl.program_id(0)

    @pl.when(step == 0)
    def _():
        total_ref[...] = jnp.zeros_like(total_ref)

    wide = 256
    lanes = lax.broadcasted_iota(jnp.int32, (wide, wide), 0).astype(jnp.bfloat16)
    zero = jnp.zeros((32, wide), jnp.bfloat16)
    left = lax.broadcasted_iota(jnp.int32, (8, 128), 1) < 64
    for quad in range(BUCKETS // 4):
        turned, ids = [], []
        for pair in range(2):
            first = quad * 4 + pair * 2
            rows = jnp.concatenate([msg_ref[first, 0:64], msg_ref[first + 1, 0:64]], 0)
            turned.append(jnp.transpose(rows))
            ids.append(
                jnp.where(
                    left,
                    msg_ref[first, 64:72].astype(jnp.float32),
                    msg_ref[first + 1, 64:72].astype(jnp.float32),
                )
            )
        turned = jnp.concatenate(turned, 1)
        ids = jnp.concatenate(ids, 1)
        for base in (0, 2):
            spreads, hots = [], []
            for quarter in (base, base + 1):
                features = turned[quarter * 32 : quarter * 32 + 32]
                high = jnp.broadcast_to(ids[quarter : quarter + 1], (wide, wide))
                low = jnp.broadcast_to(ids[quarter + 4 : quarter + 5], (32, wide))
                high, low = high.astype(jnp.bfloat16), low.astype(jnp.bfloat16)
                hots.append(jnp.where(lanes == high, 1.0, 0.0).astype(jnp.bfloat16))
                spreads += [
                    jnp.concatenate(
                        [jnp.where(low == jnp.bfloat16(i), features, zero) for i in range(32)], 0
                    )
                ]
            total_ref[...] += lax.dot_general(
                jnp.concatenate(spreads, 1),
                jnp.concatenate(hots, 1),
                (((1,), (1,)), ((), ())),
                preferred_element_type=jnp.float32,
            )

    @pl.when(step == pl.num_programs(0) - 1)
    def _():
        for part in range(4):
            summed = jnp.transpose(total_ref[part * wide : part * wide + wide])
            coarse = summed.astype(jnp.bfloat16)
            lanes = slice(part * wide, part * wide + wide)
            coarse_ref[:, lanes] = coarse
            fine_ref[:, lanes] = (summed - coarse.astype(jnp.float32)).astype(jnp.bfloat16)
            west_ref[:, lanes] = coarse[:64]
            east_ref[:, lanes] = coarse[192:]
            if part == 0:
                south_ref[...] = coarse
            if part == 3:
                north_ref[...] = coarse


def scatter(messages):
    sources, rows, width = messages.shape
    shapes = [(256, 1024)] * 2 + [(64, 1024)] * 2 + [(256, 256)] * 2
    return pl.pallas_call(
        scatter_kernel,
        grid=(sources // BUCKETS,),
        in_specs=[
            pl.BlockSpec((BUCKETS, rows, width), lambda i: (i, 0, 0)),
        ],
        out_specs=[pl.BlockSpec(memory_space=pltpu.VMEM)] * 6,
        out_shape=[jax.ShapeDtypeStruct(shape, jnp.bfloat16) for shape in shapes],
        scratch_shapes=[pltpu.VMEM((1024, 256), jnp.float32)],
        compiler_params=pltpu.CompilerParams(vmem_limit_bytes=14 << 20),
        name="scatter",
    )(messages)


def leaf_taps_kernel(convs_ref, taps_ref):
    zero = jnp.zeros((64, 64), jnp.bfloat16)
    for layer in range(2):
        for dx in range(3):
            for kind in range(2):
                for step_y in range(4):
                    for half in range(2):
                        row = kind * 512 + step_y * 128 + half * 64
                        for out_y in range(2):
                            blocks = []
                            for out_z in range(2):
                                dy = step_y - out_y
                                if kind == 0:
                                    dz = half - out_z + 1
                                else:
                                    dz = 3 - out_z if half == 0 else -out_z
                                inside = 0 <= dy <= 2 and 0 <= dz <= 2
                                blocks.append(convs_ref[layer, dx, dy, dz] if inside else zero)
                            taps_ref[layer, dx, row : row + 64, out_y * 128 : out_y * 128 + 128] = (
                                jnp.concatenate(blocks, 1)
                            )


def leaf_taps(leaf_convs):
    return pl.pallas_call(
        leaf_taps_kernel,
        out_shape=jax.ShapeDtypeStruct((2, 3, 1024, 256), jnp.bfloat16),
        name="leaf_taps",
    )(leaf_convs)


def row_shifts(values, period):
    count = values.shape[0]
    place = lax.rem(lax.broadcasted_iota(jnp.int32, values.shape, 0), period)
    before = jnp.where(place == 0, 0.0, pltpu.roll(values, 1, 0))
    after = jnp.where(place == period - 1, 0.0, pltpu.roll(values, count - 1, 0))
    return before, after


def z_neighbours(values):
    before, after = row_shifts(values, 16)
    lane = lax.rem(lax.broadcasted_iota(jnp.int32, values.shape, 1), 128)
    return jnp.where(lane < 64, after, before).astype(jnp.bfloat16)


def spread_bricks(near, flags):
    side = lax.rem(lax.axis_index("gy"), 2)
    columns = []
    for y in range(4):
        for x in range(4):
            source_x, source_y = (0, 1, 1, 2)[x], (0, 1, 1, 2)[y]
            lane = ((1, 0, 1, 0)[x] * 2 + (1, 0, 1, 0)[y]) * 16
            tile = near[source_x * 3 + source_y].astype(jnp.float32)
            upper = side == 0 if source_y == 1 else side == 1
            value = jnp.where(upper, tile[:, 64 + lane : 65 + lane], tile[:, lane : lane + 1])
            flag = flags[0][source_x] * flags[1][source_y]
            columns.append(jnp.broadcast_to(value, (8, 128)) * flag)
    return columns


def doubled(column):
    level = lax.broadcasted_iota(jnp.int32, (16, 128), 0) // 4
    tile = jnp.broadcast_to(column[0:1], (16, 128))
    for z in range(1, 4):
        tile = jnp.where(level == z, jnp.broadcast_to(column[2 * z : 2 * z + 1], (16, 128)), tile)
    return tile


def grid_flags():
    here_x, here_y = lax.axis_index("gx"), lax.axis_index("gy")
    last_x, last_y = lax.axis_size("gx") - 1, lax.axis_size("gy") - 1
    return (
        (jnp.where(here_x > 0, 1.0, 0.0), 1.0, jnp.where(here_x < last_x, 1.0, 0.0)),
        (jnp.where(here_y > 0, 1.0, 0.0), 1.0, jnp.where(here_y < last_y, 1.0, 0.0)),
    )


def fill_leaf_mask(columns, leaf_mask_ref):
    for y in range(4):
        for x in range(4):
            tile = doubled(columns[y * 4 + x])
            for place_x in range(*((0, 4), (4, 12), (12, 20), (20, 24))[x]):
                leaf_mask_ref[y, place_x * 16 : place_x * 16 + 16] = tile


def leaf_sweep(sources, taps, rows):
    windows = []
    for source_ref, source_z_ref, lane in sources:
        pieces = []
        for dx in range(3):
            pieces.append(source_ref[dx * 16 : dx * 16 + rows, pl.ds(lane, 512)])
            pieces.append(source_z_ref[dx * 16 : dx * 16 + rows, pl.ds(lane, 512)])
        windows.append(jnp.concatenate(pieces, 1))
    total = jnp.dot(jnp.concatenate(windows, 0), taps, preferred_element_type=jnp.float32)
    total = jnp.maximum(total, 0.0)
    return [total[i * rows : i * rows + rows] for i in range(len(sources))]


def own_kernel(
    coarse_ref,
    fine_ref,
    lift_ref,
    arrived_ref,
    cells_ref,
    cell_z_ref,
    bricks_ref,
    near_vmem,
    near_sem,
):
    last_x, last_y = lax.axis_size("gx") - 1, lax.axis_size("gy") - 1
    copies = []
    for x in range(3):
        for y in range(3):
            source = jnp.clip(lax.axis_index("gx") + x - 1, 0, last_x) * (last_y + 1)
            source = source + jnp.clip(lax.axis_index("gy") + y - 1, 0, last_y)
            copies.append(
                pltpu.make_async_copy(
                    arrived_ref.at[source, 64:72], near_vmem.at[x * 3 + y], near_sem.at[x, y]
                )
            )
    for copy in copies:
        copy.start()

    @pl.loop(0, 4)
    def _(part):
        sums = pl.ds(pl.multiple_of(part * 256, 256), 256)
        lanes = pl.ds(pl.multiple_of(part * 512, 512), 512)
        lifted = jnp.dot(coarse_ref[:, sums], lift_ref[...], preferred_element_type=jnp.float32)
        lifted += jnp.dot(fine_ref[:, sums], lift_ref[...], preferred_element_type=jnp.float32)
        cells = lifted.astype(jnp.bfloat16)
        cells_ref[:, lanes] = cells
        cell_z_ref[:, lanes] = z_neighbours(cells.astype(jnp.float32))

    for copy in copies:
        copy.wait()
    for index, column in enumerate(spread_bricks([near_vmem[i] for i in range(9)], grid_flags())):
        bricks_ref[index] = column


def own_part(coarse, fine, lift_block, arrived):
    return pl.pallas_call(
        own_kernel,
        out_shape=[
            jax.ShapeDtypeStruct((256, 2048), jnp.bfloat16),
            jax.ShapeDtypeStruct((256, 2048), jnp.bfloat16),
            jax.ShapeDtypeStruct((16, 8, 128), jnp.float32),
        ],
        in_specs=[pl.BlockSpec(memory_space=pltpu.VMEM)] * 3
        + [pl.BlockSpec(memory_space=pl.ANY)],
        out_specs=[pl.BlockSpec(memory_space=pltpu.VMEM)] * 3,
        scratch_shapes=[
            pltpu.VMEM((9, 8, 128), jnp.bfloat16),
            pltpu.SemaphoreType.DMA((3, 3)),
        ],
        compiler_params=pltpu.CompilerParams(vmem_limit_bytes=8 << 20),
        name="leaf_own",
    )(coarse, fine, lift_block, arrived)


def middle_kernel(
    cells_ref,
    west_ref,
    east_ref,
    lift_ref,
    taps_ref,
    own_z_ref,
    bricks_ref,
    one_ref,
    one_z_ref,
    low_ref,
    high_ref,
    cell_ref,
    cell_z_ref,
    leaf_mask_ref,
):
    flags = grid_flags()
    cell_ref[64:320] = cells_ref[...]
    for part in range(4):
        for row, ref, flag in ((0, west_ref, flags[0][0]), (320, east_ref, flags[0][2])):
            sums = ref[:, part * 256 : part * 256 + 256]
            lifted = jnp.dot(sums, lift_ref[...], preferred_element_type=jnp.float32) * flag
            cell_ref[row : row + 64, part * 512 : part * 512 + 512] = lifted.astype(jnp.bfloat16)
    low_ref[...] = cell_ref[:, :256]
    high_ref[...] = cell_ref[:, 1792:]

    cell_z_ref[64:320] = own_z_ref[...]
    for row in (0, 320):
        for part in range(4):
            lanes = slice(part * 512, part * 512 + 512)
            halo = cell_ref[row : row + 64, lanes].astype(jnp.float32)
            cell_z_ref[row : row + 64, lanes] = z_neighbours(halo)
    fill_leaf_mask([bricks_ref[i] for i in range(16)], leaf_mask_ref)
    taps = taps_ref[0].reshape(3072, 256)
    for first, count in ((0, 4), (4, 3)):
        sources = [(cell_ref, cell_z_ref, (first + i) * 256) for i in range(count)]
        for window, total in enumerate(leaf_sweep(sources, taps, 352)):
            step = first + window
            masks = [leaf_mask_ref[(2 * step + half + 9) // 8, 16:368] for half in range(2)]
            values = (total * jnp.concatenate(masks, 1)).astype(jnp.bfloat16)
            one_ref[:, step * 256 : step * 256 + 256] = values
            one_z_ref[:, step * 256 : step * 256 + 256] = z_neighbours(values.astype(jnp.float32))


def middle_part(cells, west, east, lift_block, taps, own_z, bricks):
    return pl.pallas_call(
        middle_kernel,
        out_shape=[
            jax.ShapeDtypeStruct((352, 1792), jnp.bfloat16),
            jax.ShapeDtypeStruct((352, 1792), jnp.bfloat16),
            jax.ShapeDtypeStruct((384, 256), jnp.bfloat16),
            jax.ShapeDtypeStruct((384, 256), jnp.bfloat16),
        ],
        in_specs=[pl.BlockSpec(memory_space=pltpu.VMEM)] * 7,
        out_specs=[pl.BlockSpec(memory_space=pltpu.VMEM)] * 4,
        scratch_shapes=[
            pltpu.VMEM((384, 2048), jnp.bfloat16),
            pltpu.VMEM((384, 2048), jnp.bfloat16),
            pltpu.VMEM((4, 384, 128), jnp.float32),
        ],
        compiler_params=pltpu.CompilerParams(vmem_limit_bytes=24 << 20),
        name="leaf_middle",
    )(cells, west, east, lift_block, taps, own_z, bricks)


def border_kernel(
    low_ref,
    high_ref,
    north_ref,
    south_ref,
    lift_ref,
    taps_ref,
    bricks_ref,
    one_middle_ref,
    one_z_middle_ref,
    down_leaf_ref,
    coarse_ref,
    down_ref,
    features_ref,
    down_two_ref,
    edge_ref,
    edge_z_ref,
    one_ref,
    one_z_ref,
    down_one_ref,
    parts_ref,
    down_leaf_vmem,
    coarse_vmem,
    down_vmem,
    leaf_mask_ref,
    one_sem,
    leaf_sem,
    coarse_sem,
    down_sem,
):
    early = [
        pltpu.make_async_copy(one_middle_ref, one_ref.at[:, 512:2304], one_sem.at[0]),
        pltpu.make_async_copy(one_z_middle_ref, one_z_ref.at[:, 512:2304], one_sem.at[1]),
        pltpu.make_async_copy(down_leaf_ref, down_leaf_vmem, leaf_sem),
    ]
    copies = []
    for dx in range(3):
        for dz in range(3):
            copies.append(
                pltpu.make_async_copy(
                    coarse_ref.at[0, dx, :, dz], coarse_vmem.at[dx, dz], coarse_sem.at[dx, dz]
                )
            )
    for a in range(2):
        for b in range(2):
            for c in range(2):
                copies.append(
                    pltpu.make_async_copy(
                        down_ref.at[0, a, b, c],
                        down_vmem.at[a, b, :, c * 128 : c * 128 + 128],
                        down_sem.at[a, b, c],
                    )
                )
    for copy in early + copies:
        copy.start()
    flags = grid_flags()
    edge_ref[0, :, 512:768] = low_ref[...]
    edge_ref[1, :, 0:256] = high_ref[...]
    for edge, lane, ref, flag in ((0, 0, south_ref, flags[1][0]), (1, 256, north_ref, flags[1][2])):
        for row, rows, other in ((0, 64, flags[0][0]), (64, 256, 1.0), (320, 64, flags[0][2])):
            sums = ref[row : row + rows]
            lifted = jnp.dot(sums, lift_ref[...], preferred_element_type=jnp.float32)
            lifted = (lifted * (flag * other)).astype(jnp.bfloat16)
            edge_ref[edge, row : row + rows, lane : lane + 512] = lifted
    fill_leaf_mask([bricks_ref[i] for i in range(16)], leaf_mask_ref)
    for edge in range(2):
        for part in range(3):
            lanes = slice(part * 256, part * 256 + 256)
            edge_z_ref[edge, :, lanes] = z_neighbours(edge_ref[edge, :, lanes].astype(jnp.float32))
    sources, steps = [], []
    for edge in range(2):
        for window in range(2):
            sources.append((edge_ref.at[edge], edge_z_ref.at[edge], window * 256))
            steps.append(edge * 9 + window)
    taps = taps_ref[0].reshape(3072, 256)
    for step, total in zip(steps, leaf_sweep(sources, taps, 352)):
        masks = [leaf_mask_ref[(2 * step + half + 5) // 8, 16:368] for half in range(2)]
        values = (total * jnp.concatenate(masks, 1)).astype(jnp.bfloat16)
        one_ref[:, step * 256 : step * 256 + 256] = values
        one_z_ref[:, step * 256 : step * 256 + 256] = z_neighbours(values.astype(jnp.float32))
    for copy in early:
        copy.wait()

    @pl.loop(0, 2)
    def _(half_step):
        first = half_step * 5
        lanes = [pl.multiple_of((first + i) * 256, 256) for i in range(5)]
        taps = taps_ref[1].reshape(3072, 256)
        totals = leaf_sweep([(one_ref, one_z_ref, lane) for lane in lanes], taps, 320)
        merges, masks = [], []
        for window, total in enumerate(totals):
            step = first + window
            mask = leaf_mask_ref[(2 * step + 6) // 8, 32:352]
            values = (total * jnp.concatenate([mask, mask], 1)).astype(jnp.bfloat16)

            @pl.when((step >= 1) & (step < 9))
            def _():
                for half in range(2):
                    inner = values[32:288, half * 128 : half * 128 + 128]
                    features_ref[:, 2 * step - 2 + half] = inner.reshape(16, 16, 128)

            pairs = values.reshape(10, 2, 16, 256)
            halves = [pairs[:, a].reshape(160, 256) for a in range(2)]
            merges.append(jnp.concatenate(halves, 1))
            masks.append(mask.reshape(10, 2, 16, 128)[:, 0].reshape(160, 128))
        taps = down_leaf_vmem[...].reshape(512, 128)
        total = jnp.dot(jnp.concatenate(merges, 0), taps, preferred_element_type=jnp.float32)
        total = jnp.maximum(total, 0.0) * jnp.concatenate(masks, 0)
        for window in range(5):
            down = total[window * 160 : window * 160 + 160].astype(jnp.bfloat16)
            before, after = row_shifts(down.astype(jnp.float32), 16)
            here = pl.ds(pl.multiple_of((first + window) * 128, 128), 128)
            down_one_ref[0, :, here] = before.astype(jnp.bfloat16)
            down_one_ref[1, :, here] = down
            down_one_ref[2, :, here] = after.astype(jnp.bfloat16)

    for copy in copies:
        copy.wait()
    windows = []
    for y in range(8):
        windows.append(
            jnp.concatenate(
                [
                    down_one_ref[dz, dx * 16 : dx * 16 + 128, y * 128 : y * 128 + 384]
                    for dx in range(3)
                    for dz in range(3)
                ],
                1,
            )
        )
    taps = coarse_vmem[...].reshape(3456, 128)
    total = jnp.dot(jnp.concatenate(windows, 0), taps, preferred_element_type=jnp.float32)
    total = jnp.maximum(total, 0.0).reshape(8, 128, 128)
    masks = [leaf_mask_ref[1 + y // 4, 64:320].reshape(8, 2, 16, 128)[:, 0] for y in range(8)]
    level = total * jnp.concatenate(masks, 0).reshape(8, 128, 128)
    level = level.astype(jnp.bfloat16).reshape(4, 2, 4, 2, 16, 128)
    merged = jnp.concatenate(
        [level[:, b, :, a].reshape(256, 128) for a in range(2) for b in range(2)], 1
    )
    taps = down_vmem[...].reshape(512, 256)
    parts = jnp.dot(merged, taps, preferred_element_type=jnp.float32)
    parts_ref[0] = parts[:, :128]
    parts_ref[1] = parts[:, 128:]
    total = parts_ref[0, pl.ds(0, 128, stride=2)] + parts_ref[1, pl.ds(1, 128, stride=2)]
    tiles = [bricks_ref[(1 + y // 2) * 4 + 1 + x // 2] for y in range(4) for x in range(4)]
    mask = jnp.concatenate(tiles, 0)
    down_two_ref[...] = (jnp.maximum(total, 0.0) * mask).astype(jnp.bfloat16)


def border_part(low, high, north, south, lift_block, taps, bricks, one, one_z, down_leaf, coarse, down):
    return pl.pallas_call(
        border_kernel,
        out_shape=[
            jax.ShapeDtypeStruct((16, 16, 16, 128), jnp.bfloat16),
            jax.ShapeDtypeStruct((128, 128), jnp.bfloat16),
        ],
        in_specs=[pl.BlockSpec(memory_space=pltpu.VMEM)] * 7
        + [pl.BlockSpec(memory_space=pl.ANY)] * 3
        + [pl.BlockSpec(memory_space=pltpu.HBM)] * 2,
        scratch_shapes=[
            pltpu.VMEM((2, 384, 768), jnp.bfloat16),
            pltpu.VMEM((2, 384, 768), jnp.bfloat16),
            pltpu.VMEM((352, 2816), jnp.bfloat16),
            pltpu.VMEM((352, 2816), jnp.bfloat16),
            pltpu.VMEM((3, 160, 1280), jnp.bfloat16),
            pltpu.VMEM((2, 256, 128), jnp.float32),
            pltpu.VMEM((2, 2, 2, 64, 128), jnp.bfloat16),
            pltpu.VMEM((3, 3, 3, 128, 128), jnp.bfloat16),
            pltpu.VMEM((2, 2, 128, 256), jnp.bfloat16),
            pltpu.VMEM((4, 384, 128), jnp.float32),
            pltpu.SemaphoreType.DMA((2,)),
            pltpu.SemaphoreType.DMA,
            pltpu.SemaphoreType.DMA((3, 3)),
            pltpu.SemaphoreType.DMA((2, 2, 2)),
        ],
        compiler_params=pltpu.CompilerParams(vmem_limit_bytes=32 << 20),
        name="leaf_border",
    )(low, high, north, south, lift_block, taps, bricks, one, one_z, down_leaf, coarse, down)


def coarse_kernel(
    north_ref,
    middle_ref,
    south_ref,
    coarse_ref,
    down_ref,
    bricks_ref,
    top_ref,
    parts_ref,
):
    here_x = lax.axis_index("gx")
    here_y = lax.axis_index("gy")
    from_west = jnp.where(here_x > 0, 1.0, 0.0)
    from_east = jnp.where(here_x < lax.axis_size("gx") - 1, 1.0, 0.0)
    from_south = jnp.where(here_y > 0, 1.0, 0.0)
    from_north = jnp.where(here_y < lax.axis_size("gy") - 1, 1.0, 0.0)

    strips = []
    for ref, first, flag in ((south_ref, 1, from_south), (middle_ref, 0, 1.0), (north_ref, 0, from_north)):
        count = 4 if ref is middle_ref else 3
        tiles = [ref[i].astype(jnp.float32).reshape(4, 4, 8, 128) for i in (2, 1, 0)]
        tiles = [tile[first : first + count] for tile in tiles]
        tiles = [
            tiles[0][:, 1:] * (flag * from_west),
            tiles[1] * flag,
            tiles[2][:, :3] * (flag * from_east),
        ]
        strips.append(jnp.concatenate(tiles, 1))
    grid = jnp.concatenate(strips, 0)
    before, after = row_shifts(grid.reshape(800, 128), 8)
    grids = [before.reshape(10, 10, 8, 128), grid, after.reshape(10, 10, 8, 128)]
    pieces = [
        grids[dz][dy : dy + 8, dx : dx + 8].reshape(512, 128).astype(jnp.bfloat16)
        for dx in range(3)
        for dy in range(3)
        for dz in range(3)
    ]
    taps = coarse_ref[1].reshape(3456, 128)
    total = jnp.dot(jnp.concatenate(pieces, 1), taps, preferred_element_type=jnp.float32)
    tiles = [bricks_ref[y // 2 * 4 + x // 2] for y in range(8) for x in range(8)]
    mask = jnp.concatenate(tiles, 0)
    level = jnp.maximum(total, 0.0) * mask
    level = level.reshape(4, 2, 4, 2, 8, 128)
    merged = jnp.concatenate(
        [level[:, b, :, a].reshape(128, 128) for a in range(2) for b in range(2)], 1
    ).astype(jnp.bfloat16)
    taps = [
        jnp.concatenate([down_ref[1, a, b, c] for c in range(2)], 1)
        for a in range(2)
        for b in range(2)
    ]
    taps = jnp.concatenate(taps, 0)
    parts = jnp.dot(merged, taps, preferred_element_type=jnp.float32)
    parts_ref[0] = parts[:, :128]
    parts_ref[1] = parts[:, 128:]
    total = parts_ref[0, pl.ds(0, 64, stride=2)] + parts_ref[1, pl.ds(1, 64, stride=2)]
    picks = lax.broadcasted_iota(jnp.int32, (64, 128), 0) * 2
    picks = picks == lax.broadcasted_iota(jnp.int32, (64, 128), 1)
    picks = jnp.where(picks, 1.0, 0.0).astype(jnp.bfloat16)
    bricks = bricks_ref[...].reshape(128, 128).astype(jnp.bfloat16)
    mask = jnp.dot(picks, bricks, preferred_element_type=jnp.float32)
    down = jnp.maximum(total, 0.0) * mask
    down = down.astype(jnp.bfloat16).astype(jnp.float32)
    before, after = row_shifts(down, 4)
    shifted = [before, down, after]
    pieces = []
    for dx in range(3):
        for dy in range(3):
            for dz in range(3):
                turn = (64 - (dy - 1) * 16 - (dx - 1) * 4) % 64
                moved = pltpu.roll(shifted[dz], turn, 0) if turn else shifted[dz]
                pieces.append(moved.astype(jnp.bfloat16))
    taps = coarse_ref[2].reshape(3456, 128)
    total = jnp.dot(jnp.concatenate(pieces, 1), taps, preferred_element_type=jnp.float32)
    top = (jnp.maximum(total, 0.0) * mask).astype(jnp.bfloat16)
    for x in range(2):
        for y in range(2):
            row = (y + 1) * 16 + (x + 1) * 4
            top_ref[x, y] = top[row : row + 4]


def coarse_levels(north, middle, south, coarse, down, bricks):
    return pl.pallas_call(
        coarse_kernel,
        out_shape=jax.ShapeDtypeStruct((2, 2, 4, 128), jnp.bfloat16),
        in_specs=[pl.BlockSpec(memory_space=pltpu.VMEM)] * 6,
        scratch_shapes=[pltpu.VMEM((2, 128, 128), jnp.float32)],
        compiler_params=pltpu.CompilerParams(vmem_limit_bytes=16 << 20),
        name="coarse_levels",
    )(north, middle, south, coarse, down, bricks)


def ring(values, axis, step):
    count = lax.axis_size(axis)
    return lax.ppermute(values, axis, [(i, (i + step) % count) for i in range(count)])


def per_device(
    records, slot_voxels, brick_mask, lift_weight, leaf_convs, down_leaf, down_coarse, coarse_convs
):
    messages = pack_messages(records[0], slot_voxels[0], brick_mask)
    arrived = lax.all_to_all(messages, ("gx", "gy"), split_axis=0, concat_axis=0, tiled=True)
    lift_block = jnp.kron(jnp.eye(8, dtype=jnp.bfloat16), lift_weight)
    taps = leaf_taps(leaf_convs)
    arrived, lift_block, taps = lax.optimization_barrier((arrived, lift_block, taps))
    coarse_hbm = pltpu.with_memory_space_constraint(coarse_convs, pltpu.HBM)
    down_hbm = pltpu.with_memory_space_constraint(down_coarse, pltpu.HBM)

    coarse, fine, low_x, high_x, low_y, high_y = scatter(arrived)
    west = ring(high_x, "gx", 1)
    east = ring(low_x, "gx", -1)
    cells, own_z, bricks = own_part(coarse, fine, lift_block, arrived)
    west, east, own_z = lax.optimization_barrier((west, east, own_z))
    north = ring(jnp.concatenate([west[:, :256], low_y, east[:, :256]], 0), "gy", -1)
    south = ring(jnp.concatenate([west[:, 768:], high_y, east[:, 768:]], 0), "gy", 1)
    one, one_z, low, high = middle_part(cells, west, east, lift_block, taps, own_z, bricks)
    features, down_two = border_part(
        low,
        high,
        north,
        south,
        lift_block,
        taps,
        bricks,
        one,
        one_z,
        down_leaf,
        coarse_hbm,
        down_hbm,
    )
    west = ring(down_two, "gx", 1)
    east = ring(down_two, "gx", -1)
    middle = jnp.stack([east, down_two, west])
    south = ring(middle, "gy", 1)
    north = ring(middle, "gy", -1)
    top = coarse_levels(north, middle, south, coarse_convs, down_coarse, bricks)
    return (features, top)


def solution(mesh):
    in_specs = (
        P(("gx", "gy"), None, None, None),
        P(("gx", "gy"), None, None),
        P("gx", "gy", None),
        P(),
        P(),
        P(),
        P(),
        P(),
    )
    out_specs = (P("gx", "gy", None, None), P("gx", "gy", None, None))
    return jax.shard_map(
        per_device, mesh=mesh, in_specs=in_specs, out_specs=out_specs, check_vma=False
    )
```

```python
import functools

import jax
import jax.numpy as jnp
from jax import lax
from jax.experimental import pallas as pl
from jax.experimental.pallas import tpu as pltpu
from jax.sharding import PartitionSpec as P

BRICK = 8
BUCKETS = 64


def pack_kernel(records_ref, slots_ref, bricks_ref, messages_ref, buffer_ref, in_sem, out_sem):
    buckets = slots_ref.shape[0]
    chunk = buckets // 4
    incoming, outgoing = [], []
    for part in range(4):
        here = slice(part * chunk, part * chunk + chunk)
        incoming.append(
            pltpu.make_async_copy(records_ref.at[here], buffer_ref.at[here, 0:64], in_sem.at[part])
        )
        outgoing.append(
            pltpu.make_async_copy(buffer_ref.at[here], messages_ref.at[here], out_sem.at[part])
        )
    for copy in incoming:
        copy.start()
    side = lax.rem(lax.axis_index("gy"), 2)
    slot = lax.broadcasted_iota(jnp.int32, (256, 128), 0)
    lane = lax.broadcasted_iota(jnp.int32, (256, 128), 1)
    picks = jnp.where((slot >> 2) + side * 64 == lane, 1.0, 0.0).astype(jnp.bfloat16)
    level = lax.broadcasted_iota(jnp.int32, (8, 128), 0) // 2
    place = lax.broadcasted_iota(jnp.int32, (8, 128), 1) - (1 - side) * 64
    bricks = jnp.zeros((8, 128), jnp.int32)
    for column in range(4):
        for z in range(4):
            here = (level == z) & (place >= column * 16) & (place < column * 16 + 16)
            bricks = jnp.where(here, bricks_ref[column // 2, column % 2, z], bricks)
    bricks = jnp.broadcast_to(bricks.astype(jnp.float32)[None], (chunk, 8, 128))
    shape = (chunk, 8, 256)
    row = lax.broadcasted_iota(jnp.int32, shape, 1)
    mine = (lax.broadcasted_iota(jnp.int32, shape, 2) & 3) == (row & 3)

    for part in range(4):
        here = slice(part * chunk, part * chunk + chunk)
        slots = slots_ref[here]
        high = (slots >> 9) * 16 + ((slots & 31) >> 1)
        low = ((slots >> 5) & 15) * 2 + (slots & 1)
        both = jnp.where(
            row < 4,
            jnp.broadcast_to(high.reshape(chunk, 1, 256), shape),
            jnp.broadcast_to(low.reshape(chunk, 1, 256), shape),
        )
        both = jnp.where(mine, both, 0).astype(jnp.float32)
        both = both.reshape(chunk * 8, 256).astype(jnp.bfloat16)
        ids = jnp.dot(both, picks, preferred_element_type=jnp.float32)
        buffer_ref[here, 64:72] = (ids.reshape(chunk, 8, 128) + bricks).astype(jnp.bfloat16)
        incoming[part].wait()
        outgoing[part].start()
    for copy in outgoing:
        copy.wait()


def pack_messages(records, slot_voxels, brick_mask):
    buckets, rows, width = records.shape
    return pl.pallas_call(
        pack_kernel,
        in_specs=[
            pl.BlockSpec(memory_space=pltpu.HBM),
            pl.BlockSpec(memory_space=pltpu.VMEM),
            pl.BlockSpec(memory_space=pltpu.SMEM),
        ],
        out_specs=pl.BlockSpec(memory_space=pltpu.HBM),
        out_shape=jax.ShapeDtypeStruct((buckets, rows + 8, width), jnp.bfloat16),
        scratch_shapes=[
            pltpu.VMEM((buckets, rows + 8, width), jnp.bfloat16),
            pltpu.SemaphoreType.DMA((4,)),
            pltpu.SemaphoreType.DMA((4,)),
        ],
        name="pack",
    )(records, slot_voxels, brick_mask)


def scatter_kernel(
    msg_ref, coarse_ref, fine_ref, west_ref, east_ref, south_ref, north_ref, total_ref
):
    total_ref[...] = jnp.zeros_like(total_ref)
    wide = 256
    lanes = lax.broadcasted_iota(jnp.int32, (wide, wide), 0).astype(jnp.bfloat16)
    zero = jnp.zeros((32, wide), jnp.bfloat16)
    left = lax.broadcasted_iota(jnp.int32, (8, 128), 1) < 64
    @pl.loop(0, msg_ref.shape[0] // BUCKETS)
    def _(step):
        for quad in range(BUCKETS // 4):
            turned, ids = [], []
            for pair in range(2):
                first = step * BUCKETS + quad * 4 + pair * 2
                rows = jnp.concatenate([msg_ref[first, 0:64], msg_ref[first + 1, 0:64]], 0)
                turned.append(jnp.transpose(rows))
                ids.append(
                    jnp.where(
                        left,
                        msg_ref[first, 64:72].astype(jnp.float32),
                        msg_ref[first + 1, 64:72].astype(jnp.float32),
                    )
                )
            turned = jnp.concatenate(turned, 1)
            ids = jnp.concatenate(ids, 1)
            for base in (0, 2):
                spreads, hots = [], []
                for quarter in (base, base + 1):
                    features = turned[quarter * 32 : quarter * 32 + 32]
                    high = jnp.broadcast_to(ids[quarter : quarter + 1], (wide, wide))
                    low = jnp.broadcast_to(ids[quarter + 4 : quarter + 5], (32, wide))
                    high, low = high.astype(jnp.bfloat16), low.astype(jnp.bfloat16)
                    hots.append(jnp.where(lanes == high, 1.0, 0.0).astype(jnp.bfloat16))
                    spreads += [
                        jnp.concatenate(
                            [jnp.where(low == jnp.bfloat16(i), features, zero) for i in range(32)], 0
                        )
                    ]
                total_ref[...] += lax.dot_general(
                    jnp.concatenate(spreads, 1),
                    jnp.concatenate(hots, 1),
                    (((1,), (1,)), ((), ())),
                    preferred_element_type=jnp.float32,
                )

    for part in range(4):
        summed = jnp.transpose(total_ref[part * wide : part * wide + wide])
        coarse = summed.astype(jnp.bfloat16)
        lanes = slice(part * wide, part * wide + wide)
        coarse_ref[:, lanes] = coarse
        fine_ref[:, lanes] = (summed - coarse.astype(jnp.float32)).astype(jnp.bfloat16)
        west_ref[:, lanes] = coarse[:64]
        east_ref[:, lanes] = coarse[192:]
        if part == 0:
            south_ref[...] = coarse
        if part == 3:
            north_ref[...] = coarse


def scatter(messages):
    shapes = [(256, 1024)] * 2 + [(64, 1024)] * 2 + [(256, 256)] * 2
    return pl.pallas_call(
        scatter_kernel,
        in_specs=[pl.BlockSpec(memory_space=pltpu.VMEM)],
        out_specs=[pl.BlockSpec(memory_space=pltpu.VMEM)] * 6,
        out_shape=[jax.ShapeDtypeStruct(shape, jnp.bfloat16) for shape in shapes],
        scratch_shapes=[pltpu.VMEM((1024, 256), jnp.float32)],
        compiler_params=pltpu.CompilerParams(vmem_limit_bytes=14 << 20),
        name="scatter",
    )(messages)


def leaf_taps_kernel(convs_ref, taps_ref):
    zero = jnp.zeros((64, 64), jnp.bfloat16)
    for layer in range(2):
        for dx in range(3):
            for kind in range(2):
                for step_y in range(4):
                    for half in range(2):
                        row = kind * 512 + step_y * 128 + half * 64
                        for out_y in range(2):
                            blocks = []
                            for out_z in range(2):
                                dy = step_y - out_y
                                if kind == 0:
                                    dz = half - out_z + 1
                                else:
                                    dz = 3 - out_z if half == 0 else -out_z
                                inside = 0 <= dy <= 2 and 0 <= dz <= 2
                                blocks.append(convs_ref[layer, dx, dy, dz] if inside else zero)
                            taps_ref[layer, dx, row : row + 64, out_y * 128 : out_y * 128 + 128] = (
                                jnp.concatenate(blocks, 1)
                            )


def leaf_taps(leaf_convs):
    return pl.pallas_call(
        leaf_taps_kernel,
        out_shape=jax.ShapeDtypeStruct((2, 3, 1024, 256), jnp.bfloat16),
        name="leaf_taps",
    )(leaf_convs)


def row_shifts(values, period):
    count = values.shape[0]
    place = lax.rem(lax.broadcasted_iota(jnp.int32, values.shape, 0), period)
    before = jnp.where(place == 0, 0.0, pltpu.roll(values, 1, 0))
    after = jnp.where(place == period - 1, 0.0, pltpu.roll(values, count - 1, 0))
    return before, after


def z_neighbours(values):
    before, after = row_shifts(values, 16)
    lane = lax.rem(lax.broadcasted_iota(jnp.int32, values.shape, 1), 128)
    return jnp.where(lane < 64, after, before).astype(jnp.bfloat16)


def spread_bricks(near, flags):
    side = lax.rem(lax.axis_index("gy"), 2)
    columns = []
    for y in range(4):
        for x in range(4):
            source_x, source_y = (0, 1, 1, 2)[x], (0, 1, 1, 2)[y]
            lane = ((1, 0, 1, 0)[x] * 2 + (1, 0, 1, 0)[y]) * 16
            tile = near[source_x * 3 + source_y].astype(jnp.float32)
            upper = side == 0 if source_y == 1 else side == 1
            value = jnp.where(upper, tile[:, 64 + lane : 65 + lane], tile[:, lane : lane + 1])
            flag = flags[0][source_x] * flags[1][source_y]
            columns.append(jnp.broadcast_to(value, (8, 128)) * flag)
    return columns


def doubled(column):
    level = lax.broadcasted_iota(jnp.int32, (16, 128), 0) // 4
    tile = jnp.broadcast_to(column[0:1], (16, 128))
    for z in range(1, 4):
        tile = jnp.where(level == z, jnp.broadcast_to(column[2 * z : 2 * z + 1], (16, 128)), tile)
    return tile


def grid_flags():
    here_x, here_y = lax.axis_index("gx"), lax.axis_index("gy")
    last_x, last_y = lax.axis_size("gx") - 1, lax.axis_size("gy") - 1
    return (
        (jnp.where(here_x > 0, 1.0, 0.0), 1.0, jnp.where(here_x < last_x, 1.0, 0.0)),
        (jnp.where(here_y > 0, 1.0, 0.0), 1.0, jnp.where(here_y < last_y, 1.0, 0.0)),
    )


def fill_leaf_mask(columns, leaf_mask_ref):
    for y in range(4):
        for x in range(4):
            tile = doubled(columns[y * 4 + x])
            for place_x in range(*((0, 4), (4, 12), (12, 20), (20, 24))[x]):
                leaf_mask_ref[y, place_x * 16 : place_x * 16 + 16] = tile


def leaf_sweep(sources, taps, rows):
    windows = []
    for source_ref, source_z_ref, lane in sources:
        pieces = []
        for dx in range(3):
            pieces.append(source_ref[dx * 16 : dx * 16 + rows, pl.ds(lane, 512)])
            pieces.append(source_z_ref[dx * 16 : dx * 16 + rows, pl.ds(lane, 512)])
        windows.append(jnp.concatenate(pieces, 1))
    total = jnp.dot(jnp.concatenate(windows, 0), taps, preferred_element_type=jnp.float32)
    total = jnp.maximum(total, 0.0)
    return [total[i * rows : i * rows + rows] for i in range(len(sources))]


def own_kernel(
    coarse_ref,
    fine_ref,
    lift_ref,
    arrived_ref,
    cells_ref,
    cell_z_ref,
    bricks_ref,
    near_vmem,
    near_sem,
):
    last_x, last_y = lax.axis_size("gx") - 1, lax.axis_size("gy") - 1
    copies = []
    for x in range(3):
        for y in range(3):
            source = jnp.clip(lax.axis_index("gx") + x - 1, 0, last_x) * (last_y + 1)
            source = source + jnp.clip(lax.axis_index("gy") + y - 1, 0, last_y)
            copies.append(
                pltpu.make_async_copy(
                    arrived_ref.at[source, 64:72], near_vmem.at[x * 3 + y], near_sem.at[x, y]
                )
            )
    for copy in copies:
        copy.start()

    @pl.loop(0, 4)
    def _(part):
        sums = pl.ds(pl.multiple_of(part * 256, 256), 256)
        lanes = pl.ds(pl.multiple_of(part * 512, 512), 512)
        lifted = jnp.dot(coarse_ref[:, sums], lift_ref[...], preferred_element_type=jnp.float32)
        lifted += jnp.dot(fine_ref[:, sums], lift_ref[...], preferred_element_type=jnp.float32)
        cells = lifted.astype(jnp.bfloat16)
        cells_ref[:, lanes] = cells
        cell_z_ref[:, lanes] = z_neighbours(cells.astype(jnp.float32))

    for copy in copies:
        copy.wait()
    for index, column in enumerate(spread_bricks([near_vmem[i] for i in range(9)], grid_flags())):
        bricks_ref[index] = column


def own_part(coarse, fine, lift_block, arrived):
    return pl.pallas_call(
        own_kernel,
        out_shape=[
            jax.ShapeDtypeStruct((256, 2048), jnp.bfloat16),
            jax.ShapeDtypeStruct((256, 2048), jnp.bfloat16),
            jax.ShapeDtypeStruct((16, 8, 128), jnp.float32),
        ],
        in_specs=[pl.BlockSpec(memory_space=pltpu.VMEM)] * 3
        + [pl.BlockSpec(memory_space=pl.ANY)],
        out_specs=[pl.BlockSpec(memory_space=pltpu.VMEM)] * 3,
        scratch_shapes=[
            pltpu.VMEM((9, 8, 128), jnp.bfloat16),
            pltpu.SemaphoreType.DMA((3, 3)),
        ],
        compiler_params=pltpu.CompilerParams(vmem_limit_bytes=8 << 20),
        name="leaf_own",
    )(coarse, fine, lift_block, arrived)


def middle_kernel(
    cells_ref,
    west_ref,
    east_ref,
    lift_ref,
    taps_ref,
    own_z_ref,
    bricks_ref,
    one_ref,
    one_z_ref,
    low_ref,
    high_ref,
    cell_ref,
    cell_z_ref,
    leaf_mask_ref,
):
    flags = grid_flags()
    cell_ref[64:320] = cells_ref[...]
    for part in range(4):
        for row, ref, flag in ((0, west_ref, flags[0][0]), (320, east_ref, flags[0][2])):
            sums = ref[:, part * 256 : part * 256 + 256]
            lifted = jnp.dot(sums, lift_ref[...], preferred_element_type=jnp.float32) * flag
            cell_ref[row : row + 64, part * 512 : part * 512 + 512] = lifted.astype(jnp.bfloat16)
    low_ref[...] = cell_ref[:, :256]
    high_ref[...] = cell_ref[:, 1792:]

    cell_z_ref[64:320] = own_z_ref[...]
    for row in (0, 320):
        for part in range(4):
            lanes = slice(part * 512, part * 512 + 512)
            halo = cell_ref[row : row + 64, lanes].astype(jnp.float32)
            cell_z_ref[row : row + 64, lanes] = z_neighbours(halo)
    fill_leaf_mask([bricks_ref[i] for i in range(16)], leaf_mask_ref)
    taps = taps_ref[0].reshape(3072, 256)
    for first, count in ((0, 4), (4, 3)):
        sources = [(cell_ref, cell_z_ref, (first + i) * 256) for i in range(count)]
        for window, total in enumerate(leaf_sweep(sources, taps, 352)):
            step = first + window
            masks = [leaf_mask_ref[(2 * step + half + 9) // 8, 16:368] for half in range(2)]
            values = (total * jnp.concatenate(masks, 1)).astype(jnp.bfloat16)
            one_ref[:, step * 256 : step * 256 + 256] = values
            one_z_ref[:, step * 256 : step * 256 + 256] = z_neighbours(values.astype(jnp.float32))


def middle_part(cells, west, east, lift_block, taps, own_z, bricks):
    return pl.pallas_call(
        middle_kernel,
        out_shape=[
            jax.ShapeDtypeStruct((352, 1792), jnp.bfloat16),
            jax.ShapeDtypeStruct((352, 1792), jnp.bfloat16),
            jax.ShapeDtypeStruct((384, 256), jnp.bfloat16),
            jax.ShapeDtypeStruct((384, 256), jnp.bfloat16),
        ],
        in_specs=[pl.BlockSpec(memory_space=pltpu.VMEM)] * 7,
        out_specs=[pl.BlockSpec(memory_space=pltpu.VMEM)] * 4,
        scratch_shapes=[
            pltpu.VMEM((384, 2048), jnp.bfloat16),
            pltpu.VMEM((384, 2048), jnp.bfloat16),
            pltpu.VMEM((4, 384, 128), jnp.float32),
        ],
        compiler_params=pltpu.CompilerParams(vmem_limit_bytes=24 << 20),
        name="leaf_middle",
    )(cells, west, east, lift_block, taps, own_z, bricks)


def border_kernel(
    low_ref,
    high_ref,
    north_ref,
    south_ref,
    lift_ref,
    taps_ref,
    bricks_ref,
    one_middle_ref,
    one_z_middle_ref,
    down_leaf_ref,
    coarse_ref,
    down_ref,
    features_ref,
    down_two_ref,
    edge_ref,
    edge_z_ref,
    one_ref,
    one_z_ref,
    down_one_ref,
    parts_ref,
    down_leaf_vmem,
    coarse_vmem,
    down_vmem,
    leaf_mask_ref,
    one_sem,
    leaf_sem,
    coarse_sem,
    down_sem,
):
    early = [
        pltpu.make_async_copy(one_middle_ref, one_ref.at[:, 512:2304], one_sem.at[0]),
        pltpu.make_async_copy(one_z_middle_ref, one_z_ref.at[:, 512:2304], one_sem.at[1]),
        pltpu.make_async_copy(down_leaf_ref, down_leaf_vmem, leaf_sem),
    ]
    copies = [
        pltpu.make_async_copy(coarse_ref.at[0], coarse_vmem, coarse_sem),
        pltpu.make_async_copy(down_ref.at[0], down_vmem, down_sem),
    ]
    for copy in early + copies:
        copy.start()
    flags = grid_flags()
    edge_ref[0, :, 512:768] = low_ref[...]
    edge_ref[1, :, 0:256] = high_ref[...]
    for edge, lane, ref, flag in ((0, 0, south_ref, flags[1][0]), (1, 256, north_ref, flags[1][2])):
        for row, rows, other in ((0, 64, flags[0][0]), (64, 256, 1.0), (320, 64, flags[0][2])):
            sums = ref[row : row + rows]
            lifted = jnp.dot(sums, lift_ref[...], preferred_element_type=jnp.float32)
            lifted = (lifted * (flag * other)).astype(jnp.bfloat16)
            edge_ref[edge, row : row + rows, lane : lane + 512] = lifted
    fill_leaf_mask([bricks_ref[i] for i in range(16)], leaf_mask_ref)
    for edge in range(2):
        for part in range(3):
            lanes = slice(part * 256, part * 256 + 256)
            edge_z_ref[edge, :, lanes] = z_neighbours(edge_ref[edge, :, lanes].astype(jnp.float32))
    sources, steps = [], []
    for edge in range(2):
        for window in range(2):
            sources.append((edge_ref.at[edge], edge_z_ref.at[edge], window * 256))
            steps.append(edge * 9 + window)
    taps = taps_ref[0].reshape(3072, 256)
    for step, total in zip(steps, leaf_sweep(sources, taps, 352)):
        masks = [leaf_mask_ref[(2 * step + half + 5) // 8, 16:368] for half in range(2)]
        values = (total * jnp.concatenate(masks, 1)).astype(jnp.bfloat16)
        one_ref[:, step * 256 : step * 256 + 256] = values
        one_z_ref[:, step * 256 : step * 256 + 256] = z_neighbours(values.astype(jnp.float32))
    for copy in early:
        copy.wait()

    @pl.loop(0, 2)
    def _(half_step):
        first = half_step * 5
        lanes = [pl.multiple_of((first + i) * 256, 256) for i in range(5)]
        taps = taps_ref[1].reshape(3072, 256)
        totals = leaf_sweep([(one_ref, one_z_ref, lane) for lane in lanes], taps, 320)
        merges, masks = [], []
        for window, total in enumerate(totals):
            step = first + window
            mask = leaf_mask_ref[(2 * step + 6) // 8, 32:352]
            values = (total * jnp.concatenate([mask, mask], 1)).astype(jnp.bfloat16)

            @pl.when((step >= 1) & (step < 9))
            def _():
                for half in range(2):
                    inner = values[32:288, half * 128 : half * 128 + 128]
                    features_ref[:, 2 * step - 2 + half] = inner.reshape(16, 16, 128)

            pairs = values.reshape(10, 2, 16, 256)
            halves = [pairs[:, a].reshape(160, 256) for a in range(2)]
            merges.append(jnp.concatenate(halves, 1))
            masks.append(mask.reshape(10, 2, 16, 128)[:, 0].reshape(160, 128))
        taps = down_leaf_vmem[...].reshape(512, 128)
        total = jnp.dot(jnp.concatenate(merges, 0), taps, preferred_element_type=jnp.float32)
        total = jnp.maximum(total, 0.0) * jnp.concatenate(masks, 0)
        for window in range(5):
            down = total[window * 160 : window * 160 + 160].astype(jnp.bfloat16)
            before, after = row_shifts(down.astype(jnp.float32), 16)
            here = pl.ds(pl.multiple_of((first + window) * 128, 128), 128)
            down_one_ref[0, :, here] = before.astype(jnp.bfloat16)
            down_one_ref[1, :, here] = down
            down_one_ref[2, :, here] = after.astype(jnp.bfloat16)

    for copy in copies:
        copy.wait()
    windows = []
    for y in range(8):
        windows.append(
            jnp.concatenate(
                [
                    down_one_ref[dz, dx * 16 : dx * 16 + 128, y * 128 : y * 128 + 384]
                    for dx in range(3)
                    for dz in range(3)
                ],
                1,
            )
        )
    taps = [coarse_vmem[dx, :, dz].reshape(384, 128) for dx in range(3) for dz in range(3)]
    taps = jnp.concatenate(taps, 0)
    total = jnp.dot(jnp.concatenate(windows, 0), taps, preferred_element_type=jnp.float32)
    total = jnp.maximum(total, 0.0).reshape(8, 128, 128)
    masks = [leaf_mask_ref[1 + y // 4, 64:320].reshape(8, 2, 16, 128)[:, 0] for y in range(8)]
    level = total * jnp.concatenate(masks, 0).reshape(8, 128, 128)
    level = level.astype(jnp.bfloat16).reshape(4, 2, 4, 2, 16, 128)
    merged = jnp.concatenate(
        [level[:, b, :, a].reshape(256, 128) for a in range(2) for b in range(2)], 1
    )
    taps = [
        jnp.concatenate([down_vmem[a, b, c] for c in range(2)], 1)
        for a in range(2)
        for b in range(2)
    ]
    taps = jnp.concatenate(taps, 0)
    parts = jnp.dot(merged, taps, preferred_element_type=jnp.float32)
    parts_ref[0] = parts[:, :128]
    parts_ref[1] = parts[:, 128:]
    total = parts_ref[0, pl.ds(0, 128, stride=2)] + parts_ref[1, pl.ds(1, 128, stride=2)]
    tiles = [bricks_ref[(1 + y // 2) * 4 + 1 + x // 2] for y in range(4) for x in range(4)]
    mask = jnp.concatenate(tiles, 0)
    down_two_ref[...] = (jnp.maximum(total, 0.0) * mask).astype(jnp.bfloat16)


def border_part(low, high, north, south, lift_block, taps, bricks, one, one_z, down_leaf, coarse, down):
    return pl.pallas_call(
        border_kernel,
        out_shape=[
            jax.ShapeDtypeStruct((16, 16, 16, 128), jnp.bfloat16),
            jax.ShapeDtypeStruct((128, 128), jnp.bfloat16),
        ],
        in_specs=[pl.BlockSpec(memory_space=pltpu.VMEM)] * 7
        + [pl.BlockSpec(memory_space=pl.ANY)] * 3
        + [pl.BlockSpec(memory_space=pltpu.HBM)] * 2,
        scratch_shapes=[
            pltpu.VMEM((2, 384, 768), jnp.bfloat16),
            pltpu.VMEM((2, 384, 768), jnp.bfloat16),
            pltpu.VMEM((352, 2816), jnp.bfloat16),
            pltpu.VMEM((352, 2816), jnp.bfloat16),
            pltpu.VMEM((3, 160, 1280), jnp.bfloat16),
            pltpu.VMEM((2, 256, 128), jnp.float32),
            pltpu.VMEM((2, 2, 2, 64, 128), jnp.bfloat16),
            pltpu.VMEM((3, 3, 3, 128, 128), jnp.bfloat16),
            pltpu.VMEM((2, 2, 2, 128, 128), jnp.bfloat16),
            pltpu.VMEM((4, 384, 128), jnp.float32),
            pltpu.SemaphoreType.DMA((2,)),
            pltpu.SemaphoreType.DMA,
            pltpu.SemaphoreType.DMA,
            pltpu.SemaphoreType.DMA,
        ],
        compiler_params=pltpu.CompilerParams(vmem_limit_bytes=32 << 20),
        name="leaf_border",
    )(low, high, north, south, lift_block, taps, bricks, one, one_z, down_leaf, coarse, down)


def coarse_kernel(
    north_ref,
    middle_ref,
    south_ref,
    coarse_ref,
    down_ref,
    bricks_ref,
    top_ref,
    parts_ref,
):
    here_x = lax.axis_index("gx")
    here_y = lax.axis_index("gy")
    from_west = jnp.where(here_x > 0, 1.0, 0.0)
    from_east = jnp.where(here_x < lax.axis_size("gx") - 1, 1.0, 0.0)
    from_south = jnp.where(here_y > 0, 1.0, 0.0)
    from_north = jnp.where(here_y < lax.axis_size("gy") - 1, 1.0, 0.0)

    strips = []
    for ref, first, flag in ((south_ref, 1, from_south), (middle_ref, 0, 1.0), (north_ref, 0, from_north)):
        count = 4 if ref is middle_ref else 3
        tiles = [ref[i].astype(jnp.float32).reshape(4, 4, 8, 128) for i in (2, 1, 0)]
        tiles = [tile[first : first + count] for tile in tiles]
        tiles = [
            tiles[0][:, 1:] * (flag * from_west),
            tiles[1] * flag,
            tiles[2][:, :3] * (flag * from_east),
        ]
        strips.append(jnp.concatenate(tiles, 1))
    grid = jnp.concatenate(strips, 0)
    before, after = row_shifts(grid.reshape(800, 128), 8)
    grids = [before.reshape(10, 10, 8, 128), grid, after.reshape(10, 10, 8, 128)]
    pieces = [
        grids[dz][dy : dy + 8, dx : dx + 8].reshape(512, 128).astype(jnp.bfloat16)
        for dx in range(3)
        for dy in range(3)
        for dz in range(3)
    ]
    taps = coarse_ref[1].reshape(3456, 128)
    total = jnp.dot(jnp.concatenate(pieces, 1), taps, preferred_element_type=jnp.float32)
    tiles = [bricks_ref[y // 2 * 4 + x // 2] for y in range(8) for x in range(8)]
    mask = jnp.concatenate(tiles, 0)
    level = jnp.maximum(total, 0.0) * mask
    level = level.reshape(4, 2, 4, 2, 8, 128)
    merged = jnp.concatenate(
        [level[:, b, :, a].reshape(128, 128) for a in range(2) for b in range(2)], 1
    ).astype(jnp.bfloat16)
    taps = [
        jnp.concatenate([down_ref[1, a, b, c] for c in range(2)], 1)
        for a in range(2)
        for b in range(2)
    ]
    taps = jnp.concatenate(taps, 0)
    parts = jnp.dot(merged, taps, preferred_element_type=jnp.float32)
    parts_ref[0] = parts[:, :128]
    parts_ref[1] = parts[:, 128:]
    total = parts_ref[0, pl.ds(0, 64, stride=2)] + parts_ref[1, pl.ds(1, 64, stride=2)]
    picks = lax.broadcasted_iota(jnp.int32, (64, 128), 0) * 2
    picks = picks == lax.broadcasted_iota(jnp.int32, (64, 128), 1)
    picks = jnp.where(picks, 1.0, 0.0).astype(jnp.bfloat16)
    bricks = bricks_ref[...].reshape(128, 128).astype(jnp.bfloat16)
    mask = jnp.dot(picks, bricks, preferred_element_type=jnp.float32)
    down = jnp.maximum(total, 0.0) * mask
    down = down.astype(jnp.bfloat16).astype(jnp.float32)
    before, after = row_shifts(down, 4)
    shifted = [before, down, after]
    pieces = []
    for dx in range(3):
        for dy in range(3):
            for dz in range(3):
                turn = (64 - (dy - 1) * 16 - (dx - 1) * 4) % 64
                moved = pltpu.roll(shifted[dz], turn, 0) if turn else shifted[dz]
                pieces.append(moved.astype(jnp.bfloat16))
    taps = coarse_ref[2].reshape(3456, 128)
    total = jnp.dot(jnp.concatenate(pieces, 1), taps, preferred_element_type=jnp.float32)
    top = (jnp.maximum(total, 0.0) * mask).astype(jnp.bfloat16)
    for x in range(2):
        for y in range(2):
            row = (y + 1) * 16 + (x + 1) * 4
            top_ref[x, y] = top[row : row + 4]


def coarse_levels(north, middle, south, coarse, down, bricks):
    return pl.pallas_call(
        coarse_kernel,
        out_shape=jax.ShapeDtypeStruct((2, 2, 4, 128), jnp.bfloat16),
        in_specs=[pl.BlockSpec(memory_space=pltpu.VMEM)] * 6,
        scratch_shapes=[pltpu.VMEM((2, 128, 128), jnp.float32)],
        compiler_params=pltpu.CompilerParams(vmem_limit_bytes=16 << 20),
        name="coarse_levels",
    )(north, middle, south, coarse, down, bricks)


def ring(values, axis, step):
    count = lax.axis_size(axis)
    return lax.ppermute(values, axis, [(i, (i + step) % count) for i in range(count)])


def per_device(
    records, slot_voxels, brick_mask, lift_weight, leaf_convs, down_leaf, down_coarse, coarse_convs
):
    messages = pack_messages(records[0], slot_voxels[0], brick_mask)
    arrived = lax.all_to_all(messages, ("gx", "gy"), split_axis=0, concat_axis=0, tiled=True)
    lift_block = jnp.kron(jnp.eye(8, dtype=jnp.bfloat16), lift_weight)
    taps = leaf_taps(leaf_convs)
    arrived, lift_block, taps = lax.optimization_barrier((arrived, lift_block, taps))
    coarse_hbm = pltpu.with_memory_space_constraint(coarse_convs, pltpu.HBM)
    down_hbm = pltpu.with_memory_space_constraint(down_coarse, pltpu.HBM)

    coarse, fine, low_x, high_x, low_y, high_y = scatter(arrived)
    west = ring(high_x, "gx", 1)
    east = ring(low_x, "gx", -1)
    cells, own_z, bricks = own_part(coarse, fine, lift_block, arrived)
    west, east, own_z = lax.optimization_barrier((west, east, own_z))
    north = ring(jnp.concatenate([west[:, :256], low_y, east[:, :256]], 0), "gy", -1)
    south = ring(jnp.concatenate([west[:, 768:], high_y, east[:, 768:]], 0), "gy", 1)
    one, one_z, low, high = middle_part(cells, west, east, lift_block, taps, own_z, bricks)
    features, down_two = border_part(
        low,
        high,
        north,
        south,
        lift_block,
        taps,
        bricks,
        one,
        one_z,
        down_leaf,
        coarse_hbm,
        down_hbm,
    )
    west = ring(down_two, "gx", 1)
    east = ring(down_two, "gx", -1)
    middle = jnp.stack([east, down_two, west])
    south = ring(middle, "gy", 1)
    north = ring(middle, "gy", -1)
    top = coarse_levels(north, middle, south, coarse_convs, down_coarse, bricks)
    return (features, top)


def solution(mesh):
    in_specs = (
        P(("gx", "gy"), None, None, None),
        P(("gx", "gy"), None, None),
        P("gx", "gy", None),
        P(),
        P(),
        P(),
        P(),
        P(),
    )
    out_specs = (P("gx", "gy", None, None), P("gx", "gy", None, None))
    return jax.shard_map(
        per_device, mesh=mesh, in_specs=in_specs, out_specs=out_specs, check_vma=False
    )
```

```python
import functools

import jax
import jax.numpy as jnp
from jax import lax
from jax.experimental import pallas as pl
from jax.experimental.pallas import tpu as pltpu
from jax.sharding import PartitionSpec as P

BRICK = 8
BUCKETS = 64


def pack_kernel(records_ref, slots_ref, bricks_ref, messages_ref, buffer_ref, in_sem, out_sem):
    buckets = slots_ref.shape[0]
    chunk = buckets // 4
    incoming, outgoing = [], []
    for part in range(4):
        here = slice(part * chunk, part * chunk + chunk)
        incoming.append(
            pltpu.make_async_copy(records_ref.at[here], buffer_ref.at[here, 0:64], in_sem.at[part])
        )
        outgoing.append(
            pltpu.make_async_copy(buffer_ref.at[here], messages_ref.at[here], out_sem.at[part])
        )
    for copy in incoming:
        copy.start()
    side = lax.rem(lax.axis_index("gy"), 2)
    slot = lax.broadcasted_iota(jnp.int32, (256, 128), 0)
    lane = lax.broadcasted_iota(jnp.int32, (256, 128), 1)
    picks = jnp.where((slot >> 2) + side * 64 == lane, 1.0, 0.0).astype(jnp.bfloat16)
    level = lax.broadcasted_iota(jnp.int32, (8, 128), 0) // 2
    place = lax.broadcasted_iota(jnp.int32, (8, 128), 1) - (1 - side) * 64
    bricks = jnp.zeros((8, 128), jnp.int32)
    for column in range(4):
        for z in range(4):
            here = (level == z) & (place >= column * 16) & (place < column * 16 + 16)
            bricks = jnp.where(here, bricks_ref[column // 2, column % 2, z], bricks)
    bricks = jnp.broadcast_to(bricks.astype(jnp.float32)[None], (chunk, 8, 128))
    shape = (chunk, 8, 256)
    row = lax.broadcasted_iota(jnp.int32, shape, 1)
    mine = (lax.broadcasted_iota(jnp.int32, shape, 2) & 3) == (row & 3)

    for part in range(4):
        here = slice(part * chunk, part * chunk + chunk)
        slots = slots_ref[here]
        high = (slots >> 9) * 16 + ((slots & 31) >> 1)
        low = ((slots >> 5) & 15) * 2 + (slots & 1)
        both = jnp.where(
            row < 4,
            jnp.broadcast_to(high.reshape(chunk, 1, 256), shape),
            jnp.broadcast_to(low.reshape(chunk, 1, 256), shape),
        )
        both = jnp.where(mine, both, 0).astype(jnp.float32)
        both = both.reshape(chunk * 8, 256).astype(jnp.bfloat16)
        ids = jnp.dot(both, picks, preferred_element_type=jnp.float32)
        buffer_ref[here, 64:72] = (ids.reshape(chunk, 8, 128) + bricks).astype(jnp.bfloat16)
        incoming[part].wait()
        outgoing[part].start()
    for copy in outgoing:
        copy.wait()


def pack_messages(records, slot_voxels, brick_mask):
    buckets, rows, width = records.shape
    return pl.pallas_call(
        pack_kernel,
        in_specs=[
            pl.BlockSpec(memory_space=pltpu.HBM),
            pl.BlockSpec(memory_space=pltpu.VMEM),
            pl.BlockSpec(memory_space=pltpu.SMEM),
        ],
        out_specs=pl.BlockSpec(memory_space=pltpu.HBM),
        out_shape=jax.ShapeDtypeStruct((buckets, rows + 8, width), jnp.bfloat16),
        scratch_shapes=[
            pltpu.VMEM((buckets, rows + 8, width), jnp.bfloat16),
            pltpu.SemaphoreType.DMA((4,)),
            pltpu.SemaphoreType.DMA((4,)),
        ],
        name="pack",
    )(records, slot_voxels, brick_mask)


def scatter_kernel(
    msg_ref, coarse_ref, fine_ref, west_ref, east_ref, south_ref, north_ref, total_ref
):
    step = pl.program_id(0)

    @pl.when(step == 0)
    def _():
        total_ref[...] = jnp.zeros_like(total_ref)

    wide = 256
    lanes = lax.broadcasted_iota(jnp.int32, (wide, wide), 0).astype(jnp.bfloat16)
    zero = jnp.zeros((32, wide), jnp.bfloat16)
    left = lax.broadcasted_iota(jnp.int32, (8, 128), 1) < 64
    for quad in range(BUCKETS // 4):
        turned, ids = [], []
        for pair in range(2):
            first = quad * 4 + pair * 2
            rows = jnp.concatenate([msg_ref[first, 0:64], msg_ref[first + 1, 0:64]], 0)
            turned.append(jnp.transpose(rows))
            ids.append(
                jnp.where(
                    left,
                    msg_ref[first, 64:72].astype(jnp.float32),
                    msg_ref[first + 1, 64:72].astype(jnp.float32),
                )
            )
        turned = jnp.concatenate(turned, 1)
        ids = jnp.concatenate(ids, 1)
        for base in (0, 2):
            spreads, hots = [], []
            for quarter in (base, base + 1):
                features = turned[quarter * 32 : quarter * 32 + 32]
                high = jnp.broadcast_to(ids[quarter : quarter + 1], (wide, wide))
                low = jnp.broadcast_to(ids[quarter + 4 : quarter + 5], (32, wide))
                high, low = high.astype(jnp.bfloat16), low.astype(jnp.bfloat16)
                hots.append(jnp.where(lanes == high, 1.0, 0.0).astype(jnp.bfloat16))
                spreads += [
                    jnp.concatenate(
                        [jnp.where(low == jnp.bfloat16(i), features, zero) for i in range(32)], 0
                    )
                ]
            total_ref[...] += lax.dot_general(
                jnp.concatenate(spreads, 1),
                jnp.concatenate(hots, 1),
                (((1,), (1,)), ((), ())),
                preferred_element_type=jnp.float32,
            )

    @pl.when(step == pl.num_programs(0) - 1)
    def _():
        for part in range(4):
            summed = jnp.transpose(total_ref[part * wide : part * wide + wide])
            coarse = summed.astype(jnp.bfloat16)
            lanes = slice(part * wide, part * wide + wide)
            coarse_ref[:, lanes] = coarse
            fine_ref[:, lanes] = (summed - coarse.astype(jnp.float32)).astype(jnp.bfloat16)
            west_ref[:, lanes] = coarse[:64]
            east_ref[:, lanes] = coarse[192:]
            if part == 0:
                south_ref[...] = coarse
            if part == 3:
                north_ref[...] = coarse


def scatter(messages):
    sources, rows, width = messages.shape
    shapes = [(256, 1024)] * 2 + [(64, 1024)] * 2 + [(256, 256)] * 2
    return pl.pallas_call(
        scatter_kernel,
        grid=(sources // BUCKETS,),
        in_specs=[
            pl.BlockSpec((BUCKETS, rows, width), lambda i: (i, 0, 0)),
        ],
        out_specs=[pl.BlockSpec(memory_space=pltpu.VMEM)] * 6,
        out_shape=[jax.ShapeDtypeStruct(shape, jnp.bfloat16) for shape in shapes],
        scratch_shapes=[pltpu.VMEM((1024, 256), jnp.float32)],
        compiler_params=pltpu.CompilerParams(vmem_limit_bytes=14 << 20),
        name="scatter",
    )(messages)


def leaf_taps_kernel(convs_ref, taps_ref):
    zero = jnp.zeros((64, 64), jnp.bfloat16)
    for layer in range(2):
        for dx in range(3):
            for kind in range(2):
                for step_y in range(4):
                    for half in range(2):
                        row = kind * 512 + step_y * 128 + half * 64
                        for out_y in range(2):
                            blocks = []
                            for out_z in range(2):
                                dy = step_y - out_y
                                if kind == 0:
                                    dz = half - out_z + 1
                                else:
                                    dz = 3 - out_z if half == 0 else -out_z
                                inside = 0 <= dy <= 2 and 0 <= dz <= 2
                                blocks.append(convs_ref[layer, dx, dy, dz] if inside else zero)
                            taps_ref[layer, dx, row : row + 64, out_y * 128 : out_y * 128 + 128] = (
                                jnp.concatenate(blocks, 1)
                            )


def leaf_taps(leaf_convs):
    return pl.pallas_call(
        leaf_taps_kernel,
        out_shape=jax.ShapeDtypeStruct((2, 3, 1024, 256), jnp.bfloat16),
        name="leaf_taps",
    )(leaf_convs)


def row_shifts(values, period):
    count = values.shape[0]
    place = lax.rem(lax.broadcasted_iota(jnp.int32, values.shape, 0), period)
    before = jnp.where(place == 0, 0.0, pltpu.roll(values, 1, 0))
    after = jnp.where(place == period - 1, 0.0, pltpu.roll(values, count - 1, 0))
    return before, after


def z_neighbours(values):
    before, after = row_shifts(values, 16)
    lane = lax.rem(lax.broadcasted_iota(jnp.int32, values.shape, 1), 128)
    return jnp.where(lane < 64, after, before).astype(jnp.bfloat16)


def spread_bricks(near, flags):
    side = lax.rem(lax.axis_index("gy"), 2)
    columns = []
    for y in range(4):
        for x in range(4):
            source_x, source_y = (0, 1, 1, 2)[x], (0, 1, 1, 2)[y]
            lane = ((1, 0, 1, 0)[x] * 2 + (1, 0, 1, 0)[y]) * 16
            tile = near[source_x * 3 + source_y].astype(jnp.float32)
            upper = side == 0 if source_y == 1 else side == 1
            value = jnp.where(upper, tile[:, 64 + lane : 65 + lane], tile[:, lane : lane + 1])
            flag = flags[0][source_x] * flags[1][source_y]
            columns.append(jnp.broadcast_to(value, (8, 128)) * flag)
    return columns


def doubled(column):
    level = lax.broadcasted_iota(jnp.int32, (16, 128), 0) // 4
    tile = jnp.broadcast_to(column[0:1], (16, 128))
    for z in range(1, 4):
        tile = jnp.where(level == z, jnp.broadcast_to(column[2 * z : 2 * z + 1], (16, 128)), tile)
    return tile


def grid_flags():
    here_x, here_y = lax.axis_index("gx"), lax.axis_index("gy")
    last_x, last_y = lax.axis_size("gx") - 1, lax.axis_size("gy") - 1
    return (
        (jnp.where(here_x > 0, 1.0, 0.0), 1.0, jnp.where(here_x < last_x, 1.0, 0.0)),
        (jnp.where(here_y > 0, 1.0, 0.0), 1.0, jnp.where(here_y < last_y, 1.0, 0.0)),
    )


def fill_leaf_mask(columns, leaf_mask_ref):
    for y in range(4):
        for x in range(4):
            tile = doubled(columns[y * 4 + x])
            for place_x in range(*((0, 4), (4, 12), (12, 20), (20, 24))[x]):
                leaf_mask_ref[y, place_x * 16 : place_x * 16 + 16] = tile


def leaf_sweep(sources, taps, rows):
    windows = []
    for source_ref, source_z_ref, lane in sources:
        pieces = []
        for dx in range(3):
            pieces.append(source_ref[dx * 16 : dx * 16 + rows, pl.ds(lane, 512)])
            pieces.append(source_z_ref[dx * 16 : dx * 16 + rows, pl.ds(lane, 512)])
        windows.append(jnp.concatenate(pieces, 1))
    total = jnp.dot(jnp.concatenate(windows, 0), taps, preferred_element_type=jnp.float32)
    total = jnp.maximum(total, 0.0)
    return [total[i * rows : i * rows + rows] for i in range(len(sources))]


def own_kernel(
    coarse_ref,
    fine_ref,
    lift_ref,
    arrived_ref,
    cells_ref,
    cell_z_ref,
    bricks_ref,
    near_vmem,
    near_sem,
):
    last_x, last_y = lax.axis_size("gx") - 1, lax.axis_size("gy") - 1
    copies = []
    for x in range(3):
        for y in range(3):
            source = jnp.clip(lax.axis_index("gx") + x - 1, 0, last_x) * (last_y + 1)
            source = source + jnp.clip(lax.axis_index("gy") + y - 1, 0, last_y)
            copies.append(
                pltpu.make_async_copy(
                    arrived_ref.at[source, 64:72], near_vmem.at[x * 3 + y], near_sem.at[x, y]
                )
            )
    for copy in copies:
        copy.start()

    @pl.loop(0, 4)
    def _(part):
        sums = pl.ds(pl.multiple_of(part * 256, 256), 256)
        lanes = pl.ds(pl.multiple_of(part * 512, 512), 512)
        lifted = jnp.dot(coarse_ref[:, sums], lift_ref[...], preferred_element_type=jnp.float32)
        lifted += jnp.dot(fine_ref[:, sums], lift_ref[...], preferred_element_type=jnp.float32)
        cells = lifted.astype(jnp.bfloat16)
        cells_ref[:, lanes] = cells
        cell_z_ref[:, lanes] = z_neighbours(cells.astype(jnp.float32))

    for copy in copies:
        copy.wait()
    for index, column in enumerate(spread_bricks([near_vmem[i] for i in range(9)], grid_flags())):
        bricks_ref[index] = column


def own_part(coarse, fine, lift_block, arrived):
    return pl.pallas_call(
        own_kernel,
        out_shape=[
            jax.ShapeDtypeStruct((256, 2048), jnp.bfloat16),
            jax.ShapeDtypeStruct((256, 2048), jnp.bfloat16),
            jax.ShapeDtypeStruct((16, 8, 128), jnp.float32),
        ],
        in_specs=[pl.BlockSpec(memory_space=pltpu.VMEM)] * 3
        + [pl.BlockSpec(memory_space=pl.ANY)],
        out_specs=[pl.BlockSpec(memory_space=pltpu.VMEM)] * 3,
        scratch_shapes=[
            pltpu.VMEM((9, 8, 128), jnp.bfloat16),
            pltpu.SemaphoreType.DMA((3, 3)),
        ],
        compiler_params=pltpu.CompilerParams(vmem_limit_bytes=8 << 20),
        name="leaf_own",
    )(coarse, fine, lift_block, arrived)


def middle_kernel(
    cells_ref,
    west_ref,
    east_ref,
    lift_ref,
    taps_ref,
    own_z_ref,
    bricks_ref,
    one_ref,
    one_z_ref,
    low_ref,
    high_ref,
    cell_ref,
    cell_z_ref,
    leaf_mask_ref,
):
    flags = grid_flags()
    cell_ref[64:320] = cells_ref[...]
    for part in range(4):
        for row, ref, flag in ((0, west_ref, flags[0][0]), (320, east_ref, flags[0][2])):
            sums = ref[:, part * 256 : part * 256 + 256]
            lifted = jnp.dot(sums, lift_ref[...], preferred_element_type=jnp.float32) * flag
            cell_ref[row : row + 64, part * 512 : part * 512 + 512] = lifted.astype(jnp.bfloat16)
    low_ref[...] = cell_ref[:, :256]
    high_ref[...] = cell_ref[:, 1792:]

    cell_z_ref[64:320] = own_z_ref[...]
    for row in (0, 320):
        for part in range(4):
            lanes = slice(part * 512, part * 512 + 512)
            halo = cell_ref[row : row + 64, lanes].astype(jnp.float32)
            cell_z_ref[row : row + 64, lanes] = z_neighbours(halo)
    fill_leaf_mask([bricks_ref[i] for i in range(16)], leaf_mask_ref)
    taps = taps_ref[0].reshape(3072, 256)
    for first, count in ((0, 4), (4, 3)):
        sources = [(cell_ref, cell_z_ref, (first + i) * 256) for i in range(count)]
        for window, total in enumerate(leaf_sweep(sources, taps, 352)):
            step = first + window
            masks = [leaf_mask_ref[(2 * step + half + 9) // 8, 16:368] for half in range(2)]
            values = (total * jnp.concatenate(masks, 1)).astype(jnp.bfloat16)
            one_ref[:, step * 256 : step * 256 + 256] = values
            one_z_ref[:, step * 256 : step * 256 + 256] = z_neighbours(values.astype(jnp.float32))


def middle_part(cells, west, east, lift_block, taps, own_z, bricks):
    return pl.pallas_call(
        middle_kernel,
        out_shape=[
            jax.ShapeDtypeStruct((352, 1792), jnp.bfloat16),
            jax.ShapeDtypeStruct((352, 1792), jnp.bfloat16),
            jax.ShapeDtypeStruct((384, 256), jnp.bfloat16),
            jax.ShapeDtypeStruct((384, 256), jnp.bfloat16),
        ],
        in_specs=[pl.BlockSpec(memory_space=pltpu.VMEM)] * 7,
        out_specs=[pl.BlockSpec(memory_space=pltpu.VMEM)] * 4,
        scratch_shapes=[
            pltpu.VMEM((384, 2048), jnp.bfloat16),
            pltpu.VMEM((384, 2048), jnp.bfloat16),
            pltpu.VMEM((4, 384, 128), jnp.float32),
        ],
        compiler_params=pltpu.CompilerParams(vmem_limit_bytes=24 << 20),
        name="leaf_middle",
    )(cells, west, east, lift_block, taps, own_z, bricks)


def border_kernel(
    low_ref,
    high_ref,
    north_ref,
    south_ref,
    lift_ref,
    taps_ref,
    bricks_ref,
    one_middle_ref,
    one_z_middle_ref,
    down_leaf_ref,
    coarse_ref,
    down_ref,
    features_ref,
    down_two_ref,
    edge_ref,
    edge_z_ref,
    one_ref,
    one_z_ref,
    down_one_ref,
    parts_ref,
    down_leaf_vmem,
    coarse_vmem,
    down_vmem,
    leaf_mask_ref,
    one_sem,
    leaf_sem,
    coarse_sem,
    down_sem,
):
    early = [
        pltpu.make_async_copy(one_middle_ref, one_ref.at[:, 512:2304], one_sem.at[0]),
        pltpu.make_async_copy(one_z_middle_ref, one_z_ref.at[:, 512:2304], one_sem.at[1]),
        pltpu.make_async_copy(down_leaf_ref, down_leaf_vmem, leaf_sem),
    ]
    copies = [
        pltpu.make_async_copy(coarse_ref.at[0], coarse_vmem, coarse_sem),
        pltpu.make_async_copy(down_ref.at[0], down_vmem, down_sem),
    ]
    for copy in early + copies:
        copy.start()
    flags = grid_flags()
    edge_ref[0, :, 512:768] = low_ref[...]
    edge_ref[1, :, 0:256] = high_ref[...]
    for edge, lane, ref, flag in ((0, 0, south_ref, flags[1][0]), (1, 256, north_ref, flags[1][2])):
        for row, rows, other in ((0, 64, flags[0][0]), (64, 256, 1.0), (320, 64, flags[0][2])):
            sums = ref[row : row + rows]
            lifted = jnp.dot(sums, lift_ref[...], preferred_element_type=jnp.float32)
            lifted = (lifted * (flag * other)).astype(jnp.bfloat16)
            edge_ref[edge, row : row + rows, lane : lane + 512] = lifted
    fill_leaf_mask([bricks_ref[i] for i in range(16)], leaf_mask_ref)
    for edge in range(2):
        for part in range(3):
            lanes = slice(part * 256, part * 256 + 256)
            edge_z_ref[edge, :, lanes] = z_neighbours(edge_ref[edge, :, lanes].astype(jnp.float32))
    sources, steps = [], []
    for edge in range(2):
        for window in range(2):
            sources.append((edge_ref.at[edge], edge_z_ref.at[edge], window * 256))
            steps.append(edge * 9 + window)
    taps = taps_ref[0].reshape(3072, 256)
    for step, total in zip(steps, leaf_sweep(sources, taps, 352)):
        masks = [leaf_mask_ref[(2 * step + half + 5) // 8, 16:368] for half in range(2)]
        values = (total * jnp.concatenate(masks, 1)).astype(jnp.bfloat16)
        one_ref[:, step * 256 : step * 256 + 256] = values
        one_z_ref[:, step * 256 : step * 256 + 256] = z_neighbours(values.astype(jnp.float32))
    for copy in early:
        copy.wait()

    @pl.loop(0, 2)
    def _(half_step):
        first = half_step * 5
        lanes = [pl.multiple_of((first + i) * 256, 256) for i in range(5)]
        taps = taps_ref[1].reshape(3072, 256)
        totals = leaf_sweep([(one_ref, one_z_ref, lane) for lane in lanes], taps, 320)
        merges, masks = [], []
        for window, total in enumerate(totals):
            step = first + window
            mask = leaf_mask_ref[(2 * step + 6) // 8, 32:352]
            values = (total * jnp.concatenate([mask, mask], 1)).astype(jnp.bfloat16)

            @pl.when((step >= 1) & (step < 9))
            def _():
                for half in range(2):
                    inner = values[32:288, half * 128 : half * 128 + 128]
                    features_ref[:, 2 * step - 2 + half] = inner.reshape(16, 16, 128)

            pairs = values.reshape(10, 2, 16, 256)
            halves = [pairs[:, a].reshape(160, 256) for a in range(2)]
            merges.append(jnp.concatenate(halves, 1))
            masks.append(mask.reshape(10, 2, 16, 128)[:, 0].reshape(160, 128))
        taps = down_leaf_vmem[...].reshape(512, 128)
        total = jnp.dot(jnp.concatenate(merges, 0), taps, preferred_element_type=jnp.float32)
        total = jnp.maximum(total, 0.0) * jnp.concatenate(masks, 0)
        for window in range(5):
            down = total[window * 160 : window * 160 + 160].astype(jnp.bfloat16)
            before, after = row_shifts(down.astype(jnp.float32), 16)
            here = pl.ds(pl.multiple_of((first + window) * 128, 128), 128)
            down_one_ref[0, :, here] = before.astype(jnp.bfloat16)
            down_one_ref[1, :, here] = down
            down_one_ref[2, :, here] = after.astype(jnp.bfloat16)

    for copy in copies:
        copy.wait()
    windows = []
    for y in range(8):
        windows.append(
            jnp.concatenate(
                [
                    down_one_ref[dz, dx * 16 : dx * 16 + 128, y * 128 : y * 128 + 384]
                    for dx in range(3)
                    for dz in range(3)
                ],
                1,
            )
        )
    taps = [coarse_vmem[dx, :, dz].reshape(384, 128) for dx in range(3) for dz in range(3)]
    taps = jnp.concatenate(taps, 0)
    total = jnp.dot(jnp.concatenate(windows, 0), taps, preferred_element_type=jnp.float32)
    total = jnp.maximum(total, 0.0).reshape(8, 128, 128)
    masks = [leaf_mask_ref[1 + y // 4, 64:320].reshape(8, 2, 16, 128)[:, 0] for y in range(8)]
    level = total * jnp.concatenate(masks, 0).reshape(8, 128, 128)
    level = level.astype(jnp.bfloat16).reshape(4, 2, 4, 2, 16, 128)
    merged = jnp.concatenate(
        [level[:, b, :, a].reshape(256, 128) for a in range(2) for b in range(2)], 1
    )
    taps = [
        jnp.concatenate([down_vmem[a, b, c] for c in range(2)], 1)
        for a in range(2)
        for b in range(2)
    ]
    taps = jnp.concatenate(taps, 0)
    parts = jnp.dot(merged, taps, preferred_element_type=jnp.float32)
    parts_ref[0] = parts[:, :128]
    parts_ref[1] = parts[:, 128:]
    total = parts_ref[0, pl.ds(0, 128, stride=2)] + parts_ref[1, pl.ds(1, 128, stride=2)]
    tiles = [bricks_ref[(1 + y // 2) * 4 + 1 + x // 2] for y in range(4) for x in range(4)]
    mask = jnp.concatenate(tiles, 0)
    down_two_ref[...] = (jnp.maximum(total, 0.0) * mask).astype(jnp.bfloat16)


def border_part(low, high, north, south, lift_block, taps, bricks, one, one_z, down_leaf, coarse, down):
    return pl.pallas_call(
        border_kernel,
        out_shape=[
            jax.ShapeDtypeStruct((16, 16, 16, 128), jnp.bfloat16),
            jax.ShapeDtypeStruct((128, 128), jnp.bfloat16),
        ],
        in_specs=[pl.BlockSpec(memory_space=pltpu.VMEM)] * 7
        + [pl.BlockSpec(memory_space=pl.ANY)] * 3
        + [pl.BlockSpec(memory_space=pltpu.HBM)] * 2,
        scratch_shapes=[
            pltpu.VMEM((2, 384, 768), jnp.bfloat16),
            pltpu.VMEM((2, 384, 768), jnp.bfloat16),
            pltpu.VMEM((352, 2816), jnp.bfloat16),
            pltpu.VMEM((352, 2816), jnp.bfloat16),
            pltpu.VMEM((3, 160, 1280), jnp.bfloat16),
            pltpu.VMEM((2, 256, 128), jnp.float32),
            pltpu.VMEM((2, 2, 2, 64, 128), jnp.bfloat16),
            pltpu.VMEM((3, 3, 3, 128, 128), jnp.bfloat16),
            pltpu.VMEM((2, 2, 2, 128, 128), jnp.bfloat16),
            pltpu.VMEM((4, 384, 128), jnp.float32),
            pltpu.SemaphoreType.DMA((2,)),
            pltpu.SemaphoreType.DMA,
            pltpu.SemaphoreType.DMA,
            pltpu.SemaphoreType.DMA,
        ],
        compiler_params=pltpu.CompilerParams(vmem_limit_bytes=32 << 20),
        name="leaf_border",
    )(low, high, north, south, lift_block, taps, bricks, one, one_z, down_leaf, coarse, down)


def coarse_kernel(
    north_ref,
    middle_ref,
    south_ref,
    coarse_ref,
    down_ref,
    bricks_ref,
    top_ref,
    parts_ref,
):
    here_x = lax.axis_index("gx")
    here_y = lax.axis_index("gy")
    from_west = jnp.where(here_x > 0, 1.0, 0.0)
    from_east = jnp.where(here_x < lax.axis_size("gx") - 1, 1.0, 0.0)
    from_south = jnp.where(here_y > 0, 1.0, 0.0)
    from_north = jnp.where(here_y < lax.axis_size("gy") - 1, 1.0, 0.0)

    strips = []
    for ref, first, flag in ((south_ref, 1, from_south), (middle_ref, 0, 1.0), (north_ref, 0, from_north)):
        count = 4 if ref is middle_ref else 3
        tiles = [ref[i].astype(jnp.float32).reshape(4, 4, 8, 128) for i in (2, 1, 0)]
        tiles = [tile[first : first + count] for tile in tiles]
        tiles = [
            tiles[0][:, 1:] * (flag * from_west),
            tiles[1] * flag,
            tiles[2][:, :3] * (flag * from_east),
        ]
        strips.append(jnp.concatenate(tiles, 1))
    grid = jnp.concatenate(strips, 0)
    before, after = row_shifts(grid.reshape(800, 128), 8)
    grids = [before.reshape(10, 10, 8, 128), grid, after.reshape(10, 10, 8, 128)]
    pieces = [
        grids[dz][dy : dy + 8, dx : dx + 8].reshape(512, 128).astype(jnp.bfloat16)
        for dx in range(3)
        for dy in range(3)
        for dz in range(3)
    ]
    taps = coarse_ref[1].reshape(3456, 128)
    total = jnp.dot(jnp.concatenate(pieces, 1), taps, preferred_element_type=jnp.float32)
    tiles = [bricks_ref[y // 2 * 4 + x // 2] for y in range(8) for x in range(8)]
    mask = jnp.concatenate(tiles, 0)
    level = jnp.maximum(total, 0.0) * mask
    level = level.reshape(4, 2, 4, 2, 8, 128)
    merged = jnp.concatenate(
        [level[:, b, :, a].reshape(128, 128) for a in range(2) for b in range(2)], 1
    ).astype(jnp.bfloat16)
    taps = [
        jnp.concatenate([down_ref[1, a, b, c] for c in range(2)], 1)
        for a in range(2)
        for b in range(2)
    ]
    taps = jnp.concatenate(taps, 0)
    parts = jnp.dot(merged, taps, preferred_element_type=jnp.float32)
    parts_ref[0] = parts[:, :128]
    parts_ref[1] = parts[:, 128:]
    total = parts_ref[0, pl.ds(0, 64, stride=2)] + parts_ref[1, pl.ds(1, 64, stride=2)]
    picks = lax.broadcasted_iota(jnp.int32, (64, 128), 0) * 2
    picks = picks == lax.broadcasted_iota(jnp.int32, (64, 128), 1)
    picks = jnp.where(picks, 1.0, 0.0).astype(jnp.bfloat16)
    bricks = bricks_ref[...].reshape(128, 128).astype(jnp.bfloat16)
    mask = jnp.dot(picks, bricks, preferred_element_type=jnp.float32)
    down = jnp.maximum(total, 0.0) * mask
    down = down.astype(jnp.bfloat16).astype(jnp.float32)
    before, after = row_shifts(down, 4)
    shifted = [before, down, after]
    pieces = []
    for dx in range(3):
        for dy in range(3):
            for dz in range(3):
                turn = (64 - (dy - 1) * 16 - (dx - 1) * 4) % 64
                moved = pltpu.roll(shifted[dz], turn, 0) if turn else shifted[dz]
                pieces.append(moved.astype(jnp.bfloat16))
    taps = coarse_ref[2].reshape(3456, 128)
    total = jnp.dot(jnp.concatenate(pieces, 1), taps, preferred_element_type=jnp.float32)
    top = (jnp.maximum(total, 0.0) * mask).astype(jnp.bfloat16)
    for x in range(2):
        for y in range(2):
            row = (y + 1) * 16 + (x + 1) * 4
            top_ref[x, y] = top[row : row + 4]


def coarse_levels(north, middle, south, coarse, down, bricks):
    return pl.pallas_call(
        coarse_kernel,
        out_shape=jax.ShapeDtypeStruct((2, 2, 4, 128), jnp.bfloat16),
        in_specs=[pl.BlockSpec(memory_space=pltpu.VMEM)] * 6,
        scratch_shapes=[pltpu.VMEM((2, 128, 128), jnp.float32)],
        compiler_params=pltpu.CompilerParams(vmem_limit_bytes=16 << 20),
        name="coarse_levels",
    )(north, middle, south, coarse, down, bricks)


def ring(values, axis, step):
    count = lax.axis_size(axis)
    return lax.ppermute(values, axis, [(i, (i + step) % count) for i in range(count)])


def per_device(
    records, slot_voxels, brick_mask, lift_weight, leaf_convs, down_leaf, down_coarse, coarse_convs
):
    messages = pack_messages(records[0], slot_voxels[0], brick_mask)
    arrived = lax.all_to_all(messages, ("gx", "gy"), split_axis=0, concat_axis=0, tiled=True)
    lift_block = jnp.kron(jnp.eye(8, dtype=jnp.bfloat16), lift_weight)
    taps = leaf_taps(leaf_convs)
    arrived, lift_block, taps = lax.optimization_barrier((arrived, lift_block, taps))
    coarse_hbm = pltpu.with_memory_space_constraint(coarse_convs, pltpu.HBM)
    down_hbm = pltpu.with_memory_space_constraint(down_coarse, pltpu.HBM)

    coarse, fine, low_x, high_x, low_y, high_y = scatter(arrived)
    west = ring(high_x, "gx", 1)
    east = ring(low_x, "gx", -1)
    cells, own_z, bricks = own_part(coarse, fine, lift_block, arrived)
    west, east, own_z = lax.optimization_barrier((west, east, own_z))
    north = ring(jnp.concatenate([west[:, :256], low_y, east[:, :256]], 0), "gy", -1)
    south = ring(jnp.concatenate([west[:, 768:], high_y, east[:, 768:]], 0), "gy", 1)
    one, one_z, low, high = middle_part(cells, west, east, lift_block, taps, own_z, bricks)
    features, down_two = border_part(
        low,
        high,
        north,
        south,
        lift_block,
        taps,
        bricks,
        one,
        one_z,
        down_leaf,
        coarse_hbm,
        down_hbm,
    )
    west = ring(down_two, "gx", 1)
    east = ring(down_two, "gx", -1)
    middle = jnp.stack([east, down_two, west])
    south = ring(middle, "gy", 1)
    north = ring(middle, "gy", -1)
    top = coarse_levels(north, middle, south, coarse_convs, down_coarse, bricks)
    return (features, top)


def solution(mesh):
    in_specs = (
        P(("gx", "gy"), None, None, None),
        P(("gx", "gy"), None, None),
        P("gx", "gy", None),
        P(),
        P(),
        P(),
        P(),
        P(),
    )
    out_specs = (P("gx", "gy", None, None), P("gx", "gy", None, None))
    return jax.shard_map(
        per_device, mesh=mesh, in_specs=in_specs, out_specs=out_specs, check_vma=False
    )
```
